32 devices in a mesh: role: 4 (over y, core), tile: 8 (over z, x).
Axes of the slice: x: 2, y: 2, z: 4, core: 2. Of those that a mesh axis runs over, the one named last changes fastest.
Arguments:
- velocity: float32 [3, 32, 512, 128], P(None, 'role', 'tile'), may hold values from -5 to 5
- params: float32 [819200], replicated, may hold values from -0.36 to 0.36
- first_moment: float32 [819200], P(('role', 'tile')), may hold values from -1.8 to 1.8
- second_moment: float32 [819200], P(('role', 'tile')), may hold values from 0.02 to 2
- patch_index: int32 [65536], P(('role', 'tile')), may hold values from 0 to 1023
- patch_count: int32 [32], P(('role', 'tile')), may hold values from 1 to 2048, 16384 in all
Outputs:
- velocity_out: float32 [3, 32, 512, 128], P(None, 'role', 'tile')
- sgs_force: float32 [3, 32, 512, 128], P(None, 'role', 'tile')
- params_out: float32 [819200], replicated
- first_out: float32 [819200], P(('role', 'tile'))
- second_out: float32 [819200], P(('role', 'tile'))
The draws below stay inside these ranges and needn't reach their ends.
Inputs may be any that keep to these rules, and one draw needn't show every extreme that they name: `patch_index`: only the first patch_count entries of a device's list are used. `patch_count`: the counts of all devices sum to 16384; the largest is 2048.
All inputs are finite; a program needn't handle non-finite values.
Results may differ from the reference program's by a relative error of at most 0.0091.
Values may be sent and summed in bfloat16 or wider, within the bound.
No kernel may reach another device: no remote copies, remote signals or barrier semaphores. Data moves between devices by JAX's collectives and lax.ppermute only.
A program may use at most 128 MiB of HBM per device.

```python
import math
import jax
import jax.numpy as jnp
import numpy as np
from jax import lax

CX = 8
CY = 64
CZ = 128
SEL = 2048
FEAT = 192
TGT = 384
HID = 512
MIDS = 2
SUBSTEPS = 2
ADAM_STEP = 100
NX = 32
NY = 512
NZ = 128
NPATCH = 1024
SHARE = 512
TOTAL = 16384
NPAR = 819200
N_ROLE = 4
N_TILE = 8
DEVICES = 32


def set_ends(result, own_key, least, largest):
    shape = result.shape
    place = [jax.random.randint(jax.random.fold_in(own_key, axis), (), 0, shape[axis]) for axis in range(len(shape))]
    result = result.at[tuple(place)].set(least)
    longest = shape.index(max(shape))
    place[longest] = (place[longest] + 1) % shape[longest]
    return result.at[tuple(place)].set(largest)


def block_scale(stream_key, dims, cuts, low, high):
    level = 1.0
    for axis_at, parts in cuts:
        draws = jax.random.uniform(jax.random.fold_in(jax.random.fold_in(stream_key, 6), axis_at), (parts,), jnp.float32, low / len(cuts), high / len(cuts))
        level = level * jnp.repeat(jnp.exp(draws), dims[axis_at] // parts).reshape((-1,) + (1,) * (len(dims) - 1 - axis_at))
    return level


def split_up(count, total, bound, skew):
    weights = [(1 << 20) // math.isqrt(rank ** skew) + 1 for rank in range(2, count + 1)]
    surplus, counts = total - bound - (count - 1), [1] * (count - 1)
    while surplus > 0:
        free = [i for i in range(count - 1) if counts[i] < bound]
        mass, budget = sum([weights[i] for i in free]), surplus
        for i in free:
            extra = min(bound - counts[i], max(1, budget * weights[i] // mass), surplus)
            counts[i] = counts[i] + extra
            surplus = surplus - extra
    return np.array([bound] + counts)


def ragged_sizes(own_key, amount, total, bound, skew):
    if amount == 2:
        one = jax.random.randint(own_key, (), max(1, total - bound), min(bound, total - 1) + 1)
        return jnp.stack([one, total - one])
    tallies = jnp.asarray(split_up(amount, total, bound, skew), jnp.int32)
    couples = (amount - 1) // 2
    source_of, receiver = tallies[1:1 + 2 * couples:2], tallies[2:2 + 2 * couples:2]
    slack = jnp.minimum(source_of - 1, bound - receiver)
    passed = jax.random.randint(jax.random.fold_in(own_key, 1), (couples,), 0, 1 << 20) % (slack + 1)
    tallies = tallies.at[1:1 + 2 * couples:2].set(source_of - passed).at[2:2 + 2 * couples:2].set(receiver + passed)
    return tallies[jax.random.permutation(jax.random.fold_in(own_key, 2), amount)]


def gaussian(own_key, dims, deviation, limit, cuts=(), held_as=jnp.bfloat16):
    entries = deviation * jax.random.normal(own_key, dims, jnp.float32)
    if cuts:
        entries = entries * block_scale(own_key, dims, cuts, -0.22, 0.18)
    return jnp.clip(entries, -limit, limit).astype(held_as)


def setup_inputs(seed: int = 0) -> dict:
    seeds = jax.random.split(jax.random.key(seed), 7)
    velocity = gaussian(seeds[0], (3, NX, NY, NZ), 1.0, 5.0, ((1, 4), (2, 8)), jnp.float32)
    params = gaussian(seeds[1], (NPAR,), 0.06, 0.36, (), jnp.float32)
    first_moment = gaussian(seeds[2], (NPAR,), 0.3, 1.8, ((0, 32),), jnp.float32)
    second_moment = jnp.clip(jnp.exp(math.log(2.0) - 4.6051702 * jax.random.uniform(seeds[3], (NPAR,), jnp.float32) ** block_scale(seeds[3], (NPAR,), ((0, 32),), -0.2, 0.2)), 0.02, 2.0)
    patch_index = set_ends(jax.random.randint(seeds[4], (SEL * DEVICES,), 0, NPATCH), jax.random.fold_in(seeds[4], 1), 0, NPATCH - 1).astype(jnp.int32)
    patch_count = ragged_sizes(seeds[5], DEVICES, TOTAL, SEL, 2).astype(jnp.int32)
    return {"velocity": velocity, "params": params, "first_moment": first_moment, "second_moment": second_moment, "patch_index": patch_index, "patch_count": patch_count}


STEP_DT = 0.1
VISCOSITY = 0.1
SGS_SCALE = 1.5
BETA_ONE = 0.9
BETA_TWO = 0.999
LEARN_RATE = 0.001
EPSILON = 1e-08
PAIRS = ((0, 0), (1, 1), (2, 2), (0, 1), (0, 2), (1, 2))
COMPONENT = ((0, 3, 4), (3, 1, 5), (4, 5, 2))

def wrap_pad(grid_field, margin):
    return jnp.pad(grid_field, ((0, 0), (margin, margin), (margin, margin), (0, 0)), mode='wrap')

def advance(padded):
    centre = padded[:, 1:-1, 1:-1, :]
    after_first = padded[:, 2:, 1:-1, :]
    before_first = padded[:, :-2, 1:-1, :]
    after_second = padded[:, 1:-1, 2:, :]
    before_second = padded[:, 1:-1, :-2, :]
    after_third = jnp.roll(centre, -1, axis=3)
    before_third = jnp.roll(centre, 1, axis=3)
    transport = centre[0:1] * (0.5 * (after_first - before_first))
    transport = transport + centre[1:2] * (0.5 * (after_second - before_second))
    transport = transport + centre[2:3] * (0.5 * (after_third - before_third))
    laplace = after_first + before_first + after_second + before_second + after_third + before_third - 6.0 * centre
    return centre + STEP_DT * (VISCOSITY * laplace - transport)

def box_mean(padded):
    along_first = padded[:, :-2] + padded[:, 1:-1] + padded[:, 2:]
    along_second = along_first[:, :, :-2] + along_first[:, :, 1:-1] + along_first[:, :, 2:]
    return (along_second + jnp.roll(along_second, 1, axis=3) + jnp.roll(along_second, -1, axis=3)) / 27.0

def stress_targets(padded):
    smooth = box_mean(padded)
    pieces = []
    for first_axis, second_axis in PAIRS:
        product = padded[first_axis:first_axis + 1] * padded[second_axis:second_axis + 1]
        pieces.append(box_mean(product)[0] - smooth[first_axis] * smooth[second_axis])
    return jnp.stack(pieces).astype(jnp.bfloat16)

def divergence(padded):
    centre = padded[:, 1:-1, 1:-1, :]
    slope_first = 0.5 * (padded[:, 2:, 1:-1, :] - padded[:, :-2, 1:-1, :])
    slope_second = 0.5 * (padded[:, 1:-1, 2:, :] - padded[:, 1:-1, :-2, :])
    slope_third = 0.5 * (jnp.roll(centre, -1, axis=3) - jnp.roll(centre, 1, axis=3))
    rows_out = []
    for component in range(3):
        picks = COMPONENT[component]
        rows_out.append(slope_first[picks[0]] + slope_second[picks[1]] + slope_third[picks[2]])
    return jnp.stack(rows_out)

def to_patches(grid_field):
    channels, size_first, size_second, size_third = grid_field.shape
    blocks = grid_field.reshape(channels, size_first // 4, 4, size_second // 4, 4, size_third // 4, 4)
    return blocks.transpose(1, 3, 5, 0, 2, 4, 6).reshape(-1, channels * 64)

def from_patches(row_data, channels, size_first, size_second, size_third):
    blocks = row_data.reshape(size_first // 4, size_second // 4, size_third // 4, channels, 4, 4, 4)
    return blocks.transpose(3, 0, 4, 1, 5, 2, 6).reshape(channels, size_first, size_second, size_third)

def unpack(flat_params):
    weights = flat_params.astype(jnp.bfloat16)
    first_end = FEAT * HID
    middle_end = first_end + MIDS * HID * HID
    first_layer = weights[:first_end].reshape(FEAT, HID)
    middle = weights[first_end:middle_end].reshape(MIDS, HID, HID)
    last_layer = weights[middle_end:].reshape(HID, TGT)
    matrices = [first_layer] + [middle[layer_pos] for layer_pos in range(MIDS)]
    return (matrices, last_layer)

def forward(inputs, matrices, last_layer):
    hidden = inputs
    stored_pre = []
    stored_act = [inputs]
    for matrix in matrices:
        pre_act = jnp.dot(hidden, matrix, preferred_element_type=jnp.float32)
        hidden = jax.nn.silu(pre_act).astype(jnp.bfloat16)
        stored_pre.append(pre_act)
        stored_act.append(hidden)
    output = jnp.dot(hidden, last_layer, preferred_element_type=jnp.float32)
    return (output, stored_pre, stored_act)

def contract_rows(left, right):
    return lax.dot_general(left, right, (((0,), (0,)), ((), ())), preferred_element_type=jnp.float32)

def contract_cols(left, right):
    return lax.dot_general(left, right, (((1,), (1,)), ((), ())), preferred_element_type=jnp.float32)

def gradients(inputs, targets, live_rows, matrices, last_layer, row_scale):
    output, stored_pre, stored_act = forward(inputs, matrices, last_layer)
    residual_err = ((output - targets.astype(jnp.float32)) * (live_rows[:, None] * row_scale)).astype(jnp.bfloat16)
    grad_last = contract_rows(stored_act[-1], residual_err)
    upstream = contract_cols(residual_err, last_layer)
    grad_list = []
    for layer_pos in reversed(range(len(matrices))):
        sigmoid_z = jax.nn.sigmoid(stored_pre[layer_pos])
        slope_bf = (upstream * (sigmoid_z * (1.0 + stored_pre[layer_pos] * (1.0 - sigmoid_z)))).astype(jnp.bfloat16)
        grad_list.insert(0, contract_rows(stored_act[layer_pos], slope_bf))
        if layer_pos > 0:
            upstream = contract_cols(slope_bf, matrices[layer_pos])
    return jnp.concatenate([grad_piece.reshape(-1) for grad_piece in grad_list] + [grad_last.reshape(-1)])

def adam_update(param_part, grad_part, first_part, second_part):
    first_new = BETA_ONE * first_part + (1.0 - BETA_ONE) * grad_part
    second_new = BETA_TWO * second_part + (1.0 - BETA_TWO) * grad_part * grad_part
    fix_first = 1.0 - BETA_ONE ** ADAM_STEP
    fix_second = 1.0 - BETA_TWO ** ADAM_STEP
    update = LEARN_RATE * (first_new / fix_first) / (jnp.sqrt(second_new / fix_second) + EPSILON)
    return (param_part - update, first_new, second_new)

def to_devices(grid_field):
    channels = grid_field.shape[0]
    blocks = grid_field.reshape(channels, N_ROLE, CX, N_TILE, CY, CZ).transpose(1, 3, 0, 2, 4, 5)
    return blocks.reshape(N_ROLE * N_TILE, channels, CX, CY, CZ)

def reference(velocity, params, first_moment, second_moment, patch_index, patch_count):
    flow_now = velocity
    start_pad = wrap_pad(velocity, 1)
    for substep in range(SUBSTEPS):
        flow_now = advance(wrap_pad(flow_now, 1))
    targets = stress_targets(start_pad)
    feature_rows = jax.vmap(to_patches)(to_devices(velocity.astype(jnp.bfloat16)))
    target_rows = jax.vmap(to_patches)(to_devices(targets))
    all_rows = jnp.concatenate([feature_rows, target_rows], axis=2)
    picks = patch_index.reshape(N_ROLE * N_TILE, SEL).astype(jnp.int32)
    listed = jnp.take_along_axis(all_rows, picks[:, :, None], axis=1).reshape(-1, FEAT + TGT)
    live_rows = (jnp.arange(SEL, dtype=jnp.int32)[None, :] < patch_count[:, None]).astype(jnp.float32).reshape(-1)
    matrices, last_layer = unpack(params)
    gradient = gradients(listed[:, :FEAT], listed[:, FEAT:], live_rows, matrices, last_layer, 1.0 / SHARE)
    params_out, first_out, second_out = adam_update(params, gradient, first_moment, second_moment)
    new_matrices, new_last = unpack(params_out)

    def predict(block):
        modelled = forward(to_patches(block.astype(jnp.bfloat16)), new_matrices, new_last)[0].astype(jnp.bfloat16)
        return from_patches(modelled, 6, CX, CY, CZ)
    stress_blocks = lax.map(predict, to_devices(flow_now))
    stress_model = stress_blocks.reshape(N_ROLE, N_TILE, 6, CX, CY, CZ).transpose(2, 0, 3, 1, 4, 5).reshape(6, NX, NY, NZ)
    sgs_force = -SGS_SCALE * divergence(wrap_pad(stress_model, 1).astype(jnp.float32))
    velocity_out = flow_now + sgs_force
    return (velocity_out, sgs_force, params_out, first_out, second_out)
```

```python
import functools

import jax
import jax.numpy as jnp
import numpy as np
from jax import lax
from jax.experimental import pallas as pl
from jax.experimental.pallas import tpu as pltpu
from jax.sharding import PartitionSpec as P

FEAT = 192
TGT = 384
HID = 512
ADAM_STEP = 100
STEP_DT = 0.1
VISCOSITY = 0.1
SGS_SCALE = 1.5
BETA_ONE = 0.9
BETA_TWO = 0.999
LEARN_RATE = 0.001
EPSILON = 1e-08
PAIRS = ((0, 0), (1, 1), (2, 2), (0, 1), (0, 2), (1, 2))
COMPONENT = ((0, 3, 4), (3, 1, 5), (4, 5, 2))

CX, CY, CZ = 8, 64, 128
NPATCH = 1024
ROWS = 6400
W1_AT = 768
W2_AT = W1_AT + 2048
WO_AT = W2_AT + 2048
BOTH = ("role", "tile")
F32, BF16 = jnp.float32, jnp.bfloat16
VMEM_LIMIT = 56 * 1024 * 1024


def row_matrix():
    matrix = np.zeros((256, 256), np.float32)
    for dx in range(4):
        for j in range(4):
            for pyl in range(4):
                for dy in range(4):
                    matrix[pyl * 64 + j * 16 + dx * 4 + dy, dx * 64 + j * 16 + pyl * 4 + dy] = 1
    return matrix


def lane_matrix():
    matrix = np.zeros((512, 512), np.float32)
    for pyl in range(4):
        for pz in range(32):
            for dz in range(4):
                matrix[pyl * 128 + pz * 4 + dz, dz * 128 + pyl * 32 + pz] = 1
    return matrix


def feature_matrix():
    matrix = np.zeros((128, 128), np.float32)
    for c in range(2):
        for off in range(16):
            for dz in range(4):
                matrix[c * 64 + off * 4 + dz, c * 64 + dz * 16 + off] = 1
    return matrix


def dot(a, b):
    return jnp.dot(a, b, preferred_element_type=F32)


def dot_tn(a, b):
    return lax.dot_general(a, b, (((0,), (0,)), ((), ())), preferred_element_type=F32)


def dot_nt(a, b):
    return lax.dot_general(a, b, (((1,), (1,)), ((), ())), preferred_element_type=F32)


def permute_features(feature_mat, x, channels):
    pieces = []
    at = 0
    while at < channels * 64:
        size = min(128, channels * 64 - at)
        pieces.append(dot(feature_mat[:size, :size], x[at : at + size]).astype(BF16))
        at += size
    return jnp.concatenate(pieces, axis=0)


def cells_to_patches(blocks, row_mat, lane_mat, feature_mat, channels):
    moved = dot(row_mat, jnp.concatenate(blocks, axis=1)).astype(BF16)
    rows = []
    for i in range(2 * channels):
        part = moved[:, i * 128 : (i + 1) * 128]
        rows.append(jnp.concatenate([part[p * 64 : (p + 1) * 64] for p in range(4)], axis=1))
    spread = dot(jnp.concatenate(rows, axis=0), lane_mat).astype(BF16)
    bands = []
    for c in range(channels):
        for dz in range(4):
            bands.append(
                jnp.concatenate(
                    [
                        spread[((c * 2 + px) * 4 + j) * 16 : ((c * 2 + px) * 4 + j) * 16 + 16, dz * 128 : dz * 128 + 128]
                        for px in range(2)
                        for j in range(4)
                    ],
                    axis=1,
                )
            )
    return permute_features(feature_mat, jnp.concatenate(bands, axis=0), channels)


def patches_to_cells(x, row_mat, lane_mat, feature_mat, channels):
    pieces = []
    for at in range(0, channels * 64, 128):
        pieces.append(dot_tn(feature_mat, x[at : at + 128]).astype(BF16))
    x = jnp.concatenate(pieces, axis=0)
    rows = []
    for c in range(channels):
        for px in range(2):
            for j in range(4):
                lanes = (px * 4 + j) * 128
                rows.append(
                    jnp.concatenate(
                        [x[c * 64 + dz * 16 : c * 64 + dz * 16 + 16, lanes : lanes + 128] for dz in range(4)], axis=1
                    )
                )
    spread = dot_nt(jnp.concatenate(rows, axis=0), lane_mat).astype(BF16)
    columns = []
    for i in range(2 * channels):
        part = spread[i * 64 : (i + 1) * 64]
        columns.append(jnp.concatenate([part[:, p * 128 : (p + 1) * 128] for p in range(4)], axis=0))
    moved = dot_tn(row_mat, jnp.concatenate(columns, axis=1))
    return [moved[:, i * 128 : (i + 1) * 128] for i in range(2 * channels)]


def load_weights(p_ref, w0, w1, w2, wo):
    for k in range(4):
        lanes = slice(k * 128, (k + 1) * 128)
        w0[:, lanes] = p_ref[pl.ds(k, FEAT, stride=4), :].astype(BF16)
        w1[:, lanes] = p_ref[pl.ds(W1_AT + k, HID, stride=4), :].astype(BF16)
        w2[:, lanes] = p_ref[pl.ds(W2_AT + k, HID, stride=4), :].astype(BF16)
    for k in range(3):
        wo[:, k * 128 : (k + 1) * 128] = p_ref[pl.ds(WO_AT + k, HID, stride=3), :].astype(BF16)


def velocity_blocks(v_ref):
    return [
        v_ref[c, px * 4 : px * 4 + 4].reshape(256, 128).astype(BF16) for c in range(3) for px in range(2)
    ]


def forward_kernel(v_ref, p_ref, row_ref, lane_ref, feat_ref, x_out, a_out, d_out, pred_out, w0, w1, w2, wo):
    load_weights(p_ref, w0, w1, w2, wo)
    x = cells_to_patches(velocity_blocks(v_ref), row_ref[...], lane_ref[...], feat_ref[...], 3)
    x_out[...] = x
    hidden = x
    for layer, w in enumerate((w0, w1, w2)):
        z = dot_tn(w[...], hidden)
        s = 0.5 * jnp.tanh(0.5 * z) + 0.5
        a = z * s
        d_out[layer] = s + a * (1.0 - s)
        hidden = a.astype(BF16)
        a_out[layer] = hidden
    pred_out[...] = dot_tn(wo[...], hidden)


def fill_padded(pad, v_ref, xlo_ref, xhi_ref, ylo_ref, yhi_ref):
    pad[:, 2:10, 8:72, :] = v_ref[...]
    pad[:, 0:2, 8:72, :] = xlo_ref[...]
    pad[:, 10:12, 8:72, :] = xhi_ref[...]
    pad[:, :, 6:8, :] = ylo_ref[...]
    pad[:, :, 72:74, :] = yhi_ref[...]


def box(field_sum):
    along = field_sum[:, 0:64] + field_sum[:, 1:65] + field_sum[:, 2:66]
    return (along + roll_z(along, 1) + roll_z(along, CZ - 1)) * (1.0 / 27.0)


def roll_z(x, by):
    return pltpu.roll(x, by, x.ndim - 1)


def stress_blocks(pad):
    out = [None] * 12
    for px in range(2):
        first = 1 + px * 4
        planes = [[pad[c, first + i, 7:73, :] for i in range(6)] for c in range(3)]
        smooth = []
        for c in range(3):
            sums = jnp.stack([planes[c][i] + planes[c][i + 1] + planes[c][i + 2] for i in range(4)])
            smooth.append(box(sums))
        for k, (a, b) in enumerate(PAIRS):
            prod = [planes[a][i] * planes[b][i] for i in range(6)]
            sums = jnp.stack([prod[i] + prod[i + 1] + prod[i + 2] for i in range(4)])
            value = box(sums) - smooth[a] * smooth[b]
            out[k * 2 + px] = value.astype(BF16).reshape(256, 128)
    return out


def multiplicity(index_ref, count_ref):
    index = index_ref[...]
    selected = index.shape[1]
    live = lax.broadcasted_iota(jnp.int32, (16, selected), 1) < count_ref[0]
    high = lax.broadcasted_iota(jnp.int32, (16, selected), 0) == (index >> 7)
    left = jnp.where(high & live, 1.0, 0.0).astype(BF16)
    low = lax.broadcasted_iota(jnp.int32, (128, selected), 0) == (index & 127)
    right = jnp.where(low, 1.0, 0.0).astype(BF16)
    return dot_nt(left, right)


def backward_kernel(row_scale, rows, in_order, order_ref, count_ref, index_ref, v_ref, xlo_ref, xhi_ref, ylo_ref, yhi_ref, p_ref, row_ref, lane_ref,
                    feat_ref, x_ref, a_ref, d_ref, pred_ref, *rest):
    if in_order:
        send_out, keep_out, pad, w0, w1, w2, wo, grads = rest
    else:
        grads, pad, w0, w1, w2, wo = rest
    load_weights(p_ref, w0, w1, w2, wo)
    weight = multiplicity(index_ref, count_ref) * row_scale
    weight = jnp.concatenate([weight[q : q + 1] for q in range(8)], axis=1)
    fill_padded(pad, v_ref, xlo_ref, xhi_ref, ylo_ref, yhi_ref)
    target = cells_to_patches(stress_blocks(pad), row_ref[...], lane_ref[...], feat_ref[...], 6)
    error = ((pred_ref[...] - target.astype(F32)) * weight).astype(BF16)
    grad = dot_nt(a_ref[2], error)
    for k in range(3):
        grads[pl.ds(WO_AT + k, HID, stride=3), :] = grad[:, k * 128 : (k + 1) * 128]
    up = dot(wo[...], error)
    for layer, at, size, w in ((2, W2_AT, HID, w2), (1, W1_AT, HID, w1), (0, 0, FEAT, None)):
        slope = (up * d_ref[layer]).astype(BF16)
        left = a_ref[layer - 1] if layer else x_ref[...]
        grad = dot_nt(left, slope)
        for k in range(4):
            grads[pl.ds(at + k, size, stride=4), :] = grad[:, k * 128 : (k + 1) * 128]
        if layer:
            up = dot(w[...], slope)
    if in_order:
        half = keep_out.shape[0]

        def place(i, carry):
            here = pl.multiple_of(order_ref[i + half] * rows, 8)
            send_out[i] = grads[pl.ds(here, rows), :].astype(BF16)
            here = pl.multiple_of(order_ref[i] * rows, 8)
            keep_out[i] = grads[pl.ds(here, rows), :]
            return carry

        lax.fori_loop(0, half, place, 0)


def substep(now, after_x, before_x, after_y, before_y):
    after_z = [roll_z(f, CZ - 1) for f in now]
    before_z = [roll_z(f, 1) for f in now]
    out = []
    for c in range(3):
        transport = now[0] * (0.5 * (after_x[c] - before_x[c]))
        transport = transport + now[1] * (0.5 * (after_y[c] - before_y[c]))
        transport = transport + now[2] * (0.5 * (after_z[c] - before_z[c]))
        laplace = after_x[c] + before_x[c] + after_y[c] + before_y[c] + after_z[c] + before_z[c] - 6.0 * now[c]
        out.append(now[c] + STEP_DT * (VISCOSITY * laplace - transport))
    return out


def flow_kernel(v_ref, xlo_ref, xhi_ref, ylo_ref, yhi_ref, row_ref, lane_ref, feat_ref, flow_out, x_out, pad, mid):
    fill_padded(pad, v_ref, xlo_ref, xhi_ref, ylo_ref, yhi_ref)
    for src, dst, first, count, low, high in ((pad, mid, 1, 10, 7, 73), (mid, flow_out, 2, 8, 8, 72)):
        for i in range(first, first + count):
            now = [src[c, i, low:high, :] for c in range(3)]
            after_x = [src[c, i + 1, low:high, :] for c in range(3)]
            before_x = [src[c, i - 1, low:high, :] for c in range(3)]
            after_y = [src[c, i, low + 1 : high + 1, :] for c in range(3)]
            before_y = [src[c, i, low - 1 : high - 1, :] for c in range(3)]
            new = substep(now, after_x, before_x, after_y, before_y)
            for c in range(3):
                if dst is mid:
                    mid[c, i, low:high, :] = new[c]
                else:
                    flow_out[c, i - 2] = new[c]
    x_out[...] = cells_to_patches(velocity_blocks(flow_out), row_ref[...], lane_ref[...], feat_ref[...], 3)


def model_kernel(rows, in_order, order_ref, p_ref, own_ref, other_ref, x_ref, row_ref, lane_ref, feat_ref, p_out, s_out, xfirst, xlast, yfirst, ylast, w0, w1, w2, wo):
    half = own_ref.shape[0]
    if in_order:

        def place(i, carry):
            here = pl.ds(pl.multiple_of(order_ref[i] * rows, 8), rows)
            p_out[here, :] = p_ref[here, :] - own_ref[i].astype(F32)
            here = pl.ds(pl.multiple_of(order_ref[i + half] * rows, 8), rows)
            p_out[here, :] = p_ref[here, :] - other_ref[i].astype(F32)
            return carry

        lax.fori_loop(0, half, place, 0)
    else:
        p_out[...] = p_ref[...] - own_ref[...].astype(F32)
    load_weights(p_out, w0, w1, w2, wo)
    hidden = x_ref[...]
    for w in (w0, w1, w2):
        z = dot_tn(w[...], hidden)
        hidden = (z * (0.5 * jnp.tanh(0.5 * z) + 0.5)).astype(BF16)
    modelled = dot_tn(wo[...], hidden).astype(BF16)
    blocks = patches_to_cells(modelled, row_ref[...], lane_ref[...], feat_ref[...], 6)
    for k in range(6):
        for px in range(2):
            s_out[k, px * 4 : px * 4 + 4] = blocks[k * 2 + px].reshape(4, 64, 128)
    for n, k in enumerate((0, 3, 4)):
        xfirst[n] = s_out[k, 0].astype(BF16)
        xlast[n] = s_out[k, CX - 1].astype(BF16)
    for n, k in enumerate((3, 1, 5)):
        yfirst[n] = s_out[k, :, 0, :].astype(BF16)
        ylast[n] = s_out[k, :, CY - 1, :].astype(BF16)


def force_kernel(s_ref, flow_ref, xlo_ref, xhi_ref, ylo_ref, yhi_ref, v_out, force_out, pad):
    pad[:, :, 8:72, :] = jnp.stack([s_ref[k] for k in (3, 1, 5)])
    pad[:, :, 7, :] = ylo_ref[...].astype(F32)
    pad[:, :, 72, :] = yhi_ref[...].astype(F32)
    for i in range(3):
        kx, kz = COMPONENT[i][0], COMPONENT[i][2]
        for x in range(CX):
            after = s_ref[kx, x + 1] if x < CX - 1 else xhi_ref[i].astype(F32)
            before = s_ref[kx, x - 1] if x else xlo_ref[i].astype(F32)
            total = 0.5 * (after - before)
            total = total + 0.5 * (pad[i, x, 9:73, :] - pad[i, x, 7:71, :])
            centre = s_ref[kz, x]
            total = total + 0.5 * (roll_z(centre, CZ - 1) - roll_z(centre, 1))
            force = -SGS_SCALE * total
            force_out[i, x] = force
            v_out[i, x] = flow_ref[i, x] + force


def call(kernel, outs, args, scratch, scalars=0, flops=0, name=None):
    vm = pl.BlockSpec(memory_space=pltpu.VMEM)
    sm = pl.BlockSpec(memory_space=pltpu.SMEM)
    size = sum(a.size * a.dtype.itemsize for a in args) + sum(int(np.prod(s)) * np.dtype(t).itemsize for s, t in outs)
    return pl.pallas_call(
        kernel,
        out_shape=[jax.ShapeDtypeStruct(s, t) for s, t in outs],
        in_specs=[sm] * scalars + [vm] * (len(args) - scalars),
        out_specs=[vm] * len(outs),
        scratch_shapes=[pltpu.VMEM(s, t) for s, t in scratch],
        compiler_params=pltpu.CompilerParams(vmem_limit_bytes=VMEM_LIMIT),
        cost_estimate=pl.CostEstimate(flops=flops, transcendentals=0, bytes_accessed=size),
        name=name,
    )(*args)


WEIGHTS = [((FEAT, HID), BF16), ((HID, HID), BF16), ((HID, HID), BF16), ((HID, TGT), BF16)]
PADDED = ((3, 12, 80, 128), F32)


def bits(size):
    return [1 << i for i in range(size.bit_length() - 1)]


def stage_masks(n_role, n_tile):
    role = [n_tile * b for b in bits(n_role)]
    tile = bits(n_tile)
    rest = tile[:1] + role[1:] + tile[1:]
    other = rest[1::-1] + rest[2:]
    return role[:1] + rest, role[:1] + other


def shifts(axis):
    size = lax.axis_size(axis)
    up = [(i, (i + 1) % size) for i in range(size)]
    return up, [(j, i) for i, j in up]


def local(velocity, params, first_moment, second_moment, patch_index, patch_count):
    n_role, n_tile = lax.axis_size("role"), lax.axis_size("tile")
    devices = n_role * n_tile
    own_rank = lax.axis_index(BOTH)
    rows = ROWS // devices
    in_order = rows % 8 == 0
    masks = stage_masks(n_role, n_tile)
    steps = len(masks[0])
    core_of = [(d // n_tile) & 1 for d in range(devices)]

    def exchange(x, step):
        pairs = [(d, d ^ masks[core_of[d]][step]) for d in range(devices)]
        return lax.ppermute(x, BOTH, pairs)

    def offsets(core):
        return [
            functools.reduce(lambda a, b: a ^ b, [masks[core][i] if (j >> (steps - 1 - i)) & 1 else 0 for i in range(steps)])
            for j in range(devices)
        ]

    half = devices // 2
    both = [offsets(0), offsets(1)]
    table = np.array([both[c][:half] + both[1 - c][half:] for c in range(2)], np.int32)
    order = own_rank ^ jnp.where((own_rank // n_tile) % 2 == 0, table[0], table[1])

    row_mat, lane_mat, feat_mat = (jnp.asarray(m, BF16) for m in (row_matrix(), lane_matrix(), feature_matrix()))
    mats = [row_mat, lane_mat, feat_mat]
    p2 = params.reshape(ROWS, 128)
    selected = patch_index.shape[0]
    row_scale = 1.0 / (selected // 4)

    up, down = shifts("role")
    xlo = lax.ppermute(velocity[:, CX - 2 :], "role", up)
    xhi = lax.ppermute(velocity[:, :2], "role", down)
    x, act, slope, pred = call(
        forward_kernel,
        [((FEAT, NPATCH), BF16), ((3, HID, NPATCH), BF16), ((3, HID, NPATCH), F32), ((TGT, NPATCH), F32)],
        [velocity, p2] + mats,
        WEIGHTS,
        flops=2 * 819200 * NPATCH,
        name="forward",
    )
    up, down = shifts("tile")
    last = jnp.concatenate([xlo[:, :, CY - 2 :], velocity[:, :, CY - 2 :], xhi[:, :, CY - 2 :]], axis=1)
    first = jnp.concatenate([xlo[:, :, :2], velocity[:, :, :2], xhi[:, :, :2]], axis=1)
    ylo = lax.ppermute(last, "tile", up)
    yhi = lax.ppermute(first, "tile", down)
    halos = [xlo, xhi, ylo, yhi]

    grad_outs = [((half, rows, 128), BF16), ((half, rows, 128), F32)] if in_order else [((ROWS, 128), F32)]
    grads = call(
        functools.partial(backward_kernel, row_scale, rows, in_order),
        grad_outs,
        [order, patch_count, patch_index.reshape(1, selected), velocity] + halos + [p2] + mats + [x, act, slope, pred],
        [PADDED] + WEIGHTS + ([((ROWS, 128), F32)] if in_order else []),
        scalars=2,
        flops=4 * 819200 * NPATCH,
        name="backward",
    )
    if in_order:
        send, keep = grads
    else:
        placed = grads[0].reshape(devices, rows, 128)[order]
        send, keep = placed[half:].astype(BF16), placed[:half]

    got = exchange(send, 0)
    flow, x_new = call(
        flow_kernel,
        [((3, CX, CY, CZ), F32), ((FEAT, NPATCH), BF16)],
        [velocity] + halos + mats,
        [PADDED, PADDED],
        flops=1 << 30,
        name="flow",
    )
    size = half
    for step in range(1, steps):
        size //= 2
        send = (keep[size:] + got[size:].astype(F32)).astype(BF16)
        keep = keep[:size] + got[:size].astype(F32)
        got = exchange(send, step)
    grad = (keep + got.astype(F32)).reshape(-1)
    first_out = BETA_ONE * first_moment + (1.0 - BETA_ONE) * grad
    second_out = BETA_TWO * second_moment + (1.0 - BETA_TWO) * grad * grad
    fix_first = 1.0 - BETA_ONE**ADAM_STEP
    fix_second = 1.0 - BETA_TWO**ADAM_STEP
    update = LEARN_RATE * (first_out / fix_first) / (jnp.sqrt(second_out / fix_second) + EPSILON)
    held = update.astype(BF16).reshape(1, rows, 128)
    for step in range(steps - 1, 0, -1):
        held = jnp.concatenate([held, exchange(held, step)], axis=0)
    other = exchange(held, 0)
    if not in_order:
        slots = jnp.zeros((devices,), jnp.int32).at[order].set(jnp.arange(devices, dtype=jnp.int32))
        held = other = jnp.concatenate([held, other], axis=0)[slots].reshape(ROWS, 128)

    p_new, stress, xfirst, xlast, yfirst, ylast = call(
        functools.partial(model_kernel, rows, in_order),
        [((ROWS, 128), F32), ((6, CX, CY, CZ), F32)] + [((3, CY, CZ), BF16)] * 2 + [((3, CX, CZ), BF16)] * 2,
        [order, p2, held, other, x_new] + mats,
        WEIGHTS,
        scalars=1,
        flops=2 * 819200 * NPATCH,
        name="model",
    )
    up, down = shifts("role")
    sxlo = lax.ppermute(xlast, "role", up)
    sxhi = lax.ppermute(xfirst, "role", down)
    up, down = shifts("tile")
    sylo = lax.ppermute(ylast, "tile", up)
    syhi = lax.ppermute(yfirst, "tile", down)
    velocity_out, sgs_force = call(
        force_kernel,
        [((3, CX, CY, CZ), F32)] * 2,
        [stress, flow, sxlo, sxhi, sylo, syhi],
        [((3, CX, 80, CZ), F32)],
        name="force",
    )
    return (velocity_out, sgs_force, p_new.reshape(-1), first_out, second_out)


def solution(mesh):
    placed = (
        P(None, "role", "tile", None),
        P(),
        P(BOTH),
        P(BOTH),
        P(BOTH),
        P(BOTH),
    )
    return jax.shard_map(
        local,
        mesh=mesh,
        in_specs=placed,
        out_specs=(
            P(None, "role", "tile", None),
            P(None, "role", "tile", None),
            P(),
            P(BOTH),
            P(BOTH),
        ),
        check_vma=False,
    )
```

```python
import functools

import jax
import jax.numpy as jnp
import numpy as np
from jax import lax
from jax.experimental import pallas as pl
from jax.experimental.pallas import tpu as pltpu
from jax.sharding import PartitionSpec as P

FEAT = 192
TGT = 384
HID = 512
ADAM_STEP = 100
STEP_DT = 0.1
VISCOSITY = 0.1
SGS_SCALE = 1.5
BETA_ONE = 0.9
BETA_TWO = 0.999
LEARN_RATE = 0.001
EPSILON = 1e-08
PAIRS = ((0, 0), (1, 1), (2, 2), (0, 1), (0, 2), (1, 2))
COMPONENT = ((0, 3, 4), (3, 1, 5), (4, 5, 2))

CX, CY, CZ = 8, 64, 128
NPATCH = 1024
ROWS = 6400
W1_AT = 768
W2_AT = W1_AT + 2048
WO_AT = W2_AT + 2048
BOTH = ("role", "tile")
F32, BF16 = jnp.float32, jnp.bfloat16
VMEM_LIMIT = 24 * 1024 * 1024


def row_matrix():
    matrix = np.zeros((256, 256), np.float32)
    for dx in range(4):
        for j in range(4):
            for pyl in range(4):
                for dy in range(4):
                    matrix[pyl * 64 + j * 16 + dx * 4 + dy, dx * 64 + j * 16 + pyl * 4 + dy] = 1
    return matrix


def lane_matrix():
    matrix = np.zeros((512, 512), np.float32)
    for pyl in range(4):
        for pz in range(32):
            for dz in range(4):
                matrix[pyl * 128 + pz * 4 + dz, dz * 128 + pyl * 32 + pz] = 1
    return matrix


def feature_matrix():
    matrix = np.zeros((128, 128), np.float32)
    for c in range(2):
        for off in range(16):
            for dz in range(4):
                matrix[c * 64 + off * 4 + dz, c * 64 + dz * 16 + off] = 1
    return matrix


def dot(a, b):
    return jnp.dot(a, b, preferred_element_type=F32)


def dot_tn(a, b):
    return lax.dot_general(a, b, (((0,), (0,)), ((), ())), preferred_element_type=F32)


def dot_nt(a, b):
    return lax.dot_general(a, b, (((1,), (1,)), ((), ())), preferred_element_type=F32)


def permute_features(feature_mat, x, channels):
    pieces = []
    at = 0
    while at < channels * 64:
        size = min(128, channels * 64 - at)
        pieces.append(dot(feature_mat[:size, :size], x[at : at + size]).astype(BF16))
        at += size
    return jnp.concatenate(pieces, axis=0)


def cells_to_patches(blocks, row_mat, lane_mat, feature_mat, channels):
    moved = dot(row_mat, jnp.concatenate(blocks, axis=1)).astype(BF16)
    rows = []
    for i in range(2 * channels):
        part = moved[:, i * 128 : (i + 1) * 128]
        rows.append(jnp.concatenate([part[p * 64 : (p + 1) * 64] for p in range(4)], axis=1))
    spread = dot(jnp.concatenate(rows, axis=0), lane_mat).astype(BF16)
    bands = []
    for c in range(channels):
        for dz in range(4):
            bands.append(
                jnp.concatenate(
                    [
                        spread[((c * 2 + px) * 4 + j) * 16 : ((c * 2 + px) * 4 + j) * 16 + 16, dz * 128 : dz * 128 + 128]
                        for px in range(2)
                        for j in range(4)
                    ],
                    axis=1,
                )
            )
    return permute_features(feature_mat, jnp.concatenate(bands, axis=0), channels)


def patches_to_cells(x, row_mat, lane_mat, feature_mat, channels):
    pieces = []
    for at in range(0, channels * 64, 128):
        pieces.append(dot_tn(feature_mat, x[at : at + 128]).astype(BF16))
    x = jnp.concatenate(pieces, axis=0)
    rows = []
    for c in range(channels):
        for px in range(2):
            for j in range(4):
                lanes = (px * 4 + j) * 128
                rows.append(
                    jnp.concatenate(
                        [x[c * 64 + dz * 16 : c * 64 + dz * 16 + 16, lanes : lanes + 128] for dz in range(4)], axis=1
                    )
                )
    spread = dot_nt(jnp.concatenate(rows, axis=0), lane_mat).astype(BF16)
    columns = []
    for i in range(2 * channels):
        part = spread[i * 64 : (i + 1) * 64]
        columns.append(jnp.concatenate([part[:, p * 128 : (p + 1) * 128] for p in range(4)], axis=0))
    moved = dot_tn(row_mat, jnp.concatenate(columns, axis=1))
    return [moved[:, i * 128 : (i + 1) * 128] for i in range(2 * channels)]


def load_weights(p_ref, w0, w1, w2, wo):
    for k in range(4):
        lanes = slice(k * 128, (k + 1) * 128)
        w0[:, lanes] = p_ref[pl.ds(k, FEAT, stride=4), :].astype(BF16)
        w1[:, lanes] = p_ref[pl.ds(W1_AT + k, HID, stride=4), :].astype(BF16)
        w2[:, lanes] = p_ref[pl.ds(W2_AT + k, HID, stride=4), :].astype(BF16)
    for k in range(3):
        wo[:, k * 128 : (k + 1) * 128] = p_ref[pl.ds(WO_AT + k, HID, stride=3), :].astype(BF16)


def velocity_blocks(v_ref):
    return [
        v_ref[c, px * 4 : px * 4 + 4].reshape(256, 128).astype(BF16) for c in range(3) for px in range(2)
    ]


def layer(w, hidden, a_out, d_out):
    z = dot_tn(w[...], hidden)
    s = 0.5 * jnp.tanh(0.5 * z) + 0.5
    a = z * s
    d_out[...] = s + a * (1.0 - s)
    hidden = a.astype(BF16)
    a_out[...] = hidden
    return hidden


def forward_first_kernel(v_ref, p_ref, row_ref, lane_ref, feat_ref, x_out, a_out, d_out, w0, w1, w2, wo):
    load_weights(p_ref, w0, w1, w2, wo)
    x = cells_to_patches(velocity_blocks(v_ref), row_ref[...], lane_ref[...], feat_ref[...], 3)
    x_out[...] = x
    layer(w0, x, a_out, d_out)


def forward_rest_kernel(a1_ref, w1, w2, wo, a2_out, d2_out, a3_out, d3_out, pred_out):
    hidden = layer(w1, a1_ref[...], a2_out, d2_out)
    hidden = layer(w2, hidden, a3_out, d3_out)
    pred_out[...] = dot_tn(wo[...], hidden)


def fill_padded(pad, v_ref, xlo_ref, xhi_ref, ylo_ref, yhi_ref):
    pad[:, 2:10, 8:72, :] = v_ref[...]
    pad[:, 0:2, 8:72, :] = xlo_ref[...]
    pad[:, 10:12, 8:72, :] = xhi_ref[...]
    pad[:, :, 6:8, :] = ylo_ref[...]
    pad[:, :, 72:74, :] = yhi_ref[...]


def box(field_sum):
    along = field_sum[:, 0:64] + field_sum[:, 1:65] + field_sum[:, 2:66]
    return (along + roll_z(along, 1) + roll_z(along, CZ - 1)) * (1.0 / 27.0)


def roll_z(x, by):
    return pltpu.roll(x, by, x.ndim - 1)


def stress_blocks(pad):
    out = [None] * 12
    for px in range(2):
        first = 1 + px * 4
        planes = [[pad[c, first + i, 7:73, :] for i in range(6)] for c in range(3)]
        smooth = []
        for c in range(3):
            sums = jnp.stack([planes[c][i] + planes[c][i + 1] + planes[c][i + 2] for i in range(4)])
            smooth.append(box(sums))
        for k, (a, b) in enumerate(PAIRS):
            prod = [planes[a][i] * planes[b][i] for i in range(6)]
            sums = jnp.stack([prod[i] + prod[i + 1] + prod[i + 2] for i in range(4)])
            value = box(sums) - smooth[a] * smooth[b]
            out[k * 2 + px] = value.astype(BF16).reshape(256, 128)
    return out


def multiplicity(index_ref, count_ref):
    index = index_ref[...]
    selected = index.shape[1]
    live = lax.broadcasted_iota(jnp.int32, (16, selected), 1) < count_ref[0]
    high = lax.broadcasted_iota(jnp.int32, (16, selected), 0) == (index >> 7)
    left = jnp.where(high & live, 1.0, 0.0).astype(BF16)
    low = lax.broadcasted_iota(jnp.int32, (128, selected), 0) == (index & 127)
    right = jnp.where(low, 1.0, 0.0).astype(BF16)
    return dot_nt(left, right)


def backward_kernel(row_scale, rows, in_order, order_ref, count_ref, index_ref, v_ref, xlo_ref, xhi_ref, ylo_ref, yhi_ref, row_ref, lane_ref,
                    feat_ref, w1, w2, wo, x_ref, a1_ref, a2_ref, a3_ref, d1_ref, d2_ref, d3_ref, pred_ref, *rest):
    if in_order:
        send_out, keep_out, pad, grads = rest
    else:
        grads, pad = rest
    weight = multiplicity(index_ref, count_ref) * row_scale
    weight = jnp.concatenate([weight[q : q + 1] for q in range(8)], axis=1)
    fill_padded(pad, v_ref, xlo_ref, xhi_ref, ylo_ref, yhi_ref)
    target = cells_to_patches(stress_blocks(pad), row_ref[...], lane_ref[...], feat_ref[...], 6)
    error = ((pred_ref[...] - target.astype(F32)) * weight).astype(BF16)
    grad = dot_nt(a3_ref[...], error)
    for k in range(3):
        grads[pl.ds(WO_AT + k, HID, stride=3), :] = grad[:, k * 128 : (k + 1) * 128]
    up = dot(wo[...], error)
    for d_ref, left_ref, at, w in ((d3_ref, a2_ref, W2_AT, w2), (d2_ref, a1_ref, W1_AT, w1), (d1_ref, x_ref, 0, None)):
        slope = (up * d_ref[...]).astype(BF16)
        grad = dot_nt(left_ref[...], slope)
        size = left_ref.shape[0]
        for k in range(4):
            grads[pl.ds(at + k, size, stride=4), :] = grad[:, k * 128 : (k + 1) * 128]
        if w is not None:
            up = dot(w[...], slope)
    if in_order:
        half = keep_out.shape[0]

        def place(i, carry):
            here = pl.multiple_of(order_ref[i + half] * rows, 8)
            send_out[i] = grads[pl.ds(here, rows), :].astype(BF16)
            here = pl.multiple_of(order_ref[i] * rows, 8)
            keep_out[i] = grads[pl.ds(here, rows), :]
            return carry

        lax.fori_loop(0, half, place, 0)


def substep(now, after_x, before_x, after_y, before_y):
    after_z = [roll_z(f, CZ - 1) for f in now]
    before_z = [roll_z(f, 1) for f in now]
    out = []
    for c in range(3):
        transport = now[0] * (0.5 * (after_x[c] - before_x[c]))
        transport = transport + now[1] * (0.5 * (after_y[c] - before_y[c]))
        transport = transport + now[2] * (0.5 * (after_z[c] - before_z[c]))
        laplace = after_x[c] + before_x[c] + after_y[c] + before_y[c] + after_z[c] + before_z[c] - 6.0 * now[c]
        out.append(now[c] + STEP_DT * (VISCOSITY * laplace - transport))
    return out


def flow_kernel(v_ref, xlo_ref, xhi_ref, ylo_ref, yhi_ref, row_ref, lane_ref, feat_ref, flow_out, x_out, pad, mid):
    fill_padded(pad, v_ref, xlo_ref, xhi_ref, ylo_ref, yhi_ref)
    for src, dst, first, count, low, high in ((pad, mid, 1, 10, 7, 73), (mid, flow_out, 2, 8, 8, 72)):
        for i in range(first, first + count):
            now = [src[c, i, low:high, :] for c in range(3)]
            after_x = [src[c, i + 1, low:high, :] for c in range(3)]
            before_x = [src[c, i - 1, low:high, :] for c in range(3)]
            after_y = [src[c, i, low + 1 : high + 1, :] for c in range(3)]
            before_y = [src[c, i, low - 1 : high - 1, :] for c in range(3)]
            new = substep(now, after_x, before_x, after_y, before_y)
            for c in range(3):
                if dst is mid:
                    mid[c, i, low:high, :] = new[c]
                else:
                    flow_out[c, i - 2] = new[c]
    x_out[...] = cells_to_patches(velocity_blocks(flow_out), row_ref[...], lane_ref[...], feat_ref[...], 3)


def model_kernel(rows, in_order, order_ref, p_ref, own_ref, other_ref, x_ref, row_ref, lane_ref, feat_ref, p_out, s_out, xfirst, xlast, yfirst, ylast, w0, w1, w2, wo):
    half = own_ref.shape[0]
    if in_order:

        def place(i, carry):
            here = pl.ds(pl.multiple_of(order_ref[i] * rows, 8), rows)
            p_out[here, :] = p_ref[here, :] - own_ref[i].astype(F32)
            here = pl.ds(pl.multiple_of(order_ref[i + half] * rows, 8), rows)
            p_out[here, :] = p_ref[here, :] - other_ref[i].astype(F32)
            return carry

        lax.fori_loop(0, half, place, 0)
    else:
        p_out[...] = p_ref[...] - own_ref[...].astype(F32)
    load_weights(p_out, w0, w1, w2, wo)
    hidden = x_ref[...]
    for w in (w0, w1, w2):
        z = dot_tn(w[...], hidden)
        hidden = (z * (0.5 * jnp.tanh(0.5 * z) + 0.5)).astype(BF16)
    modelled = dot_tn(wo[...], hidden).astype(BF16)
    blocks = patches_to_cells(modelled, row_ref[...], lane_ref[...], feat_ref[...], 6)
    for k in range(6):
        for px in range(2):
            s_out[k, px * 4 : px * 4 + 4] = blocks[k * 2 + px].reshape(4, 64, 128)
    for n, k in enumerate((0, 3, 4)):
        xfirst[n] = s_out[k, 0].astype(BF16)
        xlast[n] = s_out[k, CX - 1].astype(BF16)
    for n, k in enumerate((3, 1, 5)):
        yfirst[n] = s_out[k, :, 0, :].astype(BF16)
        ylast[n] = s_out[k, :, CY - 1, :].astype(BF16)


def force_kernel(s_ref, flow_ref, xlo_ref, xhi_ref, ylo_ref, yhi_ref, v_out, force_out, pad):
    pad[:, :, 8:72, :] = jnp.stack([s_ref[k] for k in (3, 1, 5)])
    pad[:, :, 7, :] = ylo_ref[...].astype(F32)
    pad[:, :, 72, :] = yhi_ref[...].astype(F32)
    for i in range(3):
        kx, kz = COMPONENT[i][0], COMPONENT[i][2]
        for x in range(CX):
            after = s_ref[kx, x + 1] if x < CX - 1 else xhi_ref[i].astype(F32)
            before = s_ref[kx, x - 1] if x else xlo_ref[i].astype(F32)
            total = 0.5 * (after - before)
            total = total + 0.5 * (pad[i, x, 9:73, :] - pad[i, x, 7:71, :])
            centre = s_ref[kz, x]
            total = total + 0.5 * (roll_z(centre, CZ - 1) - roll_z(centre, 1))
            force = -SGS_SCALE * total
            force_out[i, x] = force
            v_out[i, x] = flow_ref[i, x] + force


def call(kernel, outs, args, scratch, scalars=0, flops=0, name=None, final=0):
    args = list(args[:scalars]) + [pltpu.with_memory_space_constraint(a, pltpu.VMEM) for a in args[scalars:]]
    vm = pl.BlockSpec(memory_space=pltpu.VMEM)
    sm = pl.BlockSpec(memory_space=pltpu.SMEM)
    size = sum(a.size * a.dtype.itemsize for a in args) + sum(int(np.prod(s)) * np.dtype(t).itemsize for s, t in outs)
    return pl.pallas_call(
        kernel,
        out_shape=[jax.ShapeDtypeStruct(s, t) if i < final else pltpu.VMEM(s, t) for i, (s, t) in enumerate(outs)],
        in_specs=[sm] * scalars + [vm] * (len(args) - scalars),
        out_specs=[vm] * len(outs),
        scratch_shapes=[pltpu.VMEM(s, t) for s, t in scratch],
        compiler_params=pltpu.CompilerParams(vmem_limit_bytes=VMEM_LIMIT),
        cost_estimate=pl.CostEstimate(flops=flops, transcendentals=0, bytes_accessed=size),
        name=name,
    )(*args)


WEIGHTS = [((FEAT, HID), BF16), ((HID, HID), BF16), ((HID, HID), BF16), ((HID, TGT), BF16)]
PADDED = ((3, 12, 80, 128), F32)
ACT = ((HID, NPATCH), BF16)
DER = ((HID, NPATCH), F32)


def bits(size):
    return [1 << i for i in range(size.bit_length() - 1)]


def stage_masks(n_role, n_tile):
    role = [n_tile * b for b in bits(n_role)]
    tile = bits(n_tile)
    rest = tile[:1] + role[1:] + tile[1:]
    other = rest[1::-1] + rest[2:]
    return role[:1] + rest, role[:1] + other


def shifts(axis):
    size = lax.axis_size(axis)
    up = [(i, (i + 1) % size) for i in range(size)]
    return up, [(j, i) for i, j in up]


def local(velocity, params, first_moment, second_moment, patch_index, patch_count):
    n_role, n_tile = lax.axis_size("role"), lax.axis_size("tile")
    devices = n_role * n_tile
    own_rank = lax.axis_index(BOTH)
    rows = ROWS // devices
    in_order = rows % 8 == 0
    masks = stage_masks(n_role, n_tile)
    steps = len(masks[0])
    core_of = [(d // n_tile) & 1 for d in range(devices)]

    def exchange(x, step):
        pairs = [(d, d ^ masks[core_of[d]][step]) for d in range(devices)]
        return lax.ppermute(x, BOTH, pairs)

    def offsets(core):
        return [
            functools.reduce(lambda a, b: a ^ b, [masks[core][i] if (j >> (steps - 1 - i)) & 1 else 0 for i in range(steps)])
            for j in range(devices)
        ]

    half = devices // 2
    both = [offsets(0), offsets(1)]
    table = np.array([both[c][:half] + both[1 - c][half:] for c in range(2)], np.int32)
    order = own_rank ^ jnp.where((own_rank // n_tile) % 2 == 0, table[0], table[1])

    row_mat, lane_mat, feat_mat = (jnp.asarray(m, BF16) for m in (row_matrix(), lane_matrix(), feature_matrix()))
    mats = [row_mat, lane_mat, feat_mat]
    p2 = params.reshape(ROWS, 128)
    selected = patch_index.shape[0]
    row_scale = 1.0 / (selected // 4)

    up, down = shifts("role")
    xlo = lax.ppermute(velocity[:, CX - 2 :], "role", up)
    xhi = lax.ppermute(velocity[:, :2], "role", down)
    x, a1, d1, *weights = call(
        forward_first_kernel,
        [((FEAT, NPATCH), BF16), ACT, DER] + WEIGHTS,
        [velocity, p2] + mats,
        [],
        flops=2 * FEAT * HID * NPATCH,
        name="forward_first",
    )
    xlo, xhi, a1 = lax.optimization_barrier((xlo, xhi, a1))
    up, down = shifts("tile")
    last = jnp.concatenate([xlo[:, :, CY - 2 :], velocity[:, :, CY - 2 :], xhi[:, :, CY - 2 :]], axis=1)
    first = jnp.concatenate([xlo[:, :, :2], velocity[:, :, :2], xhi[:, :, :2]], axis=1)
    ylo = lax.ppermute(last, "tile", up)
    yhi = lax.ppermute(first, "tile", down)
    a2, d2, a3, d3, pred = call(
        forward_rest_kernel,
        [ACT, DER, ACT, DER, ((TGT, NPATCH), F32)],
        [a1] + weights[1:],
        [],
        flops=2 * (819200 - FEAT * HID) * NPATCH,
        name="forward_rest",
    )
    halos = [xlo, xhi, ylo, yhi]

    grad_outs = [((half, rows, 128), BF16), ((half, rows, 128), F32)] if in_order else [((ROWS, 128), F32)]
    grads = call(
        functools.partial(backward_kernel, row_scale, rows, in_order),
        grad_outs,
        [order, patch_count, patch_index.reshape(1, selected), velocity]
        + halos
        + mats
        + weights[1:]
        + [x, a1, a2, a3, d1, d2, d3, pred],
        [PADDED] + ([((ROWS, 128), F32)] if in_order else []),
        scalars=2,
        flops=4 * 819200 * NPATCH,
        name="backward",
    )
    if in_order:
        send, keep = grads
    else:
        placed = grads[0].reshape(devices, rows, 128)[order]
        send, keep = placed[half:].astype(BF16), placed[:half]

    size = half
    got = exchange(send, 0)
    for step in range(1, steps):
        size //= 2
        send = (keep[size:] + got[size:].astype(F32)).astype(BF16)
        keep = keep[:size] + got[:size].astype(F32)
        if step == 1:
            send, still = lax.optimization_barrier((send, velocity))
        got = exchange(send, step)
        if step == 1:
            flow, x_new = call(
                flow_kernel,
                [((3, CX, CY, CZ), F32), ((FEAT, NPATCH), BF16)],
                [still] + halos + mats,
                [PADDED, PADDED],
                flops=1 << 30,
                name="flow",
            )
            got, flow, x_new = lax.optimization_barrier((got, flow, x_new))
    grad = (keep + got.astype(F32)).reshape(-1)
    first_out = BETA_ONE * first_moment + (1.0 - BETA_ONE) * grad
    second_out = BETA_TWO * second_moment + (1.0 - BETA_TWO) * grad * grad
    fix_first = 1.0 - BETA_ONE**ADAM_STEP
    fix_second = 1.0 - BETA_TWO**ADAM_STEP
    update = LEARN_RATE * (first_out / fix_first) / (jnp.sqrt(second_out / fix_second) + EPSILON)
    held = update.astype(BF16).reshape(1, rows, 128)
    for step in range(steps - 1, 0, -1):
        held = jnp.concatenate([held, exchange(held, step)], axis=0)
    other = exchange(held, 0)
    if not in_order:
        slots = jnp.zeros((devices,), jnp.int32).at[order].set(jnp.arange(devices, dtype=jnp.int32))
        held = other = jnp.concatenate([held, other], axis=0)[slots].reshape(ROWS, 128)

    p_new, stress, xfirst, xlast, yfirst, ylast = call(
        functools.partial(model_kernel, rows, in_order),
        [((ROWS, 128), F32), ((6, CX, CY, CZ), F32)] + [((3, CY, CZ), BF16)] * 2 + [((3, CX, CZ), BF16)] * 2,
        [order, p2, held, other, x_new] + mats,
        WEIGHTS,
        scalars=1,
        flops=2 * 819200 * NPATCH,
        final=1,
        name="model",
    )
    up, down = shifts("role")
    sxlo = lax.ppermute(xlast, "role", up)
    sxhi = lax.ppermute(xfirst, "role", down)
    up, down = shifts("tile")
    sylo = lax.ppermute(ylast, "tile", up)
    syhi = lax.ppermute(yfirst, "tile", down)
    velocity_out, sgs_force = call(
        force_kernel,
        [((3, CX, CY, CZ), F32)] * 2,
        [stress, flow, sxlo, sxhi, sylo, syhi],
        [((3, CX, 80, CZ), F32)],
        final=2,
        name="force",
    )
    return (velocity_out, sgs_force, p_new.reshape(-1), first_out, second_out)


def solution(mesh):
    placed = (
        P(None, "role", "tile", None),
        P(),
        P(BOTH),
        P(BOTH),
        P(BOTH),
        P(BOTH),
    )
    return jax.shard_map(
        local,
        mesh=mesh,
        in_specs=placed,
        out_specs=(
            P(None, "role", "tile", None),
            P(None, "role", "tile", None),
            P(),
            P(BOTH),
            P(BOTH),
        ),
        check_vma=False,
    )
```

```python
import functools

import jax
import jax.numpy as jnp
import numpy as np
from jax import lax
from jax.experimental import pallas as pl
from jax.experimental.pallas import tpu as pltpu
from jax.sharding import PartitionSpec as P

FEAT = 192
TGT = 384
HID = 512
ADAM_STEP = 100
STEP_DT = 0.1
VISCOSITY = 0.1
SGS_SCALE = 1.5
BETA_ONE = 0.9
BETA_TWO = 0.999
LEARN_RATE = 0.001
EPSILON = 1e-08
PAIRS = ((0, 0), (1, 1), (2, 2), (0, 1), (0, 2), (1, 2))
COMPONENT = ((0, 3, 4), (3, 1, 5), (4, 5, 2))

CX, CY, CZ = 8, 64, 128
NPATCH = 1024
ROWS = 6400
W1_AT = 768
W2_AT = W1_AT + 2048
WO_AT = W2_AT + 2048
BOTH = ("role", "tile")
F32, BF16 = jnp.float32, jnp.bfloat16
VMEM_LIMIT = 24 * 1024 * 1024


def row_matrix():
    matrix = np.zeros((256, 256), np.float32)
    for dx in range(4):
        for j in range(4):
            for pyl in range(4):
                for dy in range(4):
                    matrix[pyl * 64 + j * 16 + dx * 4 + dy, dx * 64 + j * 16 + pyl * 4 + dy] = 1
    return matrix


def lane_matrix():
    matrix = np.zeros((512, 512), np.float32)
    for pyl in range(4):
        for pz in range(32):
            for dz in range(4):
                matrix[pyl * 128 + pz * 4 + dz, dz * 128 + pyl * 32 + pz] = 1
    return matrix


def feature_matrix():
    matrix = np.zeros((128, 128), np.float32)
    for c in range(2):
        for off in range(16):
            for dz in range(4):
                matrix[c * 64 + off * 4 + dz, c * 64 + dz * 16 + off] = 1
    return matrix


def dot(a, b):
    return jnp.dot(a, b, preferred_element_type=F32)


def dot_tn(a, b):
    return lax.dot_general(a, b, (((0,), (0,)), ((), ())), preferred_element_type=F32)


def dot_nt(a, b):
    return lax.dot_general(a, b, (((1,), (1,)), ((), ())), preferred_element_type=F32)


def permute_features(feature_mat, x, channels):
    pieces = []
    at = 0
    while at < channels * 64:
        size = min(128, channels * 64 - at)
        pieces.append(dot(feature_mat[:size, :size], x[at : at + size]).astype(BF16))
        at += size
    return jnp.concatenate(pieces, axis=0)


def cells_to_patches(blocks, row_mat, lane_mat, feature_mat, channels):
    moved = dot(row_mat, jnp.concatenate(blocks, axis=1)).astype(BF16)
    rows = []
    for i in range(2 * channels):
        part = moved[:, i * 128 : (i + 1) * 128]
        rows.append(jnp.concatenate([part[p * 64 : (p + 1) * 64] for p in range(4)], axis=1))
    spread = dot(jnp.concatenate(rows, axis=0), lane_mat).astype(BF16)
    bands = []
    for c in range(channels):
        for dz in range(4):
            bands.append(
                jnp.concatenate(
                    [
                        spread[((c * 2 + px) * 4 + j) * 16 : ((c * 2 + px) * 4 + j) * 16 + 16, dz * 128 : dz * 128 + 128]
                        for px in range(2)
                        for j in range(4)
                    ],
                    axis=1,
                )
            )
    return permute_features(feature_mat, jnp.concatenate(bands, axis=0), channels)


def spread_rows(x, lane_mat):
    rows = [
        jnp.concatenate([x[at + dz * 16 : at + dz * 16 + 16] for dz in range(4)], axis=1) for at in range(0, x.shape[0], 64)
    ]
    return dot_nt(jnp.concatenate(rows, axis=0), lane_mat).astype(BF16)


def regroup_features(feature_mat, x):
    return jnp.concatenate(
        [dot_tn(feature_mat, x[at : at + 128]).astype(BF16) for at in range(0, x.shape[0], 128)], axis=0
    )


def rows_to_blocks(spread, row_mat):
    count = spread.shape[0] // 64
    columns = []
    for i in range(count):
        part = spread[i * 64 : (i + 1) * 64]
        columns.append(jnp.concatenate([part[:, p * 128 : (p + 1) * 128] for p in range(4)], axis=0))
    moved = dot_tn(row_mat, jnp.concatenate(columns, axis=1))
    return [moved[:, i * 128 : (i + 1) * 128] for i in range(count)]


def load_weights(p_ref, w0, w1, w2, wo):
    for k in range(4):
        lanes = slice(k * 128, (k + 1) * 128)
        w0[:, lanes] = p_ref[pl.ds(k, FEAT, stride=4), :].astype(BF16)
        w1[:, lanes] = p_ref[pl.ds(W1_AT + k, HID, stride=4), :].astype(BF16)
        w2[:, lanes] = p_ref[pl.ds(W2_AT + k, HID, stride=4), :].astype(BF16)
    for k in range(3):
        wo[:, k * 128 : (k + 1) * 128] = p_ref[pl.ds(WO_AT + k, HID, stride=3), :].astype(BF16)


def velocity_blocks(v_ref):
    return [
        v_ref[c, px * 4 : px * 4 + 4].reshape(256, 128).astype(BF16) for c in range(3) for px in range(2)
    ]


def layer(w, hidden, a_out, d_out):
    z = dot_tn(w[...], hidden)
    s = 0.5 * jnp.tanh(0.5 * z) + 0.5
    a = z * s
    d_out[...] = s + a * (1.0 - s)
    hidden = a.astype(BF16)
    a_out[...] = hidden
    return hidden


def forward_first_kernel(
    v_hbm, p_hbm, row_hbm, lane_hbm, feat_hbm, v_out, p_out, row_out, lane_out, feat_out, x_out, a_out, d_out, w0, w1, w2, wo, sems
):
    copies = [
        pltpu.make_async_copy(src, dst, sems.at[i])
        for i, (src, dst) in enumerate(
            ((v_hbm, v_out), (row_hbm, row_out), (lane_hbm, lane_out), (feat_hbm, feat_out), (p_hbm, p_out))
        )
    ]
    for copy in copies:
        copy.start()
    for copy in copies[:-1]:
        copy.wait()
    x = cells_to_patches(velocity_blocks(v_out), row_out[...], lane_out[...], feat_out[...], 3)
    x_out[...] = x
    copies[-1].wait()
    load_weights(p_out, w0, w1, w2, wo)
    layer(w0, x, a_out, d_out)


def parity(rank_ref, n_tile):
    rank = rank_ref[0]
    return (rank // n_tile) % 2 == 0, rank % 2 == 0


def strips_kernel(n_tile, rank_ref, v_ref, xa_ref, xb_ref, ya_out, yb_out):
    role_even, tile_even = parity(rank_ref, n_tile)

    def fill(first_out, last_out, low_ref, high_ref):
        for out, at in ((first_out, 0), (last_out, CY - 2)):
            out[:, 2:10] = v_ref[:, :, at : at + 2, :]
            out[:, 0:2] = low_ref[:, :, at : at + 2, :]
            out[:, 10:12] = high_ref[:, :, at : at + 2, :]

    for even_r in (True, False):
        for even_t in (True, False):

            @pl.when((role_even == even_r) & (tile_even == even_t))
            def _():
                first_out, last_out = (yb_out, ya_out) if even_t else (ya_out, yb_out)
                low_ref, high_ref = (xb_ref, xa_ref) if even_r else (xa_ref, xb_ref)
                fill(first_out, last_out, low_ref, high_ref)


def forward_rest_kernel(a1_ref, w1, w2, wo, a2_out, d2_out, a3_out, d3_out, pred_out):
    hidden = layer(w1, a1_ref[...], a2_out, d2_out)
    hidden = layer(w2, hidden, a3_out, d3_out)
    pred_out[...] = dot_tn(wo[...], hidden)


def fill_padded(pad, rank_ref, n_tile, v_ref, xa_ref, xb_ref, ya_ref, yb_ref):
    role_even, tile_even = parity(rank_ref, n_tile)
    pad[:, 2:10, 8:72, :] = v_ref[...]
    for even in (True, False):

        @pl.when(role_even == even)
        def _():
            pad[:, 0:2, 8:72, :] = (xb_ref if even else xa_ref)[...]
            pad[:, 10:12, 8:72, :] = (xa_ref if even else xb_ref)[...]

        @pl.when(tile_even == even)
        def _():
            pad[:, :, 6:8, :] = (yb_ref if even else ya_ref)[...]
            pad[:, :, 72:74, :] = (ya_ref if even else yb_ref)[...]


def block_of(position, rank, masks, n_tile, send):
    core = (rank // n_tile) % 2
    if send:
        core = 1 - core
    steps = len(masks[0])
    out = rank
    for i in range(steps):
        mask = jnp.where(core == 0, masks[0][i], masks[1][i])
        out = out ^ (((position >> (steps - 1 - i)) & 1) * mask)
    return out


def box(field_sum):
    along = field_sum[:, 0:64] + field_sum[:, 1:65] + field_sum[:, 2:66]
    return (along + roll_z(along, 1) + roll_z(along, CZ - 1)) * (1.0 / 27.0)


def roll_z(x, by):
    return pltpu.roll(x, by, x.ndim - 1)


def stress_blocks(pad):
    out = [None] * 12
    for px in range(2):
        first = 1 + px * 4
        planes = [[pad[c, first + i, 7:73, :] for i in range(6)] for c in range(3)]
        smooth = []
        for c in range(3):
            sums = jnp.stack([planes[c][i] + planes[c][i + 1] + planes[c][i + 2] for i in range(4)])
            smooth.append(box(sums))
        for k, (a, b) in enumerate(PAIRS):
            prod = [planes[a][i] * planes[b][i] for i in range(6)]
            sums = jnp.stack([prod[i] + prod[i + 1] + prod[i + 2] for i in range(4)])
            value = box(sums) - smooth[a] * smooth[b]
            out[k * 2 + px] = value.astype(BF16).reshape(256, 128)
    return out


def multiplicity(index_ref, count_ref):
    index = index_ref[...]
    selected = index.shape[1]
    live = lax.broadcasted_iota(jnp.int32, (16, selected), 1) < count_ref[0]
    high = lax.broadcasted_iota(jnp.int32, (16, selected), 0) == (index >> 7)
    left = jnp.where(high & live, 1.0, 0.0).astype(BF16)
    low = lax.broadcasted_iota(jnp.int32, (128, selected), 0) == (index & 127)
    right = jnp.where(low, 1.0, 0.0).astype(BF16)
    return dot_nt(left, right)


def backward_kernel(row_scale, rows, masks, n_tile, in_order, rank_ref, count_ref, index_ref, v_ref, xa_ref, xb_ref, ya_ref, yb_ref, row_ref, lane_ref,
                    feat_ref, w1, w2, wo, x_ref, a1_ref, a2_ref, a3_ref, d1_ref, d2_ref, d3_ref, pred_ref, *rest):
    if in_order:
        send_out, keep_out, pad, grads = rest
    else:
        grads, pad = rest
    weight = multiplicity(index_ref, count_ref) * row_scale
    weight = jnp.concatenate([weight[q : q + 1] for q in range(8)], axis=1)
    fill_padded(pad, rank_ref, n_tile, v_ref, xa_ref, xb_ref, ya_ref, yb_ref)
    target = cells_to_patches(stress_blocks(pad), row_ref[...], lane_ref[...], feat_ref[...], 6)
    error = ((pred_ref[...] - target.astype(F32)) * weight).astype(BF16)
    grad = dot_nt(a3_ref[...], error)
    for k in range(3):
        grads[pl.ds(WO_AT + k, HID, stride=3), :] = grad[:, k * 128 : (k + 1) * 128]
    up = dot(wo[...], error)
    for d_ref, left_ref, at, w in ((d3_ref, a2_ref, W2_AT, w2), (d2_ref, a1_ref, W1_AT, w1), (d1_ref, x_ref, 0, None)):
        slope = (up * d_ref[...]).astype(BF16)
        grad = dot_nt(left_ref[...], slope)
        size = left_ref.shape[0]
        for k in range(4):
            grads[pl.ds(at + k, size, stride=4), :] = grad[:, k * 128 : (k + 1) * 128]
        if w is not None:
            up = dot(w[...], slope)
    if in_order:
        half = keep_out.shape[0]

        def place(i, carry):
            here = pl.multiple_of(block_of(i + half, rank_ref[0], masks, n_tile, True) * rows, 8)
            send_out[i] = grads[pl.ds(here, rows), :].astype(BF16)
            here = pl.multiple_of(block_of(i, rank_ref[0], masks, n_tile, False) * rows, 8)
            keep_out[i] = grads[pl.ds(here, rows), :]
            return carry

        lax.fori_loop(0, half, place, 0)


def substep(now, after_x, before_x, after_y, before_y):
    after_z = [roll_z(f, CZ - 1) for f in now]
    before_z = [roll_z(f, 1) for f in now]
    out = []
    for c in range(3):
        transport = now[0] * (0.5 * (after_x[c] - before_x[c]))
        transport = transport + now[1] * (0.5 * (after_y[c] - before_y[c]))
        transport = transport + now[2] * (0.5 * (after_z[c] - before_z[c]))
        laplace = after_x[c] + before_x[c] + after_y[c] + before_y[c] + after_z[c] + before_z[c] - 6.0 * now[c]
        out.append(now[c] + STEP_DT * (VISCOSITY * laplace - transport))
    return out


def flow_kernel(n_tile, rank_ref, v_ref, xa_ref, xb_ref, ya_ref, yb_ref, row_ref, lane_ref, feat_ref, flow_out, x_out, xa_out, xb_out, ya_out, yb_out, pad, mid):
    fill_padded(pad, rank_ref, n_tile, v_ref, xa_ref, xb_ref, ya_ref, yb_ref)
    for src, dst, first, count, low, high in ((pad, mid, 1, 10, 7, 73), (mid, flow_out, 2, 8, 8, 72)):
        for i in range(first, first + count):
            now = [src[c, i, low:high, :] for c in range(3)]
            after_x = [src[c, i + 1, low:high, :] for c in range(3)]
            before_x = [src[c, i - 1, low:high, :] for c in range(3)]
            after_y = [src[c, i, low + 1 : high + 1, :] for c in range(3)]
            before_y = [src[c, i, low - 1 : high - 1, :] for c in range(3)]
            new = substep(now, after_x, before_x, after_y, before_y)
            for c in range(3):
                if dst is mid:
                    mid[c, i, low:high, :] = new[c]
                else:
                    flow_out[c, i - 2] = new[c]
    x = cells_to_patches(velocity_blocks(flow_out), row_ref[...], lane_ref[...], feat_ref[...], 3)
    x_out[...] = x
    role_even, tile_even = parity(rank_ref, n_tile)
    halves = (x[:, :512], x[:, 512:])
    edges = [jnp.concatenate([half[:, at : at + 32] for half in halves] * 2, axis=1) for at in (0, 480)]
    for even in (True, False):

        @pl.when(role_even == even)
        def _():
            (xb_out if even else xa_out)[...] = halves[0]
            (xa_out if even else xb_out)[...] = halves[1]

        @pl.when(tile_even == even)
        def _():
            (yb_out if even else ya_out)[...] = edges[0]
            (ya_out if even else yb_out)[...] = edges[1]


def model_kernel(rows, masks, n_tile, in_order, rank_ref, p_ref, own_ref, other_ref, flow_ref, x_ref, xa_ref, xb_ref, ya_ref, yb_ref, row_ref, lane_ref,
                 feat_ref, p_hbm, v_hbm, force_hbm, p_new, w0, w1, w2, wo, x_all, cells, side, edge, pad, v_new, force_new, sems):
    if in_order:
        half = own_ref.shape[0]

        def place(i, carry):
            here = pl.ds(pl.multiple_of(block_of(i, rank_ref[0], masks, n_tile, False) * rows, 8), rows)
            p_new[here, :] = p_ref[here, :] - own_ref[i].astype(F32)
            here = pl.ds(pl.multiple_of(block_of(i + half, rank_ref[0], masks, n_tile, True) * rows, 8), rows)
            p_new[here, :] = p_ref[here, :] - other_ref[i].astype(F32)
            return carry

        lax.fori_loop(0, half, place, 0)
    else:
        p_new[...] = p_ref[...] - own_ref[...].astype(F32)
    copies = [pltpu.make_async_copy(p_new, p_hbm, sems.at[0])]
    copies[0].start()
    load_weights(p_new, w0, w1, w2, wo)
    role_even, tile_even = parity(rank_ref, n_tile)
    x_all[:, 0:1024] = x_ref[...]
    low = lax.broadcasted_iota(jnp.int32, (FEAT, 128), 1) < 64
    for even in (True, False):

        @pl.when(role_even == even)
        def _():
            x_all[:, 1024:1536] = (xb_ref if even else xa_ref)[...]
            x_all[:, 1536:2048] = (xa_ref if even else xb_ref)[...]

        @pl.when(tile_even == even)
        def _():
            before, after = (yb_ref, ya_ref) if even else (ya_ref, yb_ref)
            x_all[:, 2048:2176] = jnp.where(low, before[...].astype(F32), after[...].astype(F32)).astype(BF16)

    hidden = x_all[...]
    for w in (w0, w1, w2):
        z = dot_tn(w[...], hidden)
        hidden = (z * (0.5 * jnp.tanh(0.5 * z) + 0.5)).astype(BF16)
    modelled = regroup_features(feat_ref[...], dot_tn(wo[...], hidden).astype(BF16))
    groups = []
    for k in range(6):
        groups += [modelled[k * 64 : k * 64 + 64, q * 128 : q * 128 + 128] for q in range(8)]
    for first in (8, 12):
        for k in (0, 3, 4):
            groups += [modelled[k * 64 : k * 64 + 64, q * 128 : q * 128 + 128] for q in range(first, first + 4)]
    groups += [modelled[k * 64 : k * 64 + 64, 2048:2176] for k in (3, 1, 5)]
    spread = spread_rows(jnp.concatenate(groups, axis=0), lane_ref[...])
    blocks = rows_to_blocks(spread[: 18 * 64], row_ref[...])
    for k in range(6):
        for px in range(2):
            cells[k, px * 4 : px * 4 + 4] = blocks[k * 2 + px].reshape(4, CY, CZ)
    for i in range(3):
        side[0, i] = blocks[12 + i][3 * CY :]
        side[1, i] = blocks[15 + i][:CY]
    for slot in range(4):
        edge[slot] = spread[18 * 64 :, slot * 128 : slot * 128 + 128].astype(F32)
    for i, k in enumerate((3, 1, 5)):
        pad[i, :, 8:72, :] = cells[k]
        for px in range(2):
            pad[i, px * 4 : px * 4 + 4, 7, :] = edge[px, pl.ds(i * 16 + 3, 4, stride=4), :]
            pad[i, px * 4 : px * 4 + 4, 72, :] = edge[2 + px, pl.ds(i * 16, 4, stride=4), :]
    for i in range(3):
        kx, kz = COMPONENT[i][0], COMPONENT[i][2]
        for x in range(CX):
            after = cells[kx, x + 1] if x < CX - 1 else side[1, i]
            before = cells[kx, x - 1] if x else side[0, i]
            total = 0.5 * (after - before)
            total = total + 0.5 * (pad[i, x, 9:73, :] - pad[i, x, 7:71, :])
            centre = cells[kz, x]
            total = total + 0.5 * (roll_z(centre, CZ - 1) - roll_z(centre, 1))
            force = -SGS_SCALE * total
            force_new[i, x] = force
            v_new[i, x] = flow_ref[i, x] + force
        for n, (src, dst) in enumerate(((v_new, v_hbm), (force_new, force_hbm))):
            copies.append(pltpu.make_async_copy(src.at[i], dst.at[i], sems.at[1 + 2 * i + n]))
            copies[-1].start()
    for copy in copies:
        copy.wait()


def call(kernel, outs, args, scratch, scalars=0, flops=0, name=None, sems=0, hbm_in=False, hbm_out=False):
    space = {True: pltpu.HBM, False: pltpu.VMEM}
    size = sum(a.size * a.dtype.itemsize for a in args) + sum(int(np.prod(s)) * np.dtype(t).itemsize for s, t in outs)
    args = list(args)
    args[scalars:] = [pltpu.with_memory_space_constraint(a, space[hbm_in]) for a in args[scalars:]]
    return pl.pallas_call(
        kernel,
        out_shape=[space[hbm_out](s, t) for s, t in outs],
        in_specs=[pl.BlockSpec(memory_space=pltpu.SMEM)] * scalars
        + [pl.BlockSpec(memory_space=space[hbm_in])] * (len(args) - scalars),
        out_specs=[pl.BlockSpec(memory_space=space[hbm_out])] * len(outs),
        scratch_shapes=[pltpu.VMEM(s, t) for s, t in scratch] + ([pltpu.SemaphoreType.DMA((sems,))] if sems else []),
        compiler_params=pltpu.CompilerParams(vmem_limit_bytes=VMEM_LIMIT),
        cost_estimate=pl.CostEstimate(flops=flops, transcendentals=0, bytes_accessed=size),
        name=name,
    )(*args)


WEIGHTS = [((FEAT, HID), BF16), ((HID, HID), BF16), ((HID, HID), BF16), ((HID, TGT), BF16)]
PADDED = ((3, 12, 80, 128), F32)
ACT = ((HID, NPATCH), BF16)
DER = ((HID, NPATCH), F32)


def bits(size):
    return [1 << i for i in range(size.bit_length() - 1)]


def stage_masks(n_role, n_tile):
    role = [n_tile * b for b in bits(n_role)]
    tile = bits(n_tile)
    rest = tile[:1] + role[1:] + tile[1:]
    other = rest[1::-1] + rest[2:]
    return role[:1] + rest, role[:1] + other


def swaps(axis):
    size = lax.axis_size(axis)
    first = [(i, i ^ 1) for i in range(size)]
    return first, [(i, (i + 1) % size if i % 2 else (i - 1) % size) for i in range(size)]


def local(velocity, params, first_moment, second_moment, patch_index, patch_count):
    n_role, n_tile = lax.axis_size("role"), lax.axis_size("tile")
    devices = n_role * n_tile
    own_rank = lax.axis_index(BOTH)
    rows = ROWS // devices
    in_order = rows % 8 == 0
    masks = stage_masks(n_role, n_tile)
    steps = len(masks[0])
    core_of = [(d // n_tile) & 1 for d in range(devices)]

    def exchange(x, step):
        pairs = [(d, d ^ masks[core_of[d]][step]) for d in range(devices)]
        return lax.ppermute(x, BOTH, pairs)

    def offsets(core):
        return [
            functools.reduce(lambda a, b: a ^ b, [masks[core][i] if (j >> (steps - 1 - i)) & 1 else 0 for i in range(steps)])
            for j in range(devices)
        ]

    half = devices // 2
    rank = own_rank.astype(jnp.int32).reshape(1)
    role_even = (own_rank // n_tile) % 2 == 0
    role_swaps, tile_swaps = swaps("role"), swaps("tile")
    p2 = params.reshape(ROWS, 128)
    selected = patch_index.shape[0]
    row_scale = 1.0 / (selected // 4)

    first, last = velocity[:, :2], velocity[:, CX - 2 :]
    xb = lax.ppermute(jnp.where(role_even, first, last), "role", role_swaps[1])
    xa = lax.ppermute(jnp.where(role_even, last, first), "role", role_swaps[0])
    v_in, p_in, row_mat, lane_mat, feat_mat, x, a1, d1, *weights = call(
        forward_first_kernel,
        [((3, CX, CY, CZ), F32), ((ROWS, 128), F32), ((256, 256), BF16), ((512, 512), BF16), ((128, 128), BF16)]
        + [((FEAT, NPATCH), BF16), ACT, DER]
        + WEIGHTS,
        [velocity, p2] + [jnp.asarray(m, BF16) for m in (row_matrix(), lane_matrix(), feature_matrix())],
        [],
        flops=2 * FEAT * HID * NPATCH,
        name="forward_first",
        sems=5,
        hbm_in=True,
    )
    mats = [row_mat, lane_mat, feat_mat]
    xa, xb, v_in, a1 = lax.optimization_barrier((xa, xb, v_in, a1))
    strip = ((3, CX + 4, 2, CZ), F32)
    ya, yb = call(functools.partial(strips_kernel, n_tile), [strip] * 2, [rank, v_in, xa, xb], [], scalars=1, name="strips")
    yb = lax.ppermute(yb, "tile", tile_swaps[1])
    ya = lax.ppermute(ya, "tile", tile_swaps[0])
    a2, d2, a3, d3, pred = call(
        forward_rest_kernel,
        [ACT, DER, ACT, DER, ((TGT, NPATCH), F32)],
        [a1] + weights[1:],
        [],
        flops=2 * (819200 - FEAT * HID) * NPATCH,
        name="forward_rest",
    )
    halos = [xa, xb, ya, yb]

    grad_outs = [((half, rows, 128), BF16), ((half, rows, 128), F32)] if in_order else [((ROWS, 128), F32)]
    grads = call(
        functools.partial(backward_kernel, row_scale, rows, masks, n_tile, in_order),
        grad_outs,
        [rank, patch_count, patch_index.reshape(1, selected), v_in]
        + halos
        + mats
        + weights[1:]
        + [x, a1, a2, a3, d1, d2, d3, pred],
        [PADDED] + ([((ROWS, 128), F32)] if in_order else []),
        scalars=2,
        flops=4 * 819200 * NPATCH,
        name="backward",
    )
    if in_order:
        send, keep = grads
    else:
        here = jnp.arange(devices, dtype=jnp.int32)
        order = jnp.where(
            here < half,
            block_of(here, own_rank, masks, n_tile, False),
            block_of(here, own_rank, masks, n_tile, True),
        )
        placed = grads[0].reshape(devices, rows, 128)[order]
        send, keep = placed[half:].astype(BF16), placed[:half]

    size = half
    got = exchange(send, 0)
    for step in range(1, steps):
        size //= 2
        send = (keep[size:] + got[size:].astype(F32)).astype(BF16)
        keep = keep[:size] + got[:size].astype(F32)
        if step == 1:
            send, still = lax.optimization_barrier((send, v_in))
        got = exchange(send, step)
        if step == 1:
            flow, x_new, fxa, fxb, fya, fyb = call(
                functools.partial(flow_kernel, n_tile),
                [((3, CX, CY, CZ), F32), ((FEAT, NPATCH), BF16)]
                + [((FEAT, NPATCH // 2), BF16)] * 2
                + [((FEAT, 128), BF16)] * 2,
                [rank, still] + halos + mats,
                [PADDED, PADDED],
                scalars=1,
                flops=1 << 30,
                name="flow",
            )
            fxa = lax.ppermute(fxa, "role", role_swaps[0])
            fxb = lax.ppermute(fxb, "role", role_swaps[1])
            got, flow, x_new, fya, fyb = lax.optimization_barrier((got, flow, x_new, fya, fyb))
        if step == 2:
            fya = lax.ppermute(fya, "tile", tile_swaps[0])
        if step == 3:
            fyb = lax.ppermute(fyb, "tile", tile_swaps[1])
    grad = (keep + got.astype(F32)).reshape(-1)
    first_out = BETA_ONE * first_moment + (1.0 - BETA_ONE) * grad
    second_out = BETA_TWO * second_moment + (1.0 - BETA_TWO) * grad * grad
    fix_first = 1.0 - BETA_ONE**ADAM_STEP
    fix_second = 1.0 - BETA_TWO**ADAM_STEP
    update = LEARN_RATE * (first_out / fix_first) / (jnp.sqrt(second_out / fix_second) + EPSILON)
    held = update.astype(BF16).reshape(1, rows, 128)
    for step in range(steps - 1, 0, -1):
        held = jnp.concatenate([held, exchange(held, step)], axis=0)
    other = exchange(held, 0)
    if not in_order:
        slots = jnp.zeros((devices,), jnp.int32).at[order].set(jnp.arange(devices, dtype=jnp.int32))
        held = other = jnp.concatenate([held, other], axis=0)[slots].reshape(ROWS, 128)

    p_new, velocity_out, sgs_force = call(
        functools.partial(model_kernel, rows, masks, n_tile, in_order),
        [((ROWS, 128), F32)] + [((3, CX, CY, CZ), F32)] * 2,
        [rank, p_in, held, other, flow, x_new, fxa, fxb, fya, fyb] + mats,
        [((ROWS, 128), F32)]
        + WEIGHTS
        + [((FEAT, 17 * 128), BF16), ((6, CX, CY, CZ), F32), ((2, 3, CY, CZ), F32), ((4, 48, 128), F32), ((3, CX, 80, CZ), F32)]
        + [((3, CX, CY, CZ), F32)] * 2,
        scalars=1,
        flops=4 * 819200 * NPATCH,
        name="model",
        sems=7,
        hbm_out=True,
    )
    return (velocity_out, sgs_force, p_new.reshape(-1), first_out, second_out)


def solution(mesh):
    placed = (
        P(None, "role", "tile", None),
        P(),
        P(BOTH),
        P(BOTH),
        P(BOTH),
        P(BOTH),
    )
    return jax.shard_map(
        local,
        mesh=mesh,
        in_specs=placed,
        out_specs=(
            P(None, "role", "tile", None),
            P(None, "role", "tile", None),
            P(),
            P(BOTH),
            P(BOTH),
        ),
        check_vma=False,
    )
```

```python
import functools

import jax
import jax.numpy as jnp
import numpy as np
from jax import lax
from jax.experimental import pallas as pl
from jax.experimental.pallas import tpu as pltpu
from jax.sharding import PartitionSpec as P

FEAT = 192
TGT = 384
HID = 512
ADAM_STEP = 100
STEP_DT = 0.1
VISCOSITY = 0.1
SGS_SCALE = 1.5
BETA_ONE = 0.9
BETA_TWO = 0.999
LEARN_RATE = 0.001
EPSILON = 1e-08
PAIRS = ((0, 0), (1, 1), (2, 2), (0, 1), (0, 2), (1, 2))
COMPONENT = ((0, 3, 4), (3, 1, 5), (4, 5, 2))

CX, CY, CZ = 8, 64, 128
NPATCH = 1024
ROWS = 6400
W1_AT = 768
W2_AT = W1_AT + 2048
WO_AT = W2_AT + 2048
BOTH = ("role", "tile")
F32, BF16 = jnp.float32, jnp.bfloat16
VMEM_LIMIT = 24 * 1024 * 1024


def row_matrix():
    matrix = np.zeros((256, 256), np.float32)
    for dx in range(4):
        for j in range(4):
            for pyl in range(4):
                for dy in range(4):
                    matrix[pyl * 64 + j * 16 + dx * 4 + dy, dx * 64 + j * 16 + pyl * 4 + dy] = 1
    return matrix


def lane_matrix():
    matrix = np.zeros((512, 512), np.float32)
    for pyl in range(4):
        for pz in range(32):
            for dz in range(4):
                matrix[pyl * 128 + pz * 4 + dz, dz * 128 + pyl * 32 + pz] = 1
    return matrix


def feature_matrix():
    matrix = np.zeros((128, 128), np.float32)
    for c in range(2):
        for off in range(16):
            for dz in range(4):
                matrix[c * 64 + off * 4 + dz, c * 64 + dz * 16 + off] = 1
    return matrix


def dot(a, b):
    return jnp.dot(a, b, preferred_element_type=F32)


def dot_tn(a, b):
    return lax.dot_general(a, b, (((0,), (0,)), ((), ())), preferred_element_type=F32)


def dot_nt(a, b):
    return lax.dot_general(a, b, (((1,), (1,)), ((), ())), preferred_element_type=F32)


def permute_features(feature_mat, x, channels):
    pieces = []
    at = 0
    while at < channels * 64:
        size = min(128, channels * 64 - at)
        pieces.append(dot(feature_mat[:size, :size], x[at : at + size]).astype(BF16))
        at += size
    return jnp.concatenate(pieces, axis=0)


def cells_to_patches(blocks, row_mat, lane_mat, feature_mat, channels):
    moved = dot(row_mat, jnp.concatenate(blocks, axis=1)).astype(BF16)
    rows = []
    for i in range(2 * channels):
        part = moved[:, i * 128 : (i + 1) * 128]
        rows.append(jnp.concatenate([part[p * 64 : (p + 1) * 64] for p in range(4)], axis=1))
    spread = dot(jnp.concatenate(rows, axis=0), lane_mat).astype(BF16)
    bands = []
    for c in range(channels):
        for dz in range(4):
            bands.append(
                jnp.concatenate(
                    [
                        spread[((c * 2 + px) * 4 + j) * 16 : ((c * 2 + px) * 4 + j) * 16 + 16, dz * 128 : dz * 128 + 128]
                        for px in range(2)
                        for j in range(4)
                    ],
                    axis=1,
                )
            )
    return permute_features(feature_mat, jnp.concatenate(bands, axis=0), channels)


def spread_rows(x, lane_mat):
    rows = [
        jnp.concatenate([x[at + dz * 16 : at + dz * 16 + 16] for dz in range(4)], axis=1) for at in range(0, x.shape[0], 64)
    ]
    return dot_nt(jnp.concatenate(rows, axis=0), lane_mat).astype(BF16)


def regroup_features(feature_mat, x):
    return jnp.concatenate(
        [dot_tn(feature_mat, x[at : at + 128]).astype(BF16) for at in range(0, x.shape[0], 128)], axis=0
    )


def rows_to_blocks(spread, row_mat):
    count = spread.shape[0] // 64
    columns = []
    for i in range(count):
        part = spread[i * 64 : (i + 1) * 64]
        columns.append(jnp.concatenate([part[:, p * 128 : (p + 1) * 128] for p in range(4)], axis=0))
    moved = dot_tn(row_mat, jnp.concatenate(columns, axis=1))
    return [moved[:, i * 128 : (i + 1) * 128] for i in range(count)]


def load_weights(p_ref, w0, w1, w2, wo):
    for k in range(4):
        lanes = slice(k * 128, (k + 1) * 128)
        w0[:, lanes] = p_ref[pl.ds(k, FEAT, stride=4), :].astype(BF16)
        w1[:, lanes] = p_ref[pl.ds(W1_AT + k, HID, stride=4), :].astype(BF16)
        w2[:, lanes] = p_ref[pl.ds(W2_AT + k, HID, stride=4), :].astype(BF16)
    for k in range(3):
        wo[:, k * 128 : (k + 1) * 128] = p_ref[pl.ds(WO_AT + k, HID, stride=3), :].astype(BF16)


def velocity_blocks(v_ref):
    return [
        v_ref[c, px * 4 : px * 4 + 4].reshape(256, 128).astype(BF16) for c in range(3) for px in range(2)
    ]


def layer(w, hidden, a_out, d_out):
    z = dot_tn(w[...], hidden)
    s = 0.5 * jnp.tanh(0.5 * z) + 0.5
    a = z * s
    d_out[...] = s + a * (1.0 - s)
    hidden = a.astype(BF16)
    a_out[...] = hidden
    return hidden


def forward_first_kernel(
    v_hbm, p_hbm, row_hbm, lane_hbm, feat_hbm, v_out, p_out, row_out, lane_out, feat_out, x_out, a_out, d_out, w0, w1, w2, wo, sems
):
    copies = [
        pltpu.make_async_copy(src, dst, sems.at[i])
        for i, (src, dst) in enumerate(
            ((v_hbm, v_out), (row_hbm, row_out), (lane_hbm, lane_out), (feat_hbm, feat_out), (p_hbm, p_out))
        )
    ]
    for copy in copies:
        copy.start()
    for copy in copies[:-1]:
        copy.wait()
    x = cells_to_patches(velocity_blocks(v_out), row_out[...], lane_out[...], feat_out[...], 3)
    x_out[...] = x
    copies[-1].wait()
    load_weights(p_out, w0, w1, w2, wo)
    layer(w0, x, a_out, d_out)


def parity(rank_ref, n_tile):
    rank = rank_ref[0]
    return (rank // n_tile) % 2 == 0, rank % 2 == 0


def strips_kernel(n_tile, rank_ref, v_ref, xa_ref, xb_ref, ya_out, yb_out):
    role_even, tile_even = parity(rank_ref, n_tile)

    def fill(first_out, last_out, low_ref, high_ref):
        for out, at in ((first_out, 0), (last_out, CY - 2)):
            out[:, 2:10] = v_ref[:, :, at : at + 2, :]
            out[:, 0:2] = low_ref[:, :, at : at + 2, :]
            out[:, 10:12] = high_ref[:, :, at : at + 2, :]

    for even_r in (True, False):
        for even_t in (True, False):

            @pl.when((role_even == even_r) & (tile_even == even_t))
            def _():
                first_out, last_out = (yb_out, ya_out) if even_t else (ya_out, yb_out)
                low_ref, high_ref = (xb_ref, xa_ref) if even_r else (xa_ref, xb_ref)
                fill(first_out, last_out, low_ref, high_ref)


def forward_rest_kernel(a1_ref, w1, w2, wo, a2_out, d2_out, a3_out, d3_out, pred_out):
    hidden = layer(w1, a1_ref[...], a2_out, d2_out)
    hidden = layer(w2, hidden, a3_out, d3_out)
    pred_out[...] = dot_tn(wo[...], hidden)


def fill_padded(pad, rank_ref, n_tile, v_ref, xa_ref, xb_ref, ya_ref, yb_ref):
    role_even, tile_even = parity(rank_ref, n_tile)
    pad[:, 2:10, 8:72, :] = v_ref[...]
    for even in (True, False):

        @pl.when(role_even == even)
        def _():
            pad[:, 0:2, 8:72, :] = (xb_ref if even else xa_ref)[...]
            pad[:, 10:12, 8:72, :] = (xa_ref if even else xb_ref)[...]

        @pl.when(tile_even == even)
        def _():
            pad[:, :, 6:8, :] = (yb_ref if even else ya_ref)[...]
            pad[:, :, 72:74, :] = (ya_ref if even else yb_ref)[...]


def block_of(position, rank, masks, n_tile, send):
    core = (rank // n_tile) % 2
    if send:
        core = 1 - core
    steps = len(masks[0])
    out = rank
    for i in range(steps):
        mask = jnp.where(core == 0, masks[0][i], masks[1][i])
        out = out ^ (((position >> (steps - 1 - i)) & 1) * mask)
    return out


def box(field_sum):
    along = field_sum[:, 0:64] + field_sum[:, 1:65] + field_sum[:, 2:66]
    return (along + roll_z(along, 1) + roll_z(along, CZ - 1)) * (1.0 / 27.0)


def roll_z(x, by):
    return pltpu.roll(x, by, x.ndim - 1)


def stress_blocks(pad):
    out = [None] * 12
    for px in range(2):
        first = 1 + px * 4
        planes = [[pad[c, first + i, 7:73, :] for i in range(6)] for c in range(3)]
        smooth = []
        for c in range(3):
            sums = jnp.stack([planes[c][i] + planes[c][i + 1] + planes[c][i + 2] for i in range(4)])
            smooth.append(box(sums))
        for k, (a, b) in enumerate(PAIRS):
            prod = [planes[a][i] * planes[b][i] for i in range(6)]
            sums = jnp.stack([prod[i] + prod[i + 1] + prod[i + 2] for i in range(4)])
            value = box(sums) - smooth[a] * smooth[b]
            out[k * 2 + px] = value.astype(BF16).reshape(256, 128)
    return out


def multiplicity(index_ref, count_ref):
    index = index_ref[...]
    selected = index.shape[1]
    live = lax.broadcasted_iota(jnp.int32, (16, selected), 1) < count_ref[0]
    high = lax.broadcasted_iota(jnp.int32, (16, selected), 0) == (index >> 7)
    left = jnp.where(high & live, 1.0, 0.0).astype(BF16)
    low = lax.broadcasted_iota(jnp.int32, (128, selected), 0) == (index & 127)
    right = jnp.where(low, 1.0, 0.0).astype(BF16)
    return dot_nt(left, right)


def backward_kernel(row_scale, rows, masks, n_tile, in_order, rank_ref, count_ref, index_ref, v_ref, xa_ref, xb_ref, ya_ref, yb_ref, row_ref, lane_ref,
                    feat_ref, w1, w2, wo, x_ref, a1_ref, a2_ref, a3_ref, d1_ref, d2_ref, d3_ref, pred_ref, *rest):
    if in_order:
        send_out, keep_out, pad, grads = rest
    else:
        grads, pad = rest
    weight = multiplicity(index_ref, count_ref) * row_scale
    weight = jnp.concatenate([weight[q : q + 1] for q in range(8)], axis=1)
    fill_padded(pad, rank_ref, n_tile, v_ref, xa_ref, xb_ref, ya_ref, yb_ref)
    target = cells_to_patches(stress_blocks(pad), row_ref[...], lane_ref[...], feat_ref[...], 6)
    error = ((pred_ref[...] - target.astype(F32)) * weight).astype(BF16)
    grad = dot_nt(a3_ref[...], error)
    for k in range(3):
        grads[pl.ds(WO_AT + k, HID, stride=3), :] = grad[:, k * 128 : (k + 1) * 128]
    up = dot(wo[...], error)
    for d_ref, left_ref, at, w in ((d3_ref, a2_ref, W2_AT, w2), (d2_ref, a1_ref, W1_AT, w1), (d1_ref, x_ref, 0, None)):
        slope = (up * d_ref[...]).astype(BF16)
        grad = dot_nt(left_ref[...], slope)
        size = left_ref.shape[0]
        for k in range(4):
            grads[pl.ds(at + k, size, stride=4), :] = grad[:, k * 128 : (k + 1) * 128]
        if w is not None:
            up = dot(w[...], slope)
    if in_order:
        half = keep_out.shape[0]

        def place(i, carry):
            here = pl.multiple_of(block_of(i + half, rank_ref[0], masks, n_tile, True) * rows, 8)
            send_out[i] = grads[pl.ds(here, rows), :].astype(BF16)
            here = pl.multiple_of(block_of(i, rank_ref[0], masks, n_tile, False) * rows, 8)
            keep_out[i] = grads[pl.ds(here, rows), :]
            return carry

        lax.fori_loop(0, half, place, 0)


def substep(now, after_x, before_x, after_y, before_y):
    after_z = [roll_z(f, CZ - 1) for f in now]
    before_z = [roll_z(f, 1) for f in now]
    out = []
    for c in range(3):
        transport = now[0] * (0.5 * (after_x[c] - before_x[c]))
        transport = transport + now[1] * (0.5 * (after_y[c] - before_y[c]))
        transport = transport + now[2] * (0.5 * (after_z[c] - before_z[c]))
        laplace = after_x[c] + before_x[c] + after_y[c] + before_y[c] + after_z[c] + before_z[c] - 6.0 * now[c]
        out.append(now[c] + STEP_DT * (VISCOSITY * laplace - transport))
    return out


def flow_kernel(n_tile, rank_ref, v_ref, xa_ref, xb_ref, ya_ref, yb_ref, row_ref, lane_ref, feat_ref, flow_out, x_out, xa_out, xb_out, ya_out, yb_out, pad, mid):
    fill_padded(pad, rank_ref, n_tile, v_ref, xa_ref, xb_ref, ya_ref, yb_ref)
    for src, dst, first, count, low, high in ((pad, mid, 1, 10, 7, 73), (mid, flow_out, 2, 8, 8, 72)):
        for i in range(first, first + count):
            now = [src[c, i, low:high, :] for c in range(3)]
            after_x = [src[c, i + 1, low:high, :] for c in range(3)]
            before_x = [src[c, i - 1, low:high, :] for c in range(3)]
            after_y = [src[c, i, low + 1 : high + 1, :] for c in range(3)]
            before_y = [src[c, i, low - 1 : high - 1, :] for c in range(3)]
            new = substep(now, after_x, before_x, after_y, before_y)
            for c in range(3):
                if dst is mid:
                    mid[c, i, low:high, :] = new[c]
                else:
                    flow_out[c, i - 2] = new[c]
    x = cells_to_patches(velocity_blocks(flow_out), row_ref[...], lane_ref[...], feat_ref[...], 3)
    x_out[...] = x
    role_even, tile_even = parity(rank_ref, n_tile)
    halves = (x[:, :512], x[:, 512:])
    edges = [jnp.concatenate([half[:, at : at + 32] for half in halves] * 2, axis=1) for at in (0, 480)]
    for even in (True, False):

        @pl.when(role_even == even)
        def _():
            (xb_out if even else xa_out)[...] = halves[0]
            (xa_out if even else xb_out)[...] = halves[1]

        @pl.when(tile_even == even)
        def _():
            (yb_out if even else ya_out)[...] = edges[0]
            (ya_out if even else yb_out)[...] = edges[1]


def model_kernel(rows, masks, n_tile, in_order, rank_ref, p_ref, own_ref, other_ref, flow_ref, x_ref, xa_ref, xb_ref, ya_ref, yb_ref, row_ref, lane_ref,
                 feat_ref, p_hbm, v_hbm, force_hbm, p_new, w0, w1, w2, wo, x_all, cells, side, edge, pad, v_new, force_new, sems):
    if in_order:
        half = own_ref.shape[0]

        def place(i, carry):
            here = pl.ds(pl.multiple_of(block_of(i, rank_ref[0], masks, n_tile, False) * rows, 8), rows)
            p_new[here, :] = p_ref[here, :] - own_ref[i].astype(F32)
            here = pl.ds(pl.multiple_of(block_of(i + half, rank_ref[0], masks, n_tile, True) * rows, 8), rows)
            p_new[here, :] = p_ref[here, :] - other_ref[i].astype(F32)
            return carry

        lax.fori_loop(0, half, place, 0)
    else:
        p_new[...] = p_ref[...] - own_ref[...].astype(F32)
    copies = [pltpu.make_async_copy(p_new, p_hbm, sems.at[0])]
    copies[0].start()
    load_weights(p_new, w0, w1, w2, wo)
    role_even, tile_even = parity(rank_ref, n_tile)
    x_all[:, 0:1024] = x_ref[...]
    low = lax.broadcasted_iota(jnp.int32, (FEAT, 128), 1) < 64
    for even in (True, False):

        @pl.when(role_even == even)
        def _():
            x_all[:, 1024:1536] = (xb_ref if even else xa_ref)[...]
            x_all[:, 1536:2048] = (xa_ref if even else xb_ref)[...]

        @pl.when(tile_even == even)
        def _():
            before, after = (yb_ref, ya_ref) if even else (ya_ref, yb_ref)
            x_all[:, 2048:2176] = jnp.where(low, before[...].astype(F32), after[...].astype(F32)).astype(BF16)

    hidden = x_all[...]
    for w in (w0, w1, w2):
        z = dot_tn(w[...], hidden)
        hidden = (z * (0.5 * jnp.tanh(0.5 * z) + 0.5)).astype(BF16)
    modelled = regroup_features(feat_ref[...], dot_tn(wo[...], hidden).astype(BF16))
    groups = []
    for k in range(6):
        groups += [modelled[k * 64 : k * 64 + 64, q * 128 : q * 128 + 128] for q in range(8)]
    for first in (8, 12):
        for k in (0, 3, 4):
            groups += [modelled[k * 64 : k * 64 + 64, q * 128 : q * 128 + 128] for q in range(first, first + 4)]
    groups += [modelled[k * 64 : k * 64 + 64, 2048:2176] for k in (3, 1, 5)]
    spread = spread_rows(jnp.concatenate(groups, axis=0), lane_ref[...])
    blocks = rows_to_blocks(spread[: 18 * 64], row_ref[...])
    for k in range(6):
        for px in range(2):
            cells[k, px * 4 : px * 4 + 4] = blocks[k * 2 + px].reshape(4, CY, CZ)
    for i in range(3):
        side[0, i] = blocks[12 + i][3 * CY :]
        side[1, i] = blocks[15 + i][:CY]
    for slot in range(4):
        edge[slot] = spread[18 * 64 :, slot * 128 : slot * 128 + 128].astype(F32)
    for i, k in enumerate((3, 1, 5)):
        pad[i, :, 8:72, :] = cells[k]
        for px in range(2):
            pad[i, px * 4 : px * 4 + 4, 7, :] = edge[px, pl.ds(i * 16 + 3, 4, stride=4), :]
            pad[i, px * 4 : px * 4 + 4, 72, :] = edge[2 + px, pl.ds(i * 16, 4, stride=4), :]
    for i in range(3):
        kx, kz = COMPONENT[i][0], COMPONENT[i][2]
        for x in range(CX):
            after = cells[kx, x + 1] if x < CX - 1 else side[1, i]
            before = cells[kx, x - 1] if x else side[0, i]
            total = 0.5 * (after - before)
            total = total + 0.5 * (pad[i, x, 9:73, :] - pad[i, x, 7:71, :])
            centre = cells[kz, x]
            total = total + 0.5 * (roll_z(centre, CZ - 1) - roll_z(centre, 1))
            force = -SGS_SCALE * total
            force_new[i, x] = force
            v_new[i, x] = flow_ref[i, x] + force
        for n, (src, dst) in enumerate(((v_new, v_hbm), (force_new, force_hbm))):
            copies.append(pltpu.make_async_copy(src.at[i], dst.at[i], sems.at[1 + 2 * i + n]))
            copies[-1].start()
    for copy in copies:
        copy.wait()


def call(kernel, outs, args, scratch, scalars=0, flops=0, name=None, sems=0, hbm_in=False, hbm_out=False):
    space = {True: pltpu.HBM, False: pltpu.VMEM}
    size = sum(a.size * a.dtype.itemsize for a in args) + sum(int(np.prod(s)) * np.dtype(t).itemsize for s, t in outs)
    args = list(args)
    args[scalars:] = [pltpu.with_memory_space_constraint(a, space[hbm_in]) for a in args[scalars:]]
    return pl.pallas_call(
        kernel,
        out_shape=[space[hbm_out](s, t) for s, t in outs],
        in_specs=[pl.BlockSpec(memory_space=pltpu.SMEM)] * scalars
        + [pl.BlockSpec(memory_space=space[hbm_in])] * (len(args) - scalars),
        out_specs=[pl.BlockSpec(memory_space=space[hbm_out])] * len(outs),
        scratch_shapes=[pltpu.VMEM(s, t) for s, t in scratch] + ([pltpu.SemaphoreType.DMA((sems,))] if sems else []),
        compiler_params=pltpu.CompilerParams(vmem_limit_bytes=VMEM_LIMIT),
        cost_estimate=pl.CostEstimate(flops=flops, transcendentals=0, bytes_accessed=size),
        name=name,
    )(*args)


WEIGHTS = [((FEAT, HID), BF16), ((HID, HID), BF16), ((HID, HID), BF16), ((HID, TGT), BF16)]
PADDED = ((3, 12, 80, 128), F32)
ACT = ((HID, NPATCH), BF16)
DER = ((HID, NPATCH), F32)


def bits(size):
    return [1 << i for i in range(size.bit_length() - 1)]


def stage_masks(n_role, n_tile):
    role = [n_tile * b for b in bits(n_role)]
    tile = bits(n_tile)
    rest = tile[:1] + role[1:] + tile[1:]
    other = rest[1::-1] + rest[2:]
    return role[:1] + rest, role[:1] + other


def swaps(axis):
    size = lax.axis_size(axis)
    first = [(i, i ^ 1) for i in range(size)]
    return first, [(i, (i + 1) % size if i % 2 else (i - 1) % size) for i in range(size)]


def local(velocity, params, first_moment, second_moment, patch_index, patch_count):
    n_role, n_tile = lax.axis_size("role"), lax.axis_size("tile")
    devices = n_role * n_tile
    own_rank = lax.axis_index(BOTH)
    rows = ROWS // devices
    in_order = rows % 8 == 0
    masks = stage_masks(n_role, n_tile)
    steps = len(masks[0])
    core_of = [(d // n_tile) & 1 for d in range(devices)]

    def exchange(x, step):
        pairs = [(d, d ^ masks[core_of[d]][step]) for d in range(devices)]
        return lax.ppermute(x, BOTH, pairs)

    def offsets(core):
        return [
            functools.reduce(lambda a, b: a ^ b, [masks[core][i] if (j >> (steps - 1 - i)) & 1 else 0 for i in range(steps)])
            for j in range(devices)
        ]

    half = devices // 2
    rank = own_rank.astype(jnp.int32).reshape(1)
    role_even = (own_rank // n_tile) % 2 == 0
    role_swaps, tile_swaps = swaps("role"), swaps("tile")
    p2 = params.reshape(ROWS, 128)
    selected = patch_index.shape[0]
    row_scale = 1.0 / (selected // 4)

    first, last = velocity[:, :2], velocity[:, CX - 2 :]
    xb = lax.ppermute(jnp.where(role_even, first, last), "role", role_swaps[1])
    xa = lax.ppermute(jnp.where(role_even, last, first), "role", role_swaps[0])
    v_in, p_in, row_mat, lane_mat, feat_mat, x, a1, d1, *weights = call(
        forward_first_kernel,
        [((3, CX, CY, CZ), F32), ((ROWS, 128), F32), ((256, 256), BF16), ((512, 512), BF16), ((128, 128), BF16)]
        + [((FEAT, NPATCH), BF16), ACT, DER]
        + WEIGHTS,
        [velocity, p2] + [jnp.asarray(m, BF16) for m in (row_matrix(), lane_matrix(), feature_matrix())],
        [],
        flops=2 * FEAT * HID * NPATCH,
        name="forward_first",
        sems=5,
        hbm_in=True,
    )
    mats = [row_mat, lane_mat, feat_mat]
    xa, xb, v_in, a1 = lax.optimization_barrier((xa, xb, v_in, a1))
    strip = ((3, CX + 4, 2, CZ), F32)
    ya, yb = call(functools.partial(strips_kernel, n_tile), [strip] * 2, [rank, v_in, xa, xb], [], scalars=1, name="strips")
    yb = lax.ppermute(yb, "tile", tile_swaps[1])
    ya = lax.ppermute(ya, "tile", tile_swaps[0])
    a2, d2, a3, d3, pred = call(
        forward_rest_kernel,
        [ACT, DER, ACT, DER, ((TGT, NPATCH), F32)],
        [a1] + weights[1:],
        [],
        flops=2 * (819200 - FEAT * HID) * NPATCH,
        name="forward_rest",
    )
    halos = [xa, xb, ya, yb]

    grad_outs = [((half, rows, 128), BF16), ((half, rows, 128), F32)] if in_order else [((ROWS, 128), F32)]
    grads = call(
        functools.partial(backward_kernel, row_scale, rows, masks, n_tile, in_order),
        grad_outs,
        [rank, patch_count, patch_index.reshape(1, selected), v_in]
        + halos
        + mats
        + weights[1:]
        + [x, a1, a2, a3, d1, d2, d3, pred],
        [PADDED] + ([((ROWS, 128), F32)] if in_order else []),
        scalars=2,
        flops=4 * 819200 * NPATCH,
        name="backward",
    )
    if in_order:
        send, keep = grads
    else:
        here = jnp.arange(devices, dtype=jnp.int32)
        order = jnp.where(
            here < half,
            block_of(here, own_rank, masks, n_tile, False),
            block_of(here, own_rank, masks, n_tile, True),
        )
        placed = grads[0].reshape(devices, rows, 128)[order]
        send, keep = placed[half:].astype(BF16), placed[:half]

    size = half
    fence = lax.optimization_barrier
    got = exchange(send, 0)
    for step in range(1, steps):
        size //= 2
        if step < steps - 1:
            send = (keep[size:] + got[size:].astype(F32)).astype(BF16)
            keep = keep[:size] + got[:size].astype(F32)
        else:
            send = keep = (keep + got.astype(F32)).astype(BF16)
        if step == 1:
            send, still, moments = fence((send, v_in, jnp.stack([first_moment, second_moment])))
        if step == 3:
            send, fxb = fence((send, fxb))
        if step == steps - 1:
            send, fxa, fya = fence((send, fxa, fya))
        got = exchange(send, step)
        if step == 1:
            moments_other = exchange(moments, steps - 1)
            flow, x_new, fxa, fxb, fya, fyb = call(
                functools.partial(flow_kernel, n_tile),
                [((3, CX, CY, CZ), F32), ((FEAT, NPATCH), BF16)]
                + [((FEAT, NPATCH // 2), BF16)] * 2
                + [((FEAT, 128), BF16)] * 2,
                [rank, still] + halos + mats,
                [PADDED, PADDED],
                scalars=1,
                flops=1 << 30,
                name="flow",
            )
            got, flow, x_new, fxa, fxb, fya, fyb = fence((got, flow, x_new, fxa, fxb, fya, fyb))
        if step == 2:
            got, moments_other = fence((got, moments_other))
        if step == 3:
            fxb = lax.ppermute(fxb, "role", role_swaps[1])
        if step == steps - 1:
            fxa = lax.ppermute(fxa, "role", role_swaps[0])
            fya = lax.ppermute(fya, "tile", tile_swaps[0])
            got, fxb = fence((got, fxb))
    grad = (keep.astype(F32) + got[::-1].astype(F32)).reshape(2, -1)
    first_two = jnp.stack([first_moment, moments_other[0]])
    second_two = jnp.stack([second_moment, moments_other[1]])
    first_two = BETA_ONE * first_two + (1.0 - BETA_ONE) * grad
    second_two = BETA_TWO * second_two + (1.0 - BETA_TWO) * grad * grad
    first_out, second_out = first_two[0], second_two[0]
    fix_first = 1.0 - BETA_ONE**ADAM_STEP
    fix_second = 1.0 - BETA_TWO**ADAM_STEP
    update = LEARN_RATE * (first_two / fix_first) / (jnp.sqrt(second_two / fix_second) + EPSILON)
    held = update.astype(BF16).reshape(2, rows, 128)
    for step in range(steps - 2, 0, -1):
        if step == 2:
            held, fyb = fence((held, fyb))
        got = exchange(held, step)
        if step == 2:
            fyb = lax.ppermute(fyb, "tile", tile_swaps[1])
        if step == 1:
            got, fyb = fence((got, fyb))
        if step == steps - 2:
            got, fxa, fya = fence((got, fxa, fya))
        held = jnp.concatenate([held, got], axis=0)
    other = exchange(held, 0)
    if not in_order:
        slots = jnp.zeros((devices,), jnp.int32).at[order].set(jnp.arange(devices, dtype=jnp.int32))
        held = other = jnp.concatenate([held, other], axis=0)[slots].reshape(ROWS, 128)

    p_new, velocity_out, sgs_force = call(
        functools.partial(model_kernel, rows, masks, n_tile, in_order),
        [((ROWS, 128), F32)] + [((3, CX, CY, CZ), F32)] * 2,
        [rank, p_in, held, other, flow, x_new, fxa, fxb, fya, fyb] + mats,
        [((ROWS, 128), F32)]
        + WEIGHTS
        + [((FEAT, 17 * 128), BF16), ((6, CX, CY, CZ), F32), ((2, 3, CY, CZ), F32), ((4, 48, 128), F32), ((3, CX, 80, CZ), F32)]
        + [((3, CX, CY, CZ), F32)] * 2,
        scalars=1,
        flops=4 * 819200 * NPATCH,
        name="model",
        sems=7,
        hbm_out=True,
    )
    return (velocity_out, sgs_force, p_new.reshape(-1), first_out, second_out)


def solution(mesh):
    placed = (
        P(None, "role", "tile", None),
        P(),
        P(BOTH),
        P(BOTH),
        P(BOTH),
        P(BOTH),
    )
    return jax.shard_map(
        local,
        mesh=mesh,
        in_specs=placed,
        out_specs=(
            P(None, "role", "tile", None),
            P(None, "role", "tile", None),
            P(),
            P(BOTH),
            P(BOTH),
        ),
        check_vma=False,
    )
```

```python
import functools

import jax
import jax.numpy as jnp
import numpy as np
from jax import lax
from jax.experimental import pallas as pl
from jax.experimental.pallas import tpu as pltpu
from jax.sharding import PartitionSpec as P

FEAT = 192
TGT = 384
HID = 512
ADAM_STEP = 100
STEP_DT = 0.1
VISCOSITY = 0.1
SGS_SCALE = 1.5
BETA_ONE = 0.9
BETA_TWO = 0.999
LEARN_RATE = 0.001
EPSILON = 1e-08
PAIRS = ((0, 0), (1, 1), (2, 2), (0, 1), (0, 2), (1, 2))
COMPONENT = ((0, 3, 4), (3, 1, 5), (4, 5, 2))

CX, CY, CZ = 8, 64, 128
NPATCH = 1024
ROWS = 6400
W1_AT = 768
W2_AT = W1_AT + 2048
WO_AT = W2_AT + 2048
BOTH = ("role", "tile")
F32, BF16 = jnp.float32, jnp.bfloat16
VMEM_LIMIT = 24 * 1024 * 1024


def row_matrix():
    matrix = np.zeros((256, 256), np.float32)
    for dx in range(4):
        for j in range(4):
            for pyl in range(4):
                for dy in range(4):
                    matrix[pyl * 64 + j * 16 + dx * 4 + dy, dx * 64 + j * 16 + pyl * 4 + dy] = 1
    return matrix


def lane_matrix():
    matrix = np.zeros((512, 512), np.float32)
    for pyl in range(4):
        for pz in range(32):
            for dz in range(4):
                matrix[pyl * 128 + pz * 4 + dz, dz * 128 + pyl * 32 + pz] = 1
    return matrix


def feature_matrix():
    matrix = np.zeros((128, 128), np.float32)
    for c in range(2):
        for off in range(16):
            for dz in range(4):
                matrix[c * 64 + off * 4 + dz, c * 64 + dz * 16 + off] = 1
    return matrix


def side_matrix():
    matrix = np.zeros((TGT, 128), np.float32)
    for side, dx in enumerate((3, 0)):
        for dz in range(4):
            for slot, k in enumerate((0, 3, 4)):
                for dy in range(4):
                    matrix[k * 64 + dz * 16 + dx * 4 + dy, side * 64 + dz * 16 + slot * 4 + dy] = 1
    return matrix


def dot(a, b):
    return jnp.dot(a, b, preferred_element_type=F32)


def dot_tn(a, b):
    return lax.dot_general(a, b, (((0,), (0,)), ((), ())), preferred_element_type=F32)


def dot_nt(a, b):
    return lax.dot_general(a, b, (((1,), (1,)), ((), ())), preferred_element_type=F32)


def cells_to_patches(blocks, row_mat, lane_mat, channels):
    moved = dot(row_mat, jnp.concatenate(blocks, axis=1)).astype(BF16)
    rows = []
    for i in range(2 * channels):
        part = moved[:, i * 128 : (i + 1) * 128]
        rows.append(jnp.concatenate([part[p * 64 : (p + 1) * 64] for p in range(4)], axis=1))
    spread = dot(jnp.concatenate(rows, axis=0), lane_mat).astype(BF16)
    bands = []
    for c in range(channels):
        for dz in range(4):
            bands.append(
                jnp.concatenate(
                    [
                        spread[((c * 2 + px) * 4 + j) * 16 : ((c * 2 + px) * 4 + j) * 16 + 16, dz * 128 : dz * 128 + 128]
                        for px in range(2)
                        for j in range(4)
                    ],
                    axis=1,
                )
            )
    return jnp.concatenate(bands, axis=0)


def spread_rows(x, lane_mat):
    rows = [
        jnp.concatenate([x[at + dz * 16 : at + dz * 16 + 16] for dz in range(4)], axis=1) for at in range(0, x.shape[0], 64)
    ]
    return dot_nt(jnp.concatenate(rows, axis=0), lane_mat).astype(BF16)


def rows_to_blocks(spread, row_mat):
    count = spread.shape[0] // 64
    columns = []
    for i in range(count):
        part = spread[i * 64 : (i + 1) * 64]
        columns.append(jnp.concatenate([part[:, p * 128 : (p + 1) * 128] for p in range(4)], axis=0))
    moved = dot_tn(row_mat, jnp.concatenate(columns, axis=1))
    return [moved[:, i * 128 : (i + 1) * 128] for i in range(count)]


def load_weights(p_ref, feature_mat, w0, w1, w2, wo):
    for k in range(4):
        lanes = slice(k * 128, (k + 1) * 128)
        for at in first_rows():
            w0[at[0] : at[0] + 16, lanes] = p_ref[pl.ds(at[1] + k, 16, stride=16), :].astype(BF16)
        w1[:, lanes] = p_ref[pl.ds(W1_AT + k, HID, stride=4), :].astype(BF16)
        w2[:, lanes] = p_ref[pl.ds(W2_AT + k, HID, stride=4), :].astype(BF16)
    for k in range(3):
        columns = p_ref[pl.ds(WO_AT + k, HID, stride=3), :].astype(BF16)
        wo[:, k * 128 : (k + 1) * 128] = dot(columns, feature_mat).astype(BF16)


def first_rows():
    return [(c * 64 + dz * 16, (c * 64 + dz) * 4) for c in range(3) for dz in range(4)]


def velocity_blocks(v_ref):
    return [
        v_ref[c, px * 4 : px * 4 + 4].reshape(256, 128).astype(BF16) for c in range(3) for px in range(2)
    ]


def layer(w, hidden, a_out, d_out):
    z = dot_tn(w[...], hidden)
    s = 0.5 * jnp.tanh(0.5 * z) + 0.5
    a = z * s
    d_out[...] = s + a * (1.0 - s)
    hidden = a.astype(BF16)
    a_out[...] = hidden
    return hidden


def forward_first_kernel(
    v_hbm, p_hbm, row_hbm, lane_hbm, feat_hbm, side_hbm, index_hbm,
    v_out, p_out, row_out, lane_out, feat_out, side_out, index_out, x_out, sems
):
    copies = [
        pltpu.make_async_copy(src, dst, sems.at[i])
        for i, (src, dst) in enumerate(
            ((v_hbm, v_out), (row_hbm, row_out), (lane_hbm, lane_out), (p_hbm, p_out), (feat_hbm, feat_out), (side_hbm, side_out), (index_hbm, index_out))
        )
    ]
    for copy in copies:
        copy.start()
    for copy in copies[:3]:
        copy.wait()
    x_out[...] = cells_to_patches(velocity_blocks(v_out), row_out[...], lane_out[...], 3)
    for copy in copies[3:]:
        copy.wait()


def parity(rank_ref, n_tile):
    rank = rank_ref[0]
    return (rank // n_tile) % 2 == 0, rank % 2 == 0


def strips_kernel(n_tile, rank_ref, v_ref, xa_ref, xb_ref, ya_out, yb_out):
    role_even, tile_even = parity(rank_ref, n_tile)

    def fill(first_out, last_out, low_ref, high_ref):
        for out, at in ((first_out, 0), (last_out, CY - 2)):
            out[:, 2:10] = v_ref[:, :, at : at + 2, :]
            out[:, 0:2] = low_ref[...].astype(F32)[:, :, at : at + 2, :]
            out[:, 10:12] = high_ref[...].astype(F32)[:, :, at : at + 2, :]

    for even_r in (True, False):
        for even_t in (True, False):

            @pl.when((role_even == even_r) & (tile_even == even_t))
            def _():
                first_out, last_out = (yb_out, ya_out) if even_t else (ya_out, yb_out)
                low_ref, high_ref = (xb_ref, xa_ref) if even_r else (xa_ref, xb_ref)
                fill(first_out, last_out, low_ref, high_ref)


def forward_rest_kernel(p_ref, feat_ref, x_ref, a1_out, d1_out, a2_out, d2_out, a3_out, d3_out, pred_out, w0, w1, w2, wo):
    load_weights(p_ref, feat_ref[...], w0, w1, w2, wo)
    hidden = layer(w0, x_ref[...], a1_out, d1_out)
    hidden = layer(w1, hidden, a2_out, d2_out)
    hidden = layer(w2, hidden, a3_out, d3_out)
    pred_out[...] = dot_tn(wo[...], hidden)


def fill_padded(pad, rank_ref, n_tile, v_ref, xa_ref, xb_ref, ya_ref, yb_ref):
    role_even, tile_even = parity(rank_ref, n_tile)
    pad[:, 2:10, 8:72, :] = v_ref[...]
    for even in (True, False):

        @pl.when(role_even == even)
        def _():
            pad[:, 0:2, 8:72, :] = (xb_ref if even else xa_ref)[...].astype(F32)
            pad[:, 10:12, 8:72, :] = (xa_ref if even else xb_ref)[...].astype(F32)

        @pl.when(tile_even == even)
        def _():
            pad[:, :, 6:8, :] = (yb_ref if even else ya_ref)[...]
            pad[:, :, 72:74, :] = (ya_ref if even else yb_ref)[...]


def block_of(position, rank, masks, n_tile, send):
    core = (rank // n_tile) % 2
    if send:
        core = 1 - core
    steps = len(masks[0])
    out = rank
    for i in range(steps):
        mask = jnp.where(core == 0, masks[0][i], masks[1][i])
        out = out ^ (((position >> (steps - 1 - i)) & 1) * mask)
    return out


def box(field_sum):
    along = field_sum[:, 0:64] + field_sum[:, 1:65] + field_sum[:, 2:66]
    return (along + roll_z(along, 1) + roll_z(along, CZ - 1)) * (1.0 / 27.0)


def roll_z(x, by):
    return pltpu.roll(x, by, x.ndim - 1)


def stress_blocks(pad):
    out = [None] * 12
    for px in range(2):
        first = 1 + px * 4
        planes = [[pad[c, first + i, 7:73, :] for i in range(6)] for c in range(3)]
        smooth = []
        for c in range(3):
            sums = jnp.stack([planes[c][i] + planes[c][i + 1] + planes[c][i + 2] for i in range(4)])
            smooth.append(box(sums))
        for k, (a, b) in enumerate(PAIRS):
            prod = [planes[a][i] * planes[b][i] for i in range(6)]
            sums = jnp.stack([prod[i] + prod[i + 1] + prod[i + 2] for i in range(4)])
            value = box(sums) - smooth[a] * smooth[b]
            out[k * 2 + px] = value.astype(BF16).reshape(256, 128)
    return out


def multiplicity(index_ref, count_ref):
    index = index_ref[...]
    selected = index.shape[1]
    live = lax.broadcasted_iota(jnp.int32, (16, selected), 1) < count_ref[0]
    high = lax.broadcasted_iota(jnp.int32, (16, selected), 0) == (index >> 7)
    left = jnp.where(high & live, 1.0, 0.0).astype(BF16)
    low = lax.broadcasted_iota(jnp.int32, (128, selected), 0) == (index & 127)
    right = jnp.where(low, 1.0, 0.0).astype(BF16)
    return dot_nt(left, right)


def backward_kernel(row_scale, rows, masks, n_tile, in_order, rank_ref, count_ref, index_ref, v_ref, xa_ref, xb_ref, ya_ref, yb_ref, row_ref, lane_ref,
                    feat_ref, w1, w2, wo, x_ref, a1_ref, a2_ref, a3_ref, d1_ref, d2_ref, d3_ref, pred_ref, *rest):
    if in_order:
        send_out, keep_out, pad, grads = rest
    else:
        grads, pad = rest
    weight = multiplicity(index_ref, count_ref) * row_scale
    weight = jnp.concatenate([weight[q : q + 1] for q in range(8)], axis=1)
    fill_padded(pad, rank_ref, n_tile, v_ref, xa_ref, xb_ref, ya_ref, yb_ref)
    target = cells_to_patches(stress_blocks(pad), row_ref[...], lane_ref[...], 6)
    error = ((pred_ref[...] - target.astype(F32)) * weight).astype(BF16)
    grad = dot_nt(a3_ref[...], error)
    for k in range(3):
        part = grad[:, k * 128 : (k + 1) * 128]
        high = part.astype(BF16)
        low = (part - high.astype(F32)).astype(BF16)
        grads[pl.ds(WO_AT + k, HID, stride=3), :] = dot_nt(high, feat_ref[...]) + dot_nt(low, feat_ref[...])
    up = dot(wo[...], error)
    for d_ref, left_ref, at, w in ((d3_ref, a2_ref, W2_AT, w2), (d2_ref, a1_ref, W1_AT, w1), (d1_ref, x_ref, 0, None)):
        slope = (up * d_ref[...]).astype(BF16)
        grad = dot_nt(left_ref[...], slope)
        size = left_ref.shape[0]
        for k in range(4):
            lanes = slice(k * 128, (k + 1) * 128)
            if w is None:
                for src, dst in first_rows():
                    grads[pl.ds(dst + k, 16, stride=16), :] = grad[src : src + 16, lanes]
            else:
                grads[pl.ds(at + k, size, stride=4), :] = grad[:, lanes]
        if w is not None:
            up = dot(w[...], slope)
    if in_order:
        half = keep_out.shape[0]

        def place(i, carry):
            here = pl.multiple_of(block_of(i + half, rank_ref[0], masks, n_tile, True) * rows, 8)
            send_out[i] = grads[pl.ds(here, rows), :].astype(BF16)
            here = pl.multiple_of(block_of(i, rank_ref[0], masks, n_tile, False) * rows, 8)
            keep_out[i] = grads[pl.ds(here, rows), :]
            return carry

        lax.fori_loop(0, half, place, 0)


def substep(now, after_x, before_x, after_y, before_y):
    after_z = [roll_z(f, CZ - 1) for f in now]
    before_z = [roll_z(f, 1) for f in now]
    out = []
    for c in range(3):
        transport = now[0] * (0.5 * (after_x[c] - before_x[c]))
        transport = transport + now[1] * (0.5 * (after_y[c] - before_y[c]))
        transport = transport + now[2] * (0.5 * (after_z[c] - before_z[c]))
        laplace = after_x[c] + before_x[c] + after_y[c] + before_y[c] + after_z[c] + before_z[c] - 6.0 * now[c]
        out.append(now[c] + STEP_DT * (VISCOSITY * laplace - transport))
    return out


def flow_kernel(n_tile, rank_ref, v_ref, xa_ref, xb_ref, ya_ref, yb_ref, row_ref, lane_ref, flow_out, x_out, xa_out, xb_out, ya_out, yb_out, pad, mid):
    fill_padded(pad, rank_ref, n_tile, v_ref, xa_ref, xb_ref, ya_ref, yb_ref)
    for src, dst, first, count, low, high in ((pad, mid, 1, 10, 7, 73), (mid, flow_out, 2, 8, 8, 72)):
        for i in range(first, first + count):
            now = [src[c, i, low:high, :] for c in range(3)]
            after_x = [src[c, i + 1, low:high, :] for c in range(3)]
            before_x = [src[c, i - 1, low:high, :] for c in range(3)]
            after_y = [src[c, i, low + 1 : high + 1, :] for c in range(3)]
            before_y = [src[c, i, low - 1 : high - 1, :] for c in range(3)]
            new = substep(now, after_x, before_x, after_y, before_y)
            for c in range(3):
                if dst is mid:
                    mid[c, i, low:high, :] = new[c]
                else:
                    flow_out[c, i - 2] = new[c]
    x = cells_to_patches(velocity_blocks(flow_out), row_ref[...], lane_ref[...], 3)
    x_out[...] = x
    role_even, tile_even = parity(rank_ref, n_tile)
    halves = (x[:, :512], x[:, 512:])
    edges = [jnp.concatenate([half[:, at : at + 32] for half in halves] * 2, axis=1) for at in (0, 480)]
    for even in (True, False):

        @pl.when(role_even == even)
        def _():
            (xb_out if even else xa_out)[...] = halves[0]
            (xa_out if even else xb_out)[...] = halves[1]

        @pl.when(tile_even == even)
        def _():
            (yb_out if even else ya_out)[...] = edges[0]
            (ya_out if even else yb_out)[...] = edges[1]


def model_kernel(rows, masks, n_tile, in_order, rank_ref, p_ref, own_a, own_b, other_a, other_b, flow_ref, x_ref, xa_ref, xb_ref, ya_ref, yb_ref, row_ref, lane_ref,
                 feat_ref, side_ref, p_hbm, v_hbm, force_hbm, p_new, w0, w1, w2, wo, x_all, cells, side, edge, pad, v_new, force_new, sems):
    if in_order:
        half, cut = own_a.shape[0], own_a.shape[1]

        def place(i, carry):
            for low, high, at, send in ((own_a, own_b, i, False), (other_a, other_b, i + half, True)):
                base = block_of(at, rank_ref[0], masks, n_tile, send) * rows
                here = pl.ds(pl.multiple_of(base, 8), cut)
                p_new[here, :] = p_ref[here, :] - low[i].astype(F32)
                here = pl.ds(pl.multiple_of(base + cut, 8), rows - cut)
                p_new[here, :] = p_ref[here, :] - high[i].astype(F32)
            return carry

        lax.fori_loop(0, half, place, 0)
    else:
        p_new[...] = p_ref[...] - own_a[...].astype(F32)
    copies = [pltpu.make_async_copy(p_new, p_hbm, sems.at[0])]
    copies[0].start()
    load_weights(p_new, feat_ref[...], w0, w1, w2, wo)
    w_side = dot(wo[...], side_ref[...]).astype(BF16)
    role_even, tile_even = parity(rank_ref, n_tile)
    x_all[:, 0:1024] = x_ref[...]
    low = lax.broadcasted_iota(jnp.int32, (FEAT, 128), 1) < 64
    for even in (True, False):

        @pl.when(role_even == even)
        def _():
            x_all[:, 1024:1536] = (xb_ref if even else xa_ref)[...]
            x_all[:, 1536:2048] = (xa_ref if even else xb_ref)[...]

        @pl.when(tile_even == even)
        def _():
            before, after = (yb_ref, ya_ref) if even else (ya_ref, yb_ref)
            x_all[:, 2048:2176] = jnp.where(low, before[...].astype(F32), after[...].astype(F32)).astype(BF16)

    hidden = x_all[...]
    for w in (w0, w1, w2):
        z = dot_tn(w[...], hidden)
        hidden = (z * (0.5 * jnp.tanh(0.5 * z) + 0.5)).astype(BF16)
    modelled = dot_tn(wo[...], hidden[:, :1024]).astype(BF16)
    sides = dot_tn(w_side, hidden[:, 1024:2048]).astype(BF16)
    edges = dot_tn(wo[...], hidden[:, 2048:]).astype(BF16)
    for stage, ready in enumerate(((0, 3, 4), (1, 5), (2,))):
        groups = []
        for k in ready:
            groups += [modelled[k * 64 : k * 64 + 64, q * 128 : q * 128 + 128] for q in range(8)]
        if stage == 0:
            groups += [sides[q // 4 * 64 : q // 4 * 64 + 64, q * 128 : q * 128 + 128] for q in range(8)]
            groups += [edges[k * 64 : k * 64 + 64] for k in (3, 1, 5)]
        spread = spread_rows(jnp.concatenate(groups, axis=0), lane_ref[...])
        whole = spread.shape[0] // 64
        blocks = rows_to_blocks(spread[: whole * 64], row_ref[...])
        for n, k in enumerate(ready):
            for px in range(2):
                cells[k, px * 4 : px * 4 + 4] = blocks[n * 2 + px].reshape(4, CY, CZ)
        if stage == 0:
            for i in range(3):
                side[0, i] = blocks[6][i * CY : (i + 1) * CY]
                side[1, i] = blocks[7][i * CY : (i + 1) * CY]
            for slot in range(4):
                edge[slot] = spread[whole * 64 :, slot * 128 : slot * 128 + 128].astype(F32)
        i = stage
        pad[i, :, 8:72, :] = cells[(3, 1, 5)[i]]
        for px in range(2):
            pad[i, px * 4 : px * 4 + 4, 7, :] = edge[px, pl.ds(i * 16 + 3, 4, stride=4), :]
            pad[i, px * 4 : px * 4 + 4, 72, :] = edge[2 + px, pl.ds(i * 16, 4, stride=4), :]
        kx, kz = COMPONENT[i][0], COMPONENT[i][2]
        for x in range(CX):
            after = cells[kx, x + 1] if x < CX - 1 else side[1, i]
            before = cells[kx, x - 1] if x else side[0, i]
            total = 0.5 * (after - before)
            total = total + 0.5 * (pad[i, x, 9:73, :] - pad[i, x, 7:71, :])
            centre = cells[kz, x]
            total = total + 0.5 * (roll_z(centre, CZ - 1) - roll_z(centre, 1))
            force = -SGS_SCALE * total
            force_new[i, x] = force
            v_new[i, x] = flow_ref[i, x] + force
        for n, (src, dst) in enumerate(((v_new, v_hbm), (force_new, force_hbm))):
            copies.append(pltpu.make_async_copy(src.at[i], dst.at[i], sems.at[1 + 2 * i + n]))
            copies[-1].start()
    for copy in copies:
        copy.wait()


def call(kernel, outs, args, scratch, scalars=0, flops=0, name=None, sems=0, hbm_in=False, hbm_out=False):
    space = {True: pltpu.HBM, False: pltpu.VMEM}
    size = sum(a.size * a.dtype.itemsize for a in args) + sum(int(np.prod(s)) * np.dtype(t).itemsize for s, t in outs)
    args = list(args)
    args[scalars:] = [pltpu.with_memory_space_constraint(a, space[hbm_in]) for a in args[scalars:]]
    return pl.pallas_call(
        kernel,
        out_shape=[space[hbm_out](s, t) for s, t in outs],
        in_specs=[pl.BlockSpec(memory_space=pltpu.SMEM)] * scalars
        + [pl.BlockSpec(memory_space=space[hbm_in])] * (len(args) - scalars),
        out_specs=[pl.BlockSpec(memory_space=space[hbm_out])] * len(outs),
        scratch_shapes=[s if isinstance(s, pl.MemoryRef) else pltpu.VMEM(*s) for s in scratch] + ([pltpu.SemaphoreType.DMA((sems,))] if sems else []),
        compiler_params=pltpu.CompilerParams(vmem_limit_bytes=VMEM_LIMIT),
        cost_estimate=pl.CostEstimate(flops=flops, transcendentals=0, bytes_accessed=size),
        name=name,
    )(*args)


WEIGHTS = [((FEAT, HID), BF16), ((HID, HID), BF16), ((HID, HID), BF16), ((HID, TGT), BF16)]
PADDED = ((3, 12, 80, 128), F32)
ACT = ((HID, NPATCH), BF16)
DER = ((HID, NPATCH), F32)


def bits(size):
    return [1 << i for i in range(size.bit_length() - 1)]


def stage_masks(n_role, n_tile):
    role = [n_tile * b for b in bits(n_role)]
    tile = bits(n_tile)
    rest = tile[:1] + role[1:] + tile[1:]
    other = rest[1::-1] + rest[2:]
    return role[:1] + rest, role[:1] + other


def swaps(axis):
    size = lax.axis_size(axis)
    first = [(i, i ^ 1) for i in range(size)]
    return first, [(i, (i + 1) % size if i % 2 else (i - 1) % size) for i in range(size)]


def local(velocity, params, first_moment, second_moment, patch_index, patch_count):
    n_role, n_tile = lax.axis_size("role"), lax.axis_size("tile")
    devices = n_role * n_tile
    own_rank = lax.axis_index(BOTH)
    rows = ROWS // devices
    in_order = rows % 8 == 0
    masks = stage_masks(n_role, n_tile)
    steps = len(masks[0])
    core_of = [(d // n_tile) & 1 for d in range(devices)]

    def exchange(x, step):
        pairs = [(d, d ^ masks[core_of[d]][step]) for d in range(devices)]
        return lax.ppermute(x, BOTH, pairs)

    def offsets(core):
        return [
            functools.reduce(lambda a, b: a ^ b, [masks[core][i] if (j >> (steps - 1 - i)) & 1 else 0 for i in range(steps)])
            for j in range(devices)
        ]

    half = devices // 2
    rank = own_rank.astype(jnp.int32).reshape(1)
    role_even = (own_rank // n_tile) % 2 == 0
    role_swaps, tile_swaps = swaps("role"), swaps("tile")
    p2 = params.reshape(ROWS, 128)
    selected = patch_index.shape[0]
    row_scale = 1.0 / (selected // 4)

    first, last = velocity[:, :2].astype(BF16), velocity[:, CX - 2 :].astype(BF16)
    xb = lax.ppermute(jnp.where(role_even, first, last), "role", role_swaps[1])
    xa = lax.ppermute(jnp.where(role_even, last, first), "role", role_swaps[0])
    v_in, p_in, row_mat, lane_mat, feat_mat, side_mat, index, x = call(
        forward_first_kernel,
        [((3, CX, CY, CZ), F32), ((ROWS, 128), F32), ((256, 256), BF16), ((512, 512), BF16), ((128, 128), BF16)]
        + [((TGT, 128), BF16), ((1, selected), jnp.int32), ((FEAT, NPATCH), BF16)],
        [velocity, p2]
        + [jnp.asarray(m, BF16) for m in (row_matrix(), lane_matrix(), feature_matrix(), side_matrix())]
        + [patch_index.reshape(1, selected)],
        [],
        flops=1 << 28,
        name="forward_first",
        sems=7,
        hbm_in=True,
    )
    xa, xb, v_in, x = lax.optimization_barrier((xa, xb, v_in, x))
    strip = ((3, CX + 4, 2, CZ), F32)
    ya, yb = call(functools.partial(strips_kernel, n_tile), [strip] * 2, [rank, v_in, xa, xb], [], scalars=1, name="strips")
    yb = lax.ppermute(yb, "tile", tile_swaps[1])
    ya = lax.ppermute(ya, "tile", tile_swaps[0])
    a1, d1, a2, d2, a3, d3, pred, *weights = call(
        forward_rest_kernel,
        [ACT, DER, ACT, DER, ACT, DER, ((TGT, NPATCH), F32)] + WEIGHTS,
        [p_in, feat_mat, x],
        [],
        flops=2 * 819200 * NPATCH,
        name="forward_rest",
    )
    halos = [xa, xb, ya, yb]

    grad_outs = [((half, rows, 128), BF16), ((half, rows, 128), F32)] if in_order else [((ROWS, 128), F32)]
    grads = call(
        functools.partial(backward_kernel, row_scale, rows, masks, n_tile, in_order),
        grad_outs,
        [rank, patch_count, index, v_in]
        + halos
        + [row_mat, lane_mat, feat_mat]
        + weights[1:]
        + [x, a1, a2, a3, d1, d2, d3, pred],
        [PADDED] + ([((ROWS, 128), F32)] if in_order else []),
        scalars=2,
        flops=4 * 819200 * NPATCH,
        name="backward",
    )
    if in_order:
        send, keep = grads
    else:
        here = jnp.arange(devices, dtype=jnp.int32)
        order = jnp.where(
            here < half,
            block_of(here, own_rank, masks, n_tile, False),
            block_of(here, own_rank, masks, n_tile, True),
        )
        placed = grads[0].reshape(devices, rows, 128)[order]
        send, keep = placed[half:].astype(BF16), placed[:half]

    size = half
    fence = lax.optimization_barrier
    got = exchange(send, 0)
    for step in range(1, steps):
        size //= 2
        if step < steps - 1:
            send = (keep[size:] + got[size:].astype(F32)).astype(BF16)
            keep = keep[:size] + got[:size].astype(F32)
        else:
            send = keep = (keep + got.astype(F32)).astype(BF16)
        if step == 1:
            send, still, moments = fence((send, v_in, jnp.stack([first_moment, second_moment])))
        if step == 3:
            send, fxb = fence((send, fxb))
        if step == steps - 1:
            send, fxa, fya = fence((send, fxa, fya))
        got = exchange(send, step)
        if step == 1:
            moments_other = exchange(moments, steps - 1)
            flow, x_new, fxa, fxb, fya, fyb = call(
                functools.partial(flow_kernel, n_tile),
                [((3, CX, CY, CZ), F32), ((FEAT, NPATCH), BF16)]
                + [((FEAT, NPATCH // 2), BF16)] * 2
                + [((FEAT, 128), BF16)] * 2,
                [rank, still] + halos + [row_mat, lane_mat],
                [PADDED, PADDED],
                scalars=1,
                flops=1 << 30,
                name="flow",
            )
            got, flow, x_new, fxa, fxb, fya, fyb = fence((got, flow, x_new, fxa, fxb, fya, fyb))
        if step == 2:
            got, moments_other = fence((got, moments_other))
        if step == 3:
            fxb = lax.ppermute(fxb, "role", role_swaps[1])
        if step == steps - 1:
            fxa = lax.ppermute(fxa, "role", role_swaps[0])
            fya = lax.ppermute(fya, "tile", tile_swaps[0])
            got, fxb = fence((got, fxb))
    grad = (keep.astype(F32) + got[::-1].astype(F32)).reshape(2, -1)
    first_two = jnp.stack([first_moment, moments_other[0]])
    second_two = jnp.stack([second_moment, moments_other[1]])
    first_two = BETA_ONE * first_two + (1.0 - BETA_ONE) * grad
    second_two = BETA_TWO * second_two + (1.0 - BETA_TWO) * grad * grad
    first_out, second_out = first_two[0], second_two[0]
    fix_first = 1.0 - BETA_ONE**ADAM_STEP
    fix_second = 1.0 - BETA_TWO**ADAM_STEP
    update = LEARN_RATE * (first_two / fix_first) / (jnp.sqrt(second_two / fix_second) + EPSILON)
    held = update.astype(BF16).reshape(2, rows, 128)
    at = rows // 16 * 8
    held = [held[:, :at], held[:, at:]]
    for step in range(steps - 2, 0, -1):
        if step == 2:
            held[0], fyb = fence((held[0], fyb))
        got = [exchange(part, step) for part in held]
        if step == 2:
            fyb = lax.ppermute(fyb, "tile", tile_swaps[1])
        if step == 1:
            got[0], fyb = fence((got[0], fyb))
        if step == steps - 2:
            got[0], fxa, fya = fence((got[0], fxa, fya))
        held = [jnp.concatenate([part, new], axis=0) for part, new in zip(held, got)]
    other = [exchange(part, 0) for part in held]
    if not in_order:
        slots = jnp.zeros((devices,), jnp.int32).at[order].set(jnp.arange(devices, dtype=jnp.int32))
        all_parts = jnp.concatenate([jnp.concatenate(held, axis=1), jnp.concatenate(other, axis=1)], axis=0)
        held = other = [all_parts[slots].reshape(ROWS, 128)] * 2

    p_new, velocity_out, sgs_force = call(
        functools.partial(model_kernel, rows, masks, n_tile, in_order),
        [((ROWS, 128), F32)] + [((3, CX, CY, CZ), F32)] * 2,
        [rank, p_in, *held, *other, flow, x_new, fxa, fxb, fya, fyb, row_mat, lane_mat, feat_mat, side_mat],
        [((ROWS, 128), F32)]
        + WEIGHTS
        + [((FEAT, 17 * 128), BF16), ((6, CX, CY, CZ), F32), ((2, 3, CY, CZ), F32), ((4, 48, 128), F32), ((3, CX, 80, CZ), F32)]
        + [((3, CX, CY, CZ), F32)] * 2,
        scalars=1,
        flops=4 * 819200 * NPATCH,
        name="model",
        sems=7,
        hbm_out=True,
    )
    return (velocity_out, sgs_force, p_new.reshape(-1), first_out, second_out)


def solution(mesh):
    placed = (
        P(None, "role", "tile", None),
        P(),
        P(BOTH),
        P(BOTH),
        P(BOTH),
        P(BOTH),
    )
    return jax.shard_map(
        local,
        mesh=mesh,
        in_specs=placed,
        out_specs=(
            P(None, "role", "tile", None),
            P(None, "role", "tile", None),
            P(),
            P(BOTH),
            P(BOTH),
        ),
        check_vma=False,
    )
```

```python
import functools

import jax
import jax.numpy as jnp
import numpy as np
from jax import lax
from jax.experimental import pallas as pl
from jax.experimental.pallas import tpu as pltpu
from jax.sharding import PartitionSpec as P

FEAT = 192
TGT = 384
HID = 512
ADAM_STEP = 100
STEP_DT = 0.1
VISCOSITY = 0.1
SGS_SCALE = 1.5
BETA_ONE = 0.9
BETA_TWO = 0.999
LEARN_RATE = 0.001
EPSILON = 1e-08
PAIRS = ((0, 0), (1, 1), (2, 2), (0, 1), (0, 2), (1, 2))
COMPONENT = ((0, 3, 4), (3, 1, 5), (4, 5, 2))

CX, CY, CZ = 8, 64, 128
NPATCH = 1024
ROWS = 6400
W1_AT = 768
W2_AT = W1_AT + 2048
WO_AT = W2_AT + 2048
BOTH = ("role", "tile")
F32, BF16 = jnp.float32, jnp.bfloat16
VMEM_LIMIT = 24 * 1024 * 1024


def row_matrix():
    matrix = np.zeros((256, 256), np.float32)
    for dx in range(4):
        for j in range(4):
            for pyl in range(4):
                for dy in range(4):
                    matrix[pyl * 64 + j * 16 + dx * 4 + dy, dx * 64 + j * 16 + pyl * 4 + dy] = 1
    return matrix


def lane_matrix():
    matrix = np.zeros((512, 512), np.float32)
    for pyl in range(4):
        for pz in range(32):
            for dz in range(4):
                matrix[pyl * 128 + pz * 4 + dz, dz * 128 + pyl * 32 + pz] = 1
    return matrix


def feature_matrix():
    matrix = np.zeros((128, 128), np.float32)
    for c in range(2):
        for off in range(16):
            for dz in range(4):
                matrix[c * 64 + off * 4 + dz, c * 64 + dz * 16 + off] = 1
    return matrix


def side_matrix():
    matrix = np.zeros((TGT, 128), np.float32)
    for side, dx in enumerate((3, 0)):
        for dz in range(4):
            for slot, k in enumerate((0, 3, 4)):
                for dy in range(4):
                    matrix[k * 64 + dz * 16 + dx * 4 + dy, side * 64 + dz * 16 + slot * 4 + dy] = 1
    return matrix


def dot(a, b):
    return jnp.dot(a, b, preferred_element_type=F32)


def dot_tn(a, b):
    return lax.dot_general(a, b, (((0,), (0,)), ((), ())), preferred_element_type=F32)


def dot_nt(a, b):
    return lax.dot_general(a, b, (((1,), (1,)), ((), ())), preferred_element_type=F32)


def cells_to_patches(blocks, row_mat, lane_mat, channels):
    moved = dot(row_mat, jnp.concatenate(blocks, axis=1)).astype(BF16)
    rows = []
    for i in range(2 * channels):
        part = moved[:, i * 128 : (i + 1) * 128]
        rows.append(jnp.concatenate([part[p * 64 : (p + 1) * 64] for p in range(4)], axis=1))
    spread = dot(jnp.concatenate(rows, axis=0), lane_mat).astype(BF16)
    bands = []
    for c in range(channels):
        for dz in range(4):
            bands.append(
                jnp.concatenate(
                    [
                        spread[((c * 2 + px) * 4 + j) * 16 : ((c * 2 + px) * 4 + j) * 16 + 16, dz * 128 : dz * 128 + 128]
                        for px in range(2)
                        for j in range(4)
                    ],
                    axis=1,
                )
            )
    return jnp.concatenate(bands, axis=0)


def spread_rows(x, lane_mat):
    rows = [
        jnp.concatenate([x[at + dz * 16 : at + dz * 16 + 16] for dz in range(4)], axis=1) for at in range(0, x.shape[0], 64)
    ]
    return dot_nt(jnp.concatenate(rows, axis=0), lane_mat).astype(BF16)


def rows_to_blocks(spread, row_mat):
    count = spread.shape[0] // 64
    columns = []
    for i in range(count):
        part = spread[i * 64 : (i + 1) * 64]
        columns.append(jnp.concatenate([part[:, p * 128 : (p + 1) * 128] for p in range(4)], axis=0))
    moved = dot_tn(row_mat, jnp.concatenate(columns, axis=1))
    return [moved[:, i * 128 : (i + 1) * 128] for i in range(count)]


def load_weights(p_ref, feature_mat, w0, w1, w2, wo):
    for k in range(4):
        lanes = slice(k * 128, (k + 1) * 128)
        for at in first_rows():
            w0[at[0] : at[0] + 16, lanes] = p_ref[pl.ds(at[1] + k, 16, stride=16), :].astype(BF16)
        w1[:, lanes] = p_ref[pl.ds(W1_AT + k, HID, stride=4), :].astype(BF16)
        w2[:, lanes] = p_ref[pl.ds(W2_AT + k, HID, stride=4), :].astype(BF16)
    for k in range(3):
        columns = p_ref[pl.ds(WO_AT + k, HID, stride=3), :].astype(BF16)
        wo[:, k * 128 : (k + 1) * 128] = dot(columns, feature_mat).astype(BF16)


def first_rows():
    return [(c * 64 + dz * 16, (c * 64 + dz) * 4) for c in range(3) for dz in range(4)]


def velocity_blocks(v_ref):
    return [
        v_ref[c, px * 4 : px * 4 + 4].reshape(256, 128).astype(BF16) for c in range(3) for px in range(2)
    ]


def layer(w, hidden, a_out, d_out):
    z = dot_tn(w[...], hidden)
    s = 0.5 * jnp.tanh(0.5 * z) + 0.5
    a = z * s
    d_out[...] = s + a * (1.0 - s)
    hidden = a.astype(BF16)
    a_out[...] = hidden
    return hidden


def forward_first_kernel(
    v_hbm, row_hbm, lane_hbm, feat_hbm, side_hbm, index_hbm,
    v_out, row_out, lane_out, feat_out, side_out, index_out, x_out, sems
):
    copies = [
        pltpu.make_async_copy(src, dst, sems.at[i])
        for i, (src, dst) in enumerate(
            ((v_hbm, v_out), (row_hbm, row_out), (lane_hbm, lane_out), (feat_hbm, feat_out), (side_hbm, side_out), (index_hbm, index_out))
        )
    ]
    for copy in copies:
        copy.start()
    for copy in copies[:3]:
        copy.wait()
    x_out[...] = cells_to_patches(velocity_blocks(v_out), row_out[...], lane_out[...], 3)
    for copy in copies[3:]:
        copy.wait()


def parity(rank_ref, n_tile):
    rank = rank_ref[0]
    return (rank // n_tile) % 2 == 0, rank % 2 == 0


def strips_kernel(n_tile, rank_ref, v_ref, xa_ref, xb_ref, ya_out, yb_out):
    role_even, tile_even = parity(rank_ref, n_tile)

    def fill(first_out, last_out, low_ref, high_ref):
        for out, at in ((first_out, 0), (last_out, CY - 2)):
            out[:, 2:10] = v_ref[:, :, at : at + 2, :]
            out[:, 0:2] = low_ref[...].astype(F32)[:, :, at : at + 2, :]
            out[:, 10:12] = high_ref[...].astype(F32)[:, :, at : at + 2, :]

    for even_r in (True, False):
        for even_t in (True, False):

            @pl.when((role_even == even_r) & (tile_even == even_t))
            def _():
                first_out, last_out = (yb_out, ya_out) if even_t else (ya_out, yb_out)
                low_ref, high_ref = (xb_ref, xa_ref) if even_r else (xa_ref, xb_ref)
                fill(first_out, last_out, low_ref, high_ref)


def forward_rest_kernel(p_ref, feat_ref, x_ref, a1_out, d1_out, a2_out, d2_out, a3_out, d3_out, pred_out, w0, w1, w2, wo):
    load_weights(p_ref, feat_ref[...], w0, w1, w2, wo)
    hidden = layer(w0, x_ref[...], a1_out, d1_out)
    hidden = layer(w1, hidden, a2_out, d2_out)
    hidden = layer(w2, hidden, a3_out, d3_out)
    pred_out[...] = dot_tn(wo[...], hidden)


def fill_padded(pad, rank_ref, n_tile, v_ref, xa_ref, xb_ref, ya_ref, yb_ref):
    role_even, tile_even = parity(rank_ref, n_tile)
    pad[:, 2:10, 8:72, :] = v_ref[...]
    for even in (True, False):

        @pl.when(role_even == even)
        def _():
            pad[:, 0:2, 8:72, :] = (xb_ref if even else xa_ref)[...].astype(F32)
            pad[:, 10:12, 8:72, :] = (xa_ref if even else xb_ref)[...].astype(F32)

        @pl.when(tile_even == even)
        def _():
            pad[:, :, 6:8, :] = (yb_ref if even else ya_ref)[...]
            pad[:, :, 72:74, :] = (ya_ref if even else yb_ref)[...]


def block_of(position, rank, masks, n_tile, send):
    core = (rank // n_tile) % 2
    if send:
        core = 1 - core
    steps = len(masks[0])
    out = rank
    for i in range(steps):
        mask = jnp.where(core == 0, masks[0][i], masks[1][i])
        out = out ^ (((position >> (steps - 1 - i)) & 1) * mask)
    return out


def box(field_sum):
    along = field_sum[:, 0:64] + field_sum[:, 1:65] + field_sum[:, 2:66]
    return (along + roll_z(along, 1) + roll_z(along, CZ - 1)) * (1.0 / 27.0)


def roll_z(x, by):
    return pltpu.roll(x, by, x.ndim - 1)


def stress_blocks(pad):
    out = [None] * 12
    for px in range(2):
        first = 1 + px * 4
        planes = [[pad[c, first + i, 7:73, :] for i in range(6)] for c in range(3)]
        smooth = []
        for c in range(3):
            sums = jnp.stack([planes[c][i] + planes[c][i + 1] + planes[c][i + 2] for i in range(4)])
            smooth.append(box(sums))
        for k, (a, b) in enumerate(PAIRS):
            prod = [planes[a][i] * planes[b][i] for i in range(6)]
            sums = jnp.stack([prod[i] + prod[i + 1] + prod[i + 2] for i in range(4)])
            value = box(sums) - smooth[a] * smooth[b]
            out[k * 2 + px] = value.astype(BF16).reshape(256, 128)
    return out


def multiplicity(index_ref, count_ref):
    index = index_ref[...]
    selected = index.shape[1]
    live = lax.broadcasted_iota(jnp.int32, (16, selected), 1) < count_ref[0]
    high = lax.broadcasted_iota(jnp.int32, (16, selected), 0) == (index >> 7)
    left = jnp.where(high & live, 1.0, 0.0).astype(BF16)
    low = lax.broadcasted_iota(jnp.int32, (128, selected), 0) == (index & 127)
    right = jnp.where(low, 1.0, 0.0).astype(BF16)
    return dot_nt(left, right)


def backward_kernel(row_scale, rows, masks, n_tile, in_order, rank_ref, count_ref, index_ref, v_ref, xa_ref, xb_ref, ya_ref, yb_ref, row_ref, lane_ref,
                    feat_ref, w1, w2, wo, x_ref, a1_ref, a2_ref, a3_ref, d1_ref, d2_ref, d3_ref, pred_ref, *rest):
    if in_order:
        send_out, keep_out, pad, grads = rest
    else:
        grads, pad = rest
    weight = multiplicity(index_ref, count_ref) * row_scale
    weight = jnp.concatenate([weight[q : q + 1] for q in range(8)], axis=1)
    fill_padded(pad, rank_ref, n_tile, v_ref, xa_ref, xb_ref, ya_ref, yb_ref)
    target = cells_to_patches(stress_blocks(pad), row_ref[...], lane_ref[...], 6)
    error = ((pred_ref[...] - target.astype(F32)) * weight).astype(BF16)
    grad = dot_nt(a3_ref[...], error)
    for k in range(3):
        part = grad[:, k * 128 : (k + 1) * 128].astype(BF16)
        grads[pl.ds(WO_AT + k, HID, stride=3), :] = dot_nt(part, feat_ref[...])
    up = dot(wo[...], error)
    for d_ref, left_ref, at, w in ((d3_ref, a2_ref, W2_AT, w2), (d2_ref, a1_ref, W1_AT, w1), (d1_ref, x_ref, 0, None)):
        slope = (up * d_ref[...]).astype(BF16)
        grad = dot_nt(left_ref[...], slope)
        size = left_ref.shape[0]
        for k in range(4):
            lanes = slice(k * 128, (k + 1) * 128)
            if w is None:
                for src, dst in first_rows():
                    grads[pl.ds(dst + k, 16, stride=16), :] = grad[src : src + 16, lanes]
            else:
                grads[pl.ds(at + k, size, stride=4), :] = grad[:, lanes]
        if w is not None:
            up = dot(w[...], slope)
    if in_order:
        half = keep_out.shape[0]

        def place(i, carry):
            here = pl.multiple_of(block_of(i + half, rank_ref[0], masks, n_tile, True) * rows, 8)
            send_out[i] = grads[pl.ds(here, rows), :].astype(BF16)
            here = pl.multiple_of(block_of(i, rank_ref[0], masks, n_tile, False) * rows, 8)
            keep_out[i] = grads[pl.ds(here, rows), :]
            return carry

        lax.fori_loop(0, half, place, 0)


def substep(now, after_x, before_x, after_y, before_y):
    after_z = [roll_z(f, CZ - 1) for f in now]
    before_z = [roll_z(f, 1) for f in now]
    out = []
    for c in range(3):
        transport = now[0] * (0.5 * (after_x[c] - before_x[c]))
        transport = transport + now[1] * (0.5 * (after_y[c] - before_y[c]))
        transport = transport + now[2] * (0.5 * (after_z[c] - before_z[c]))
        laplace = after_x[c] + before_x[c] + after_y[c] + before_y[c] + after_z[c] + before_z[c] - 6.0 * now[c]
        out.append(now[c] + STEP_DT * (VISCOSITY * laplace - transport))
    return out


def flow_kernel(n_tile, rank_ref, v_ref, xa_ref, xb_ref, ya_ref, yb_ref, row_ref, lane_ref, flow_out, x_out, xa_out, xb_out, ya_out, yb_out, pad, mid):
    fill_padded(pad, rank_ref, n_tile, v_ref, xa_ref, xb_ref, ya_ref, yb_ref)
    for src, dst, first, count, low, high in ((pad, mid, 1, 10, 7, 73), (mid, flow_out, 2, 8, 8, 72)):
        for i in range(first, first + count):
            now = [src[c, i, low:high, :] for c in range(3)]
            after_x = [src[c, i + 1, low:high, :] for c in range(3)]
            before_x = [src[c, i - 1, low:high, :] for c in range(3)]
            after_y = [src[c, i, low + 1 : high + 1, :] for c in range(3)]
            before_y = [src[c, i, low - 1 : high - 1, :] for c in range(3)]
            new = substep(now, after_x, before_x, after_y, before_y)
            for c in range(3):
                if dst is mid:
                    mid[c, i, low:high, :] = new[c]
                else:
                    flow_out[c, i - 2] = new[c]
    x = cells_to_patches(velocity_blocks(flow_out), row_ref[...], lane_ref[...], 3)
    x_out[...] = x
    role_even, tile_even = parity(rank_ref, n_tile)
    halves = (x[:, :512], x[:, 512:])
    edges = [jnp.concatenate([half[:, at : at + 32] for half in halves] * 2, axis=1) for at in (0, 480)]
    for even in (True, False):

        @pl.when(role_even == even)
        def _():
            (xb_out if even else xa_out)[...] = halves[0]
            (xa_out if even else xb_out)[...] = halves[1]

        @pl.when(tile_even == even)
        def _():
            (yb_out if even else ya_out)[...] = edges[0]
            (ya_out if even else yb_out)[...] = edges[1]


def model_kernel(rows, masks, n_tile, in_order, rank_ref, p_ref, own_a, own_b, other_a, other_b, flow_ref, x_ref, xa_ref, xb_ref, ya_ref, yb_ref, row_ref, lane_ref,
                 feat_ref, side_ref, p_hbm, v_hbm, force_hbm, p_new, w0, w1, w2, wo, x_all, cells, side, edge, pad, v_new, force_new, sems):
    if in_order:
        half, cut = own_a.shape[0], own_a.shape[1]

        def place(i, carry):
            for low, high, at, send in ((own_a, own_b, i, False), (other_a, other_b, i + half, True)):
                base = block_of(at, rank_ref[0], masks, n_tile, send) * rows
                here = pl.ds(pl.multiple_of(base, 8), cut)
                p_new[here, :] = p_ref[here, :] - low[i].astype(F32)
                here = pl.ds(pl.multiple_of(base + cut, 8), rows - cut)
                p_new[here, :] = p_ref[here, :] - high[i].astype(F32)
            return carry

        lax.fori_loop(0, half, place, 0)
    else:
        p_new[...] = p_ref[...] - own_a[...].astype(F32)
    copies = [pltpu.make_async_copy(p_new, p_hbm, sems.at[0])]
    copies[0].start()
    load_weights(p_new, feat_ref[...], w0, w1, w2, wo)
    w_side = dot(wo[...], side_ref[...]).astype(BF16)
    role_even, tile_even = parity(rank_ref, n_tile)
    x_all[:, 0:1024] = x_ref[...]
    low = lax.broadcasted_iota(jnp.int32, (FEAT, 128), 1) < 64
    for even in (True, False):

        @pl.when(role_even == even)
        def _():
            x_all[:, 1024:1536] = (xb_ref if even else xa_ref)[...]
            x_all[:, 1536:2048] = (xa_ref if even else xb_ref)[...]

        @pl.when(tile_even == even)
        def _():
            before, after = (yb_ref, ya_ref) if even else (ya_ref, yb_ref)
            x_all[:, 2048:2176] = jnp.where(low, before[...].astype(F32), after[...].astype(F32)).astype(BF16)

    hidden = x_all[...]
    for w in (w0, w1, w2):
        z = dot_tn(w[...], hidden)
        hidden = (z * (0.5 * jnp.tanh(0.5 * z) + 0.5)).astype(BF16)
    modelled = dot_tn(wo[...], hidden[:, :1024]).astype(BF16)
    sides = dot_tn(w_side, hidden[:, 1024:2048]).astype(BF16)
    edges = dot_tn(wo[...], hidden[:, 2048:]).astype(BF16)
    for stage, ready in enumerate(((0, 3, 4), (1, 5), (2,))):
        groups = []
        for k in ready:
            groups += [modelled[k * 64 : k * 64 + 64, q * 128 : q * 128 + 128] for q in range(8)]
        if stage == 0:
            groups += [sides[q // 4 * 64 : q // 4 * 64 + 64, q * 128 : q * 128 + 128] for q in range(8)]
            groups += [edges[k * 64 : k * 64 + 64] for k in (3, 1, 5)]
        spread = spread_rows(jnp.concatenate(groups, axis=0), lane_ref[...])
        whole = spread.shape[0] // 64
        blocks = rows_to_blocks(spread[: whole * 64], row_ref[...])
        for n, k in enumerate(ready):
            for px in range(2):
                cells[k, px * 4 : px * 4 + 4] = blocks[n * 2 + px].reshape(4, CY, CZ)
        if stage == 0:
            for i in range(3):
                side[0, i] = blocks[6][i * CY : (i + 1) * CY]
                side[1, i] = blocks[7][i * CY : (i + 1) * CY]
            for slot in range(4):
                edge[slot] = spread[whole * 64 :, slot * 128 : slot * 128 + 128].astype(F32)
        i = stage
        pad[i, :, 8:72, :] = cells[(3, 1, 5)[i]]
        for px in range(2):
            pad[i, px * 4 : px * 4 + 4, 7, :] = edge[px, pl.ds(i * 16 + 3, 4, stride=4), :]
            pad[i, px * 4 : px * 4 + 4, 72, :] = edge[2 + px, pl.ds(i * 16, 4, stride=4), :]
        kx, kz = COMPONENT[i][0], COMPONENT[i][2]
        for x in range(CX):
            after = cells[kx, x + 1] if x < CX - 1 else side[1, i]
            before = cells[kx, x - 1] if x else side[0, i]
            total = 0.5 * (after - before)
            total = total + 0.5 * (pad[i, x, 9:73, :] - pad[i, x, 7:71, :])
            centre = cells[kz, x]
            total = total + 0.5 * (roll_z(centre, CZ - 1) - roll_z(centre, 1))
            force = -SGS_SCALE * total
            force_new[i, x] = force
            v_new[i, x] = flow_ref[i, x] + force
        for n, (src, dst) in enumerate(((v_new, v_hbm), (force_new, force_hbm))):
            copies.append(pltpu.make_async_copy(src.at[i], dst.at[i], sems.at[1 + 2 * i + n]))
            copies[-1].start()
    for copy in copies:
        copy.wait()


def call(kernel, outs, args, scratch, scalars=0, flops=0, name=None, sems=0, hbm_in=False, hbm_out=False):
    space = {True: pltpu.HBM, False: pltpu.VMEM}
    size = sum(a.size * a.dtype.itemsize for a in args) + sum(int(np.prod(s)) * np.dtype(t).itemsize for s, t in outs)
    args = list(args)
    args[scalars:] = [pltpu.with_memory_space_constraint(a, space[hbm_in]) for a in args[scalars:]]
    return pl.pallas_call(
        kernel,
        out_shape=[space[hbm_out](s, t) for s, t in outs],
        in_specs=[pl.BlockSpec(memory_space=pltpu.SMEM)] * scalars
        + [pl.BlockSpec(memory_space=space[hbm_in])] * (len(args) - scalars),
        out_specs=[pl.BlockSpec(memory_space=space[hbm_out])] * len(outs),
        scratch_shapes=[s if isinstance(s, pl.MemoryRef) else pltpu.VMEM(*s) for s in scratch] + ([pltpu.SemaphoreType.DMA((sems,))] if sems else []),
        compiler_params=pltpu.CompilerParams(vmem_limit_bytes=VMEM_LIMIT),
        cost_estimate=pl.CostEstimate(flops=flops, transcendentals=0, bytes_accessed=size),
        name=name,
    )(*args)


WEIGHTS = [((FEAT, HID), BF16), ((HID, HID), BF16), ((HID, HID), BF16), ((HID, TGT), BF16)]
PADDED = ((3, 12, 80, 128), F32)
ACT = ((HID, NPATCH), BF16)
DER = ((HID, NPATCH), F32)


def bits(size):
    return [1 << i for i in range(size.bit_length() - 1)]


def stage_masks(n_role, n_tile):
    role = [n_tile * b for b in bits(n_role)]
    tile = bits(n_tile)
    rest = tile[:1] + role[1:] + tile[1:]
    other = rest[1::-1] + rest[2:]
    return role[:1] + rest, role[:1] + other


def swaps(axis):
    size = lax.axis_size(axis)
    first = [(i, i ^ 1) for i in range(size)]
    return first, [(i, (i + 1) % size if i % 2 else (i - 1) % size) for i in range(size)]


def local(velocity, params, first_moment, second_moment, patch_index, patch_count):
    n_role, n_tile = lax.axis_size("role"), lax.axis_size("tile")
    devices = n_role * n_tile
    own_rank = lax.axis_index(BOTH)
    rows = ROWS // devices
    in_order = rows % 8 == 0
    masks = stage_masks(n_role, n_tile)
    steps = len(masks[0])
    core_of = [(d // n_tile) & 1 for d in range(devices)]

    def exchange(x, step):
        pairs = [(d, d ^ masks[core_of[d]][step]) for d in range(devices)]
        return lax.ppermute(x, BOTH, pairs)

    def offsets(core):
        return [
            functools.reduce(lambda a, b: a ^ b, [masks[core][i] if (j >> (steps - 1 - i)) & 1 else 0 for i in range(steps)])
            for j in range(devices)
        ]

    half = devices // 2
    rank = own_rank.astype(jnp.int32).reshape(1)
    role_even = (own_rank // n_tile) % 2 == 0
    role_swaps, tile_swaps = swaps("role"), swaps("tile")
    p2 = params.reshape(ROWS, 128)
    selected = patch_index.shape[0]
    row_scale = 1.0 / (selected // 4)

    first, last = velocity[:, :2].astype(BF16), velocity[:, CX - 2 :].astype(BF16)
    xb = lax.ppermute(jnp.where(role_even, first, last), "role", role_swaps[1])
    xa = lax.ppermute(jnp.where(role_even, last, first), "role", role_swaps[0])
    v_in, row_mat, lane_mat, feat_mat, side_mat, index, x = call(
        forward_first_kernel,
        [((3, CX, CY, CZ), F32), ((256, 256), BF16), ((512, 512), BF16), ((128, 128), BF16)]
        + [((TGT, 128), BF16), ((1, selected), jnp.int32), ((FEAT, NPATCH), BF16)],
        [velocity]
        + [jnp.asarray(m, BF16) for m in (row_matrix(), lane_matrix(), feature_matrix(), side_matrix())]
        + [patch_index.reshape(1, selected)],
        [],
        flops=1 << 28,
        name="forward_first",
        sems=6,
        hbm_in=True,
    )
    xa, xb, v_in, x = lax.optimization_barrier((xa, xb, v_in, x))
    strip = ((3, CX + 4, 2, CZ), F32)
    ya, yb = call(functools.partial(strips_kernel, n_tile), [strip] * 2, [rank, v_in, xa, xb], [], scalars=1, name="strips")
    yb = lax.ppermute(yb, "tile", tile_swaps[1])
    ya = lax.ppermute(ya, "tile", tile_swaps[0])
    a1, d1, a2, d2, a3, d3, pred, *weights = call(
        forward_rest_kernel,
        [ACT, DER, ACT, DER, ACT, DER, ((TGT, NPATCH), F32)] + WEIGHTS,
        [p2, feat_mat, x],
        [],
        flops=2 * 819200 * NPATCH,
        name="forward_rest",
    )
    halos = [xa, xb, ya, yb]

    grad_outs = [((half, rows, 128), BF16), ((half, rows, 128), F32)] if in_order else [((ROWS, 128), F32)]
    grads = call(
        functools.partial(backward_kernel, row_scale, rows, masks, n_tile, in_order),
        grad_outs,
        [rank, patch_count, index, v_in]
        + halos
        + [row_mat, lane_mat, feat_mat]
        + weights[1:]
        + [x, a1, a2, a3, d1, d2, d3, pred],
        [PADDED] + ([((ROWS, 128), F32)] if in_order else []),
        scalars=2,
        flops=4 * 819200 * NPATCH,
        name="backward",
    )
    if in_order:
        send, keep = grads
    else:
        here = jnp.arange(devices, dtype=jnp.int32)
        order = jnp.where(
            here < half,
            block_of(here, own_rank, masks, n_tile, False),
            block_of(here, own_rank, masks, n_tile, True),
        )
        placed = grads[0].reshape(devices, rows, 128)[order]
        send, keep = placed[half:].astype(BF16), placed[:half]

    size = half
    fence = lax.optimization_barrier
    got = exchange(send, 0)
    for step in range(1, steps):
        size //= 2
        if step < steps - 1:
            send = (keep[size:] + got[size:].astype(F32)).astype(BF16)
            keep = keep[:size] + got[:size].astype(F32)
        else:
            send = keep = (keep + got.astype(F32)).astype(BF16)
        if step == 1:
            send, still, moments = fence((send, v_in, jnp.stack([first_moment, second_moment])))
        if step == 3:
            send, fxb = fence((send, fxb))
        if step == steps - 1:
            send, fxa, fya = fence((send, fxa, fya))
        got = exchange(send, step)
        if step == 1:
            moments_other = exchange(moments, steps - 1)
            flow, x_new, fxa, fxb, fya, fyb = call(
                functools.partial(flow_kernel, n_tile),
                [((3, CX, CY, CZ), F32), ((FEAT, NPATCH), BF16)]
                + [((FEAT, NPATCH // 2), BF16)] * 2
                + [((FEAT, 128), BF16)] * 2,
                [rank, still] + halos + [row_mat, lane_mat],
                [PADDED, PADDED],
                scalars=1,
                flops=1 << 30,
                name="flow",
            )
            got, flow, x_new, fxa, fxb, fya, fyb = fence((got, flow, x_new, fxa, fxb, fya, fyb))
        if step == 2:
            got, moments_other = fence((got, moments_other))
        if step == 3:
            fxb = lax.ppermute(fxb, "role", role_swaps[1])
        if step == steps - 1:
            fxa = lax.ppermute(fxa, "role", role_swaps[0])
            fya = lax.ppermute(fya, "tile", tile_swaps[0])
            got, fxb = fence((got, fxb))
    grad = (keep.astype(F32) + got[::-1].astype(F32)).reshape(2, -1)
    first_two = jnp.stack([first_moment, moments_other[0]])
    second_two = jnp.stack([second_moment, moments_other[1]])
    first_two = BETA_ONE * first_two + (1.0 - BETA_ONE) * grad
    second_two = BETA_TWO * second_two + (1.0 - BETA_TWO) * grad * grad
    fix_first = 1.0 - BETA_ONE**ADAM_STEP
    fix_second = 1.0 - BETA_TWO**ADAM_STEP
    update = LEARN_RATE * (first_two / fix_first) / (jnp.sqrt(second_two / fix_second) + EPSILON)
    held = update.astype(BF16).reshape(2, rows, 128)
    at = rows // 16 * 8
    held = [held[:, :at], held[:, at:]]
    for step in range(steps - 2, 0, -1):
        if step == 2:
            held[0], fyb = fence((held[0], fyb))
        if step == 1:
            held[1], own_grad, own_first, own_second = fence((held[1], grad[0], first_moment, second_moment))
        got = [exchange(part, step) for part in held]
        if step == 1:
            first_out = BETA_ONE * own_first + (1.0 - BETA_ONE) * own_grad
            second_out = BETA_TWO * own_second + (1.0 - BETA_TWO) * own_grad * own_grad
            got[1], first_out, second_out = fence((got[1], first_out, second_out))
        if step == 2:
            fyb = lax.ppermute(fyb, "tile", tile_swaps[1])
        if step == 1:
            got[0], fyb = fence((got[0], fyb))
        if step == steps - 2:
            got[0], fxa, fya = fence((got[0], fxa, fya))
        held = [jnp.concatenate([part, new], axis=0) for part, new in zip(held, got)]
    other = [exchange(part, 0) for part in held]
    if not in_order:
        slots = jnp.zeros((devices,), jnp.int32).at[order].set(jnp.arange(devices, dtype=jnp.int32))
        all_parts = jnp.concatenate([jnp.concatenate(held, axis=1), jnp.concatenate(other, axis=1)], axis=0)
        held = other = [all_parts[slots].reshape(ROWS, 128)] * 2

    p_new, velocity_out, sgs_force = call(
        functools.partial(model_kernel, rows, masks, n_tile, in_order),
        [((ROWS, 128), F32)] + [((3, CX, CY, CZ), F32)] * 2,
        [rank, p2, *held, *other, flow, x_new, fxa, fxb, fya, fyb, row_mat, lane_mat, feat_mat, side_mat],
        [((ROWS, 128), F32)]
        + WEIGHTS
        + [((FEAT, 17 * 128), BF16), ((6, CX, CY, CZ), F32), ((2, 3, CY, CZ), F32), ((4, 48, 128), F32), ((3, CX, 80, CZ), F32)]
        + [((3, CX, CY, CZ), F32)] * 2,
        scalars=1,
        flops=4 * 819200 * NPATCH,
        name="model",
        sems=7,
        hbm_out=True,
    )
    return (velocity_out, sgs_force, p_new.reshape(-1), first_out, second_out)


def solution(mesh):
    placed = (
        P(None, "role", "tile", None),
        P(),
        P(BOTH),
        P(BOTH),
        P(BOTH),
        P(BOTH),
    )
    return jax.shard_map(
        local,
        mesh=mesh,
        in_specs=placed,
        out_specs=(
            P(None, "role", "tile", None),
            P(None, "role", "tile", None),
            P(),
            P(BOTH),
            P(BOTH),
        ),
        check_vma=False,
    )
```

```python
import functools

import jax
import jax.numpy as jnp
import numpy as np
from jax import lax
from jax.experimental import pallas as pl
from jax.experimental.pallas import tpu as pltpu
from jax.sharding import PartitionSpec as P

FEAT = 192
TGT = 384
HID = 512
ADAM_STEP = 100
STEP_DT = 0.1
VISCOSITY = 0.1
SGS_SCALE = 1.5
BETA_ONE = 0.9
BETA_TWO = 0.999
LEARN_RATE = 0.001
EPSILON = 1e-08
PAIRS = ((0, 0), (1, 1), (2, 2), (0, 1), (0, 2), (1, 2))
COMPONENT = ((0, 3, 4), (3, 1, 5), (4, 5, 2))

CX, CY, CZ = 8, 64, 128
NPATCH = 1024
ROWS = 6400
W1_AT = 768
W2_AT = W1_AT + 2048
WO_AT = W2_AT + 2048
BOTH = ("role", "tile")
F32, BF16 = jnp.float32, jnp.bfloat16
VMEM_LIMIT = 24 * 1024 * 1024


def row_matrix():
    matrix = np.zeros((256, 256), np.float32)
    for dx in range(4):
        for j in range(4):
            for pyl in range(4):
                for dy in range(4):
                    matrix[pyl * 64 + j * 16 + dx * 4 + dy, dx * 64 + j * 16 + pyl * 4 + dy] = 1
    return matrix


def lane_matrix():
    matrix = np.zeros((512, 512), np.float32)
    for pyl in range(4):
        for pz in range(32):
            for dz in range(4):
                matrix[pyl * 128 + pz * 4 + dz, dz * 128 + pyl * 32 + pz] = 1
    return matrix


def feature_matrix():
    matrix = np.zeros((128, 128), np.float32)
    for c in range(2):
        for off in range(16):
            for dz in range(4):
                matrix[c * 64 + off * 4 + dz, c * 64 + dz * 16 + off] = 1
    return matrix


def side_matrix():
    matrix = np.zeros((TGT, 128), np.float32)
    for side, dx in enumerate((3, 0)):
        for dz in range(4):
            for slot, k in enumerate((0, 3, 4)):
                for dy in range(4):
                    matrix[k * 64 + dz * 16 + dx * 4 + dy, side * 64 + dz * 16 + slot * 4 + dy] = 1
    return matrix


def dot(a, b):
    return jnp.dot(a, b, preferred_element_type=F32)


def dot_tn(a, b):
    return lax.dot_general(a, b, (((0,), (0,)), ((), ())), preferred_element_type=F32)


def dot_nt(a, b):
    return lax.dot_general(a, b, (((1,), (1,)), ((), ())), preferred_element_type=F32)


def cells_to_patches(blocks, row_mat, lane_mat, channels):
    moved = dot(row_mat, jnp.concatenate(blocks, axis=1)).astype(BF16)
    rows = []
    for i in range(2 * channels):
        part = moved[:, i * 128 : (i + 1) * 128]
        rows.append(jnp.concatenate([part[p * 64 : (p + 1) * 64] for p in range(4)], axis=1))
    spread = dot(jnp.concatenate(rows, axis=0), lane_mat).astype(BF16)
    bands = []
    for c in range(channels):
        for dz in range(4):
            bands.append(
                jnp.concatenate(
                    [
                        spread[((c * 2 + px) * 4 + j) * 16 : ((c * 2 + px) * 4 + j) * 16 + 16, dz * 128 : dz * 128 + 128]
                        for px in range(2)
                        for j in range(4)
                    ],
                    axis=1,
                )
            )
    return jnp.concatenate(bands, axis=0)


def spread_rows(x, lane_mat):
    rows = [
        jnp.concatenate([x[at + dz * 16 : at + dz * 16 + 16] for dz in range(4)], axis=1) for at in range(0, x.shape[0], 64)
    ]
    return dot_nt(jnp.concatenate(rows, axis=0), lane_mat).astype(BF16)


def rows_to_blocks(spread, row_mat):
    count = spread.shape[0] // 64
    columns = []
    for i in range(count):
        part = spread[i * 64 : (i + 1) * 64]
        columns.append(jnp.concatenate([part[:, p * 128 : (p + 1) * 128] for p in range(4)], axis=0))
    moved = dot_tn(row_mat, jnp.concatenate(columns, axis=1))
    return [moved[:, i * 128 : (i + 1) * 128] for i in range(count)]


def load_weights(p_ref, feature_mat, w0, w1, w2, wo):
    for k in range(4):
        lanes = slice(k * 128, (k + 1) * 128)
        for at in first_rows():
            w0[at[0] : at[0] + 16, lanes] = p_ref[pl.ds(at[1] + k, 16, stride=16), :].astype(BF16)
        w1[:, lanes] = p_ref[pl.ds(W1_AT + k, HID, stride=4), :].astype(BF16)
        w2[:, lanes] = p_ref[pl.ds(W2_AT + k, HID, stride=4), :].astype(BF16)
    for k in range(3):
        columns = p_ref[pl.ds(WO_AT + k, HID, stride=3), :].astype(BF16)
        wo[:, k * 128 : (k + 1) * 128] = dot(columns, feature_mat).astype(BF16)


def first_rows():
    return [(c * 64 + dz * 16, (c * 64 + dz) * 4) for c in range(3) for dz in range(4)]


def velocity_blocks(v_ref):
    return [
        v_ref[c, px * 4 : px * 4 + 4].reshape(256, 128).astype(BF16) for c in range(3) for px in range(2)
    ]


def layer(w, hidden, a_out, d_out):
    z = dot_tn(w[...], hidden)
    s = 0.5 * jnp.tanh(0.5 * z) + 0.5
    a = z * s
    d_out[...] = s + a * (1.0 - s)
    hidden = a.astype(BF16)
    a_out[...] = hidden
    return hidden


def forward_first_kernel(
    row_scale, count_ref, v_hbm, row_hbm, lane_hbm, feat_hbm, side_hbm, index_hbm,
    v_out, row_out, lane_out, feat_out, side_out, index_out, weight_out, x_out, sems
):
    copies = [
        pltpu.make_async_copy(src, dst, sems.at[i])
        for i, (src, dst) in enumerate(
            ((v_hbm, v_out), (row_hbm, row_out), (lane_hbm, lane_out), (feat_hbm, feat_out), (side_hbm, side_out), (index_hbm, index_out))
        )
    ]
    for copy in copies:
        copy.start()
    for copy in copies[:3]:
        copy.wait()
    x_out[...] = cells_to_patches(velocity_blocks(v_out), row_out[...], lane_out[...], 3)
    for copy in copies[3:]:
        copy.wait()
    weight = multiplicity(index_out, count_ref) * row_scale
    weight_out[...] = jnp.concatenate([weight[q : q + 1] for q in range(8)], axis=1)


def parity(rank_ref, n_tile):
    rank = rank_ref[0]
    return (rank // n_tile) % 2 == 0, rank % 2 == 0


def strips_kernel(n_tile, rank_ref, v_ref, xa_ref, xb_ref, ya_out, yb_out):
    role_even, tile_even = parity(rank_ref, n_tile)

    def fill(first_out, last_out, low_ref, high_ref):
        for out, at in ((first_out, 0), (last_out, CY - 2)):
            out[:, 2:10] = v_ref[:, :, at : at + 2, :]
            out[:, 0:2] = low_ref[...].astype(F32)[:, :, at : at + 2, :]
            out[:, 10:12] = high_ref[...].astype(F32)[:, :, at : at + 2, :]

    for even_r in (True, False):
        for even_t in (True, False):

            @pl.when((role_even == even_r) & (tile_even == even_t))
            def _():
                first_out, last_out = (yb_out, ya_out) if even_t else (ya_out, yb_out)
                low_ref, high_ref = (xb_ref, xa_ref) if even_r else (xa_ref, xb_ref)
                fill(first_out, last_out, low_ref, high_ref)


def forward_rest_kernel(p_ref, feat_ref, x_ref, a1_out, d1_out, a2_out, d2_out, a3_out, d3_out, pred_out, w0, w1, w2, wo):
    load_weights(p_ref, feat_ref[...], w0, w1, w2, wo)
    hidden = layer(w0, x_ref[...], a1_out, d1_out)
    hidden = layer(w1, hidden, a2_out, d2_out)
    hidden = layer(w2, hidden, a3_out, d3_out)
    pred_out[...] = dot_tn(wo[...], hidden)


def fill_padded(pad, rank_ref, n_tile, v_ref, xa_ref, xb_ref, ya_ref, yb_ref):
    role_even, tile_even = parity(rank_ref, n_tile)
    pad[:, 2:10, 8:72, :] = v_ref[...]
    for even in (True, False):

        @pl.when(role_even == even)
        def _():
            pad[:, 0:2, 8:72, :] = (xb_ref if even else xa_ref)[...].astype(F32)
            pad[:, 10:12, 8:72, :] = (xa_ref if even else xb_ref)[...].astype(F32)

        @pl.when(tile_even == even)
        def _():
            pad[:, :, 6:8, :] = (yb_ref if even else ya_ref)[...]
            pad[:, :, 72:74, :] = (ya_ref if even else yb_ref)[...]


def block_of(position, rank, masks, n_tile, send):
    core = (rank // n_tile) % 2
    if send:
        core = 1 - core
    steps = len(masks[0])
    out = rank
    for i in range(steps):
        mask = jnp.where(core == 0, masks[0][i], masks[1][i])
        out = out ^ (((position >> (steps - 1 - i)) & 1) * mask)
    return out


def box(field_sum):
    along = field_sum[:, 0:64] + field_sum[:, 1:65] + field_sum[:, 2:66]
    return (along + roll_z(along, 1) + roll_z(along, CZ - 1)) * (1.0 / 27.0)


def roll_z(x, by):
    return pltpu.roll(x, by, x.ndim - 1)


def stress_blocks(pad):
    out = [None] * 12
    for px in range(2):
        first = 1 + px * 4
        planes = [[pad[c, first + i, 7:73, :] for i in range(6)] for c in range(3)]
        smooth = []
        for c in range(3):
            sums = jnp.stack([planes[c][i] + planes[c][i + 1] + planes[c][i + 2] for i in range(4)])
            smooth.append(box(sums))
        for k, (a, b) in enumerate(PAIRS):
            prod = [planes[a][i] * planes[b][i] for i in range(6)]
            sums = jnp.stack([prod[i] + prod[i + 1] + prod[i + 2] for i in range(4)])
            value = box(sums) - smooth[a] * smooth[b]
            out[k * 2 + px] = value.astype(BF16).reshape(256, 128)
    return out


def multiplicity(index_ref, count_ref):
    index = index_ref[...]
    selected = index.shape[1]
    live = lax.broadcasted_iota(jnp.int32, (16, selected), 1) < count_ref[0]
    high = lax.broadcasted_iota(jnp.int32, (16, selected), 0) == (index >> 7)
    left = jnp.where(high & live, 1.0, 0.0).astype(BF16)
    low = lax.broadcasted_iota(jnp.int32, (128, selected), 0) == (index & 127)
    right = jnp.where(low, 1.0, 0.0).astype(BF16)
    return dot_nt(left, right)


def backward_kernel(rows, masks, n_tile, in_order, rank_ref, weight_ref, v_ref, xa_ref, xb_ref, ya_ref, yb_ref, row_ref, lane_ref,
                    feat_ref, w1, w2, wo, x_ref, a1_ref, a2_ref, a3_ref, d1_ref, d2_ref, d3_ref, pred_ref, *rest):
    if in_order:
        send_out, keep_out, pad, grads = rest
    else:
        grads, pad = rest
    weight = weight_ref[...]
    fill_padded(pad, rank_ref, n_tile, v_ref, xa_ref, xb_ref, ya_ref, yb_ref)
    target = cells_to_patches(stress_blocks(pad), row_ref[...], lane_ref[...], 6)
    error = ((pred_ref[...] - target.astype(F32)) * weight).astype(BF16)
    grad = dot_nt(a3_ref[...], error)
    for k in range(3):
        part = grad[:, k * 128 : (k + 1) * 128].astype(BF16)
        grads[pl.ds(WO_AT + k, HID, stride=3), :] = dot_nt(part, feat_ref[...])
    up = dot(wo[...], error)
    for d_ref, left_ref, at, w in ((d3_ref, a2_ref, W2_AT, w2), (d2_ref, a1_ref, W1_AT, w1), (d1_ref, x_ref, 0, None)):
        slope = (up * d_ref[...]).astype(BF16)
        grad = dot_nt(left_ref[...], slope)
        size = left_ref.shape[0]
        for k in range(4):
            lanes = slice(k * 128, (k + 1) * 128)
            if w is None:
                for src, dst in first_rows():
                    grads[pl.ds(dst + k, 16, stride=16), :] = grad[src : src + 16, lanes]
            else:
                grads[pl.ds(at + k, size, stride=4), :] = grad[:, lanes]
        if w is not None:
            up = dot(w[...], slope)
    if in_order:
        half = keep_out.shape[0]

        def place(i, carry):
            here = pl.multiple_of(block_of(i + half, rank_ref[0], masks, n_tile, True) * rows, 8)
            send_out[i] = grads[pl.ds(here, rows), :].astype(BF16)
            here = pl.multiple_of(block_of(i, rank_ref[0], masks, n_tile, False) * rows, 8)
            keep_out[i] = grads[pl.ds(here, rows), :]
            return carry

        lax.fori_loop(0, half, place, 0)


def substep(now, after_x, before_x, after_y, before_y):
    after_z = [roll_z(f, CZ - 1) for f in now]
    before_z = [roll_z(f, 1) for f in now]
    out = []
    for c in range(3):
        transport = now[0] * (0.5 * (after_x[c] - before_x[c]))
        transport = transport + now[1] * (0.5 * (after_y[c] - before_y[c]))
        transport = transport + now[2] * (0.5 * (after_z[c] - before_z[c]))
        laplace = after_x[c] + before_x[c] + after_y[c] + before_y[c] + after_z[c] + before_z[c] - 6.0 * now[c]
        out.append(now[c] + STEP_DT * (VISCOSITY * laplace - transport))
    return out


def flow_kernel(n_tile, rank_ref, v_ref, xa_ref, xb_ref, ya_ref, yb_ref, row_ref, lane_ref, flow_out, x_out, xa_out, xb_out, ya_out, yb_out, pad, mid):
    fill_padded(pad, rank_ref, n_tile, v_ref, xa_ref, xb_ref, ya_ref, yb_ref)
    for src, dst, first, count, low, high in ((pad, mid, 1, 10, 7, 73), (mid, flow_out, 2, 8, 8, 72)):
        for i in range(first, first + count):
            now = [src[c, i, low:high, :] for c in range(3)]
            after_x = [src[c, i + 1, low:high, :] for c in range(3)]
            before_x = [src[c, i - 1, low:high, :] for c in range(3)]
            after_y = [src[c, i, low + 1 : high + 1, :] for c in range(3)]
            before_y = [src[c, i, low - 1 : high - 1, :] for c in range(3)]
            new = substep(now, after_x, before_x, after_y, before_y)
            for c in range(3):
                if dst is mid:
                    mid[c, i, low:high, :] = new[c]
                else:
                    flow_out[c, i - 2] = new[c]
    x = cells_to_patches(velocity_blocks(flow_out), row_ref[...], lane_ref[...], 3)
    x_out[...] = x
    role_even, tile_even = parity(rank_ref, n_tile)
    halves = (x[:, :512], x[:, 512:])
    edges = [jnp.concatenate([half[:, at : at + 32] for half in halves] * 2, axis=1) for at in (0, 480)]
    for even in (True, False):

        @pl.when(role_even == even)
        def _():
            (xb_out if even else xa_out)[...] = halves[0]
            (xa_out if even else xb_out)[...] = halves[1]

        @pl.when(tile_even == even)
        def _():
            (yb_out if even else ya_out)[...] = edges[0]
            (ya_out if even else yb_out)[...] = edges[1]


def model_kernel(rows, masks, n_tile, in_order, rank_ref, p_ref, own_a, own_b, other_a, other_b, flow_ref, x_ref, xa_ref, xb_ref, ya_ref, yb_ref, row_ref, lane_ref,
                 feat_ref, side_ref, p_hbm, v_hbm, force_hbm, p_new, w0, w1, w2, wo, x_all, cells, side, edge, pad, v_new, force_new, sems):
    if in_order:
        half, cut = own_a.shape[0], own_a.shape[1]

        def place(i, carry):
            for low, high, at, send in ((own_a, own_b, i, False), (other_a, other_b, i + half, True)):
                base = block_of(at, rank_ref[0], masks, n_tile, send) * rows
                here = pl.ds(pl.multiple_of(base, 8), cut)
                p_new[here, :] = p_ref[here, :] - low[i].astype(F32)
                here = pl.ds(pl.multiple_of(base + cut, 8), rows - cut)
                p_new[here, :] = p_ref[here, :] - high[i].astype(F32)
            return carry

        lax.fori_loop(0, half, place, 0)
    else:
        p_new[...] = p_ref[...] - own_a[...].astype(F32)
    copies = [pltpu.make_async_copy(p_new, p_hbm, sems.at[0])]
    copies[0].start()
    load_weights(p_new, feat_ref[...], w0, w1, w2, wo)
    w_side = dot(wo[...], side_ref[...]).astype(BF16)
    role_even, tile_even = parity(rank_ref, n_tile)
    x_all[:, 0:1024] = x_ref[...]
    low = lax.broadcasted_iota(jnp.int32, (FEAT, 128), 1) < 64
    for even in (True, False):

        @pl.when(role_even == even)
        def _():
            x_all[:, 1024:1536] = (xb_ref if even else xa_ref)[...]
            x_all[:, 1536:2048] = (xa_ref if even else xb_ref)[...]

        @pl.when(tile_even == even)
        def _():
            before, after = (yb_ref, ya_ref) if even else (ya_ref, yb_ref)
            x_all[:, 2048:2176] = jnp.where(low, before[...].astype(F32), after[...].astype(F32)).astype(BF16)

    hidden = x_all[...]
    for w in (w0, w1, w2):
        z = dot_tn(w[...], hidden)
        hidden = (z * (0.5 * jnp.tanh(0.5 * z) + 0.5)).astype(BF16)
    modelled = dot_tn(wo[...], hidden[:, :1024]).astype(BF16)
    sides = dot_tn(w_side, hidden[:, 1024:2048]).astype(BF16)
    edges = dot_tn(wo[...], hidden[:, 2048:]).astype(BF16)
    for stage, ready in enumerate(((0, 3, 4), (1, 5), (2,))):
        groups = []
        for k in ready:
            groups += [modelled[k * 64 : k * 64 + 64, q * 128 : q * 128 + 128] for q in range(8)]
        if stage == 0:
            groups += [sides[q // 4 * 64 : q // 4 * 64 + 64, q * 128 : q * 128 + 128] for q in range(8)]
            groups += [edges[k * 64 : k * 64 + 64] for k in (3, 1, 5)]
        spread = spread_rows(jnp.concatenate(groups, axis=0), lane_ref[...])
        whole = spread.shape[0] // 64
        blocks = rows_to_blocks(spread[: whole * 64], row_ref[...])
        for n, k in enumerate(ready):
            for px in range(2):
                cells[k, px * 4 : px * 4 + 4] = blocks[n * 2 + px].reshape(4, CY, CZ)
        if stage == 0:
            for i in range(3):
                side[0, i] = blocks[6][i * CY : (i + 1) * CY]
                side[1, i] = blocks[7][i * CY : (i + 1) * CY]
            for slot in range(4):
                edge[slot] = spread[whole * 64 :, slot * 128 : slot * 128 + 128].astype(F32)
        i = stage
        pad[i, :, 8:72, :] = cells[(3, 1, 5)[i]]
        for px in range(2):
            pad[i, px * 4 : px * 4 + 4, 7, :] = edge[px, pl.ds(i * 16 + 3, 4, stride=4), :]
            pad[i, px * 4 : px * 4 + 4, 72, :] = edge[2 + px, pl.ds(i * 16, 4, stride=4), :]
        kx, kz = COMPONENT[i][0], COMPONENT[i][2]
        for x in range(CX):
            after = cells[kx, x + 1] if x < CX - 1 else side[1, i]
            before = cells[kx, x - 1] if x else side[0, i]
            total = 0.5 * (after - before)
            total = total + 0.5 * (pad[i, x, 9:73, :] - pad[i, x, 7:71, :])
            centre = cells[kz, x]
            total = total + 0.5 * (roll_z(centre, CZ - 1) - roll_z(centre, 1))
            force = -SGS_SCALE * total
            force_new[i, x] = force
            v_new[i, x] = flow_ref[i, x] + force
        for n, (src, dst) in enumerate(((v_new, v_hbm), (force_new, force_hbm))):
            copies.append(pltpu.make_async_copy(src.at[i], dst.at[i], sems.at[1 + 2 * i + n]))
            copies[-1].start()
    for copy in copies:
        copy.wait()


def call(kernel, outs, args, scratch, scalars=0, flops=0, name=None, sems=0, hbm_in=False, hbm_out=False):
    space = {True: pltpu.HBM, False: pltpu.VMEM}
    size = sum(a.size * a.dtype.itemsize for a in args) + sum(int(np.prod(s)) * np.dtype(t).itemsize for s, t in outs)
    args = list(args)
    args[scalars:] = [pltpu.with_memory_space_constraint(a, space[hbm_in]) for a in args[scalars:]]
    return pl.pallas_call(
        kernel,
        out_shape=[space[hbm_out](s, t) for s, t in outs],
        in_specs=[pl.BlockSpec(memory_space=pltpu.SMEM)] * scalars
        + [pl.BlockSpec(memory_space=space[hbm_in])] * (len(args) - scalars),
        out_specs=[pl.BlockSpec(memory_space=space[hbm_out])] * len(outs),
        scratch_shapes=[s if isinstance(s, pl.MemoryRef) else pltpu.VMEM(*s) for s in scratch] + ([pltpu.SemaphoreType.DMA((sems,))] if sems else []),
        compiler_params=pltpu.CompilerParams(vmem_limit_bytes=VMEM_LIMIT),
        cost_estimate=pl.CostEstimate(flops=flops, transcendentals=0, bytes_accessed=size),
        name=name,
    )(*args)


WEIGHTS = [((FEAT, HID), BF16), ((HID, HID), BF16), ((HID, HID), BF16), ((HID, TGT), BF16)]
PADDED = ((3, 12, 80, 128), F32)
ACT = ((HID, NPATCH), BF16)
DER = ((HID, NPATCH), F32)


def bits(size):
    return [1 << i for i in range(size.bit_length() - 1)]


def stage_masks(n_role, n_tile):
    role = [n_tile * b for b in bits(n_role)]
    tile = bits(n_tile)
    rest = tile[:1] + role[1:] + tile[1:]
    other = rest[1::-1] + rest[2:]
    return role[:1] + rest, role[:1] + other


def swaps(axis):
    size = lax.axis_size(axis)
    first = [(i, i ^ 1) for i in range(size)]
    return first, [(i, (i + 1) % size if i % 2 else (i - 1) % size) for i in range(size)]


def local(velocity, params, first_moment, second_moment, patch_index, patch_count):
    n_role, n_tile = lax.axis_size("role"), lax.axis_size("tile")
    devices = n_role * n_tile
    own_rank = lax.axis_index(BOTH)
    rows = ROWS // devices
    in_order = rows % 8 == 0
    masks = stage_masks(n_role, n_tile)
    steps = len(masks[0])
    core_of = [(d // n_tile) & 1 for d in range(devices)]

    def exchange(x, step):
        pairs = [(d, d ^ masks[core_of[d]][step]) for d in range(devices)]
        return lax.ppermute(x, BOTH, pairs)

    def offsets(core):
        return [
            functools.reduce(lambda a, b: a ^ b, [masks[core][i] if (j >> (steps - 1 - i)) & 1 else 0 for i in range(steps)])
            for j in range(devices)
        ]

    half = devices // 2
    rank = own_rank.astype(jnp.int32).reshape(1)
    role_even = (own_rank // n_tile) % 2 == 0
    role_swaps, tile_swaps = swaps("role"), swaps("tile")
    p2 = params.reshape(ROWS, 128)
    selected = patch_index.shape[0]
    row_scale = 1.0 / (selected // 4)

    first, last = velocity[:, :2].astype(BF16), velocity[:, CX - 2 :].astype(BF16)
    xb = lax.ppermute(jnp.where(role_even, first, last), "role", role_swaps[1])
    xa = lax.ppermute(jnp.where(role_even, last, first), "role", role_swaps[0])
    v_in, row_mat, lane_mat, feat_mat, side_mat, _, weight, x = call(
        functools.partial(forward_first_kernel, row_scale),
        [((3, CX, CY, CZ), F32), ((256, 256), BF16), ((512, 512), BF16), ((128, 128), BF16)]
        + [((TGT, 128), BF16), ((1, selected), jnp.int32), ((1, NPATCH), F32), ((FEAT, NPATCH), BF16)],
        [patch_count, velocity]
        + [jnp.asarray(m, BF16) for m in (row_matrix(), lane_matrix(), feature_matrix(), side_matrix())]
        + [patch_index.reshape(1, selected)],
        [],
        flops=1 << 28,
        name="forward_first",
        scalars=1,
        sems=6,
        hbm_in=True,
    )
    xa, xb, v_in, x = lax.optimization_barrier((xa, xb, v_in, x))
    strip = ((3, CX + 4, 2, CZ), F32)
    ya, yb = call(functools.partial(strips_kernel, n_tile), [strip] * 2, [rank, v_in, xa, xb], [], scalars=1, name="strips")
    yb = lax.ppermute(yb, "tile", tile_swaps[1])
    ya = lax.ppermute(ya, "tile", tile_swaps[0])
    a1, d1, a2, d2, a3, d3, pred, *weights = call(
        forward_rest_kernel,
        [ACT, DER, ACT, DER, ACT, DER, ((TGT, NPATCH), F32)] + WEIGHTS,
        [p2, feat_mat, x],
        [],
        flops=2 * 819200 * NPATCH,
        name="forward_rest",
    )
    halos = [xa, xb, ya, yb]

    grad_outs = [((half, rows, 128), BF16), ((half, rows, 128), F32)] if in_order else [((ROWS, 128), F32)]
    grads = call(
        functools.partial(backward_kernel, rows, masks, n_tile, in_order),
        grad_outs,
        [rank, weight, v_in]
        + halos
        + [row_mat, lane_mat, feat_mat]
        + weights[1:]
        + [x, a1, a2, a3, d1, d2, d3, pred],
        [PADDED] + ([((ROWS, 128), F32)] if in_order else []),
        scalars=1,
        flops=4 * 819200 * NPATCH,
        name="backward",
    )
    if in_order:
        send, keep = grads
    else:
        here = jnp.arange(devices, dtype=jnp.int32)
        order = jnp.where(
            here < half,
            block_of(here, own_rank, masks, n_tile, False),
            block_of(here, own_rank, masks, n_tile, True),
        )
        placed = grads[0].reshape(devices, rows, 128)[order]
        send, keep = placed[half:].astype(BF16), placed[:half]

    size = half
    fence = lax.optimization_barrier
    got = exchange(send, 0)
    for step in range(1, steps):
        size //= 2
        if step < steps - 1:
            send = (keep[size:] + got[size:].astype(F32)).astype(BF16)
            keep = keep[:size] + got[:size].astype(F32)
        else:
            send = keep = (keep + got.astype(F32)).astype(BF16)
        if step == 1:
            send, still, moments = fence((send, v_in, jnp.stack([first_moment, second_moment])))
        if step == 3:
            send, fxb = fence((send, fxb))
        if step == steps - 1:
            send, fxa, fya = fence((send, fxa, fya))
        got = exchange(send, step)
        if step == 1:
            moments_other = exchange(moments, steps - 1)
            flow, x_new, fxa, fxb, fya, fyb = call(
                functools.partial(flow_kernel, n_tile),
                [((3, CX, CY, CZ), F32), ((FEAT, NPATCH), BF16)]
                + [((FEAT, NPATCH // 2), BF16)] * 2
                + [((FEAT, 128), BF16)] * 2,
                [rank, still] + halos + [row_mat, lane_mat],
                [PADDED, PADDED],
                scalars=1,
                flops=1 << 30,
                name="flow",
            )
            got, flow, x_new, fxa, fxb, fya, fyb = fence((got, flow, x_new, fxa, fxb, fya, fyb))
        if step == 2:
            got, moments_other = fence((got, moments_other))
        if step == 3:
            fxb = lax.ppermute(fxb, "role", role_swaps[1])
        if step == steps - 1:
            fxa = lax.ppermute(fxa, "role", role_swaps[0])
            fya = lax.ppermute(fya, "tile", tile_swaps[0])
            got, fxb = fence((got, fxb))
    grad = (keep.astype(F32) + got[::-1].astype(F32)).reshape(2, -1)
    first_two = jnp.stack([first_moment, moments_other[0]])
    second_two = jnp.stack([second_moment, moments_other[1]])
    first_two = BETA_ONE * first_two + (1.0 - BETA_ONE) * grad
    second_two = BETA_TWO * second_two + (1.0 - BETA_TWO) * grad * grad
    fix_first = 1.0 - BETA_ONE**ADAM_STEP
    fix_second = 1.0 - BETA_TWO**ADAM_STEP
    update = LEARN_RATE * (first_two / fix_first) / (jnp.sqrt(second_two / fix_second) + EPSILON)
    held = update.astype(BF16).reshape(2, rows, 128)
    at = rows // 16 * 8
    held = [held[:, :at], held[:, at:]]
    for step in range(steps - 2, 0, -1):
        if step == 2:
            held[0], fyb = fence((held[0], fyb))
        if step == 1:
            held[1], own_grad, own_first, own_second = fence((held[1], grad[0], first_moment, second_moment))
        got = [exchange(part, step) for part in held]
        if step == 1:
            first_out = BETA_ONE * own_first + (1.0 - BETA_ONE) * own_grad
            second_out = BETA_TWO * own_second + (1.0 - BETA_TWO) * own_grad * own_grad
            got[1], first_out, second_out = fence((got[1], first_out, second_out))
        if step == 2:
            fyb = lax.ppermute(fyb, "tile", tile_swaps[1])
        if step == 1:
            got[0], fyb = fence((got[0], fyb))
        if step == steps - 2:
            got[0], fxa, fya = fence((got[0], fxa, fya))
        held = [jnp.concatenate([part, new], axis=0) for part, new in zip(held, got)]
    other = [exchange(part, 0) for part in held]
    if not in_order:
        slots = jnp.zeros((devices,), jnp.int32).at[order].set(jnp.arange(devices, dtype=jnp.int32))
        all_parts = jnp.concatenate([jnp.concatenate(held, axis=1), jnp.concatenate(other, axis=1)], axis=0)
        held = other = [all_parts[slots].reshape(ROWS, 128)] * 2

    p_new, velocity_out, sgs_force = call(
        functools.partial(model_kernel, rows, masks, n_tile, in_order),
        [((ROWS, 128), F32)] + [((3, CX, CY, CZ), F32)] * 2,
        [rank, p2, *held, *other, flow, x_new, fxa, fxb, fya, fyb, row_mat, lane_mat, feat_mat, side_mat],
        [((ROWS, 128), F32)]
        + WEIGHTS
        + [((FEAT, 17 * 128), BF16), ((6, CX, CY, CZ), F32), ((2, 3, CY, CZ), F32), ((4, 48, 128), F32), ((3, CX, 80, CZ), F32)]
        + [((3, CX, CY, CZ), F32)] * 2,
        scalars=1,
        flops=4 * 819200 * NPATCH,
        name="model",
        sems=7,
        hbm_out=True,
    )
    return (velocity_out, sgs_force, p_new.reshape(-1), first_out, second_out)


def solution(mesh):
    placed = (
        P(None, "role", "tile", None),
        P(),
        P(BOTH),
        P(BOTH),
        P(BOTH),
        P(BOTH),
    )
    return jax.shard_map(
        local,
        mesh=mesh,
        in_specs=placed,
        out_specs=(
            P(None, "role", "tile", None),
            P(None, "role", "tile", None),
            P(),
            P(BOTH),
            P(BOTH),
        ),
        check_vma=False,
    )
```
